32 devices in a mesh: batch: 8 (over y, x, core), seq: 4 (over z).
Axes of the slice: x: 2, y: 2, z: 4, core: 2. Of those that a mesh axis runs over, the one named last changes fastest.
Arguments:
- tokens: bfloat16 [8, 1024, 768], P('batch', 'seq'), may hold values from -6 to 6
- segments: int32 [8, 1024], P('batch', 'seq'), may hold values from 0 to 10, as said below
- prompts: float32 [50, 768], replicated, may hold values from -6 to 6
- ln1_gain: float32 [768], replicated, may hold values from 0.1 to 1.9
- ln1_shift: float32 [768], replicated, may hold values from -1.75 to 1.75
- w_qkv: bfloat16 [768, 2304], replicated, may hold values from -0.3125 to 0.3125
- q_bias: float32 [768], replicated, may hold values from -3 to 3
- v_bias: float32 [768], replicated, may hold values from -3 to 3
- w_out: bfloat16 [768, 768], replicated, may hold values from -0.875 to 0.875
- out_bias: float32 [768], replicated, may hold values from -1.75 to 1.75
- ln2_gain: float32 [768], replicated, may hold values from 0.1 to 1.9
- ln2_shift: float32 [768], replicated, may hold values from -1.75 to 1.75
- w_fc1: bfloat16 [768, 3072], replicated, may hold values from -0.21875 to 0.21875
- fc1_bias: float32 [3072], replicated, may hold values from -3 to 3
- w_fc2: bfloat16 [3072, 768], replicated, may hold values from -0.15625 to 0.15625
- fc2_bias: float32 [768], replicated, may hold values from -1.75 to 1.75
- cotangent: bfloat16 [8, 1024, 768], P('batch', 'seq'), may hold values from -6 to 6
Outputs:
- layer_out: bfloat16 [8, 1024, 768], P('batch', 'seq')
- grad_input: bfloat16 [8, 1024, 768], P('batch', 'seq')
- grad_prompts: float32 [50, 768], replicated
- grad_ln1_gain: float32 [768], replicated
- grad_ln1_shift: float32 [768], replicated
- grad_w_qkv: float32 [768, 2304], P('seq')
- grad_q_bias: float32 [768], replicated
- grad_v_bias: float32 [768], replicated
- grad_w_out: float32 [768, 768], P('seq')
- grad_out_bias: float32 [768], replicated
- grad_ln2_gain: float32 [768], replicated
- grad_ln2_shift: float32 [768], replicated
- grad_w_fc1: float32 [768, 3072], P('seq')
- grad_fc1_bias: float32 [3072], replicated
- grad_w_fc2: float32 [3072, 768], P('seq')
- grad_fc2_bias: float32 [768], replicated
The draws below stay inside these ranges and needn't reach their ends.
Inputs may be any that keep to these rules, and one draw needn't show every extreme that they name: `segments`: in each row every image has the same number n of tokens, one of 101, 197 or 577, and each of the three occurs in some row: the id at position t of a row is t // n, and the last segment of a row is shorter.
All inputs are finite; a program needn't handle non-finite values.
Results may differ from the reference program's by a relative error of at most 0.015.
The reference program's roundings to bfloat16 on the way count: a program that leaves them out, or rounds other values in their place, can miss the bound.
Values may be sent and summed in bfloat16 or wider, within the bound.
A program may use at most 192 MiB of HBM per device.

```python
import jax
import jax.numpy as jnp
from jax import lax

MODEL_WIDTH = 768
HEAD_DIM = 64
FF = 3072
PROMPTS = 50
PACKED_ROW_LEN = 1024
IMG_SMALL = 101
IMG_MID = 197
IMG_BIG = 577
TOTAL_ROWS = 8


def draw_segments(key, part):
    kind_key = jax.random.fold_in(key, 11)
    order_key = jax.random.fold_in(key, 12)
    kinds = jax.random.randint(kind_key, (TOTAL_ROWS,), 0, 3)
    chosen = jax.random.permutation(order_key, TOTAL_ROWS)[:3]
    kinds = kinds.at[chosen].set(jnp.arange(3, dtype=jnp.int32))
    lengths = jnp.where(kinds == 0, IMG_SMALL, jnp.where(kinds == 1, IMG_MID, IMG_BIG)).astype(jnp.int32)
    token_positions = jnp.arange(PACKED_ROW_LEN, dtype=jnp.int32)
    return (token_positions[None, :] // lengths[:, None]).astype(jnp.int32)


def shard_levels(stream_key, dims, split, smallest, high):
    def one(position, parts):
        heights = jax.random.uniform(jax.random.fold_in(jax.random.fold_in(stream_key, 6), position), (parts,), jnp.float32, smallest / len(split), high / len(split))
        return jnp.repeat(jnp.exp(heights), dims[position] // parts).reshape((-1,) + (1,) * (len(dims) - position - 1))

    level = one(*split[0])
    for cut in split[1:]:
        level = level * one(*cut)
    return level


def noise(key, dims, width, bound, shards=(), held_as=jnp.bfloat16):
    values = width * jax.random.normal(key, dims, jnp.float32)
    if shards:
        values = values * shard_levels(key, dims, shards, -0.22, 0.18)
    return jnp.clip(values, -bound, bound).astype(held_as)


def setup_inputs(seed: int = 0) -> dict:
    splits = jax.random.split(jax.random.key(seed), 18)
    return {
        "tokens": noise(splits[0], (TOTAL_ROWS, PACKED_ROW_LEN, MODEL_WIDTH), 1.0, 6.0, ((0, 8), (1, 4))),
        "segments": draw_segments(jax.random.fold_in(splits[17], 71), 0),
        "prompts": noise(splits[2], (PROMPTS, MODEL_WIDTH), 1.0, 6.0, (), jnp.float32),
        "ln1_gain": jnp.clip(1.0 + 0.18 * jax.random.normal(splits[3], (MODEL_WIDTH,), jnp.float32), 0.1, 1.9),
        "ln1_shift": noise(splits[4], (MODEL_WIDTH,), 0.3, 1.75, (), jnp.float32),
        "w_qkv": noise(splits[5], (MODEL_WIDTH, 3 * MODEL_WIDTH), (MODEL_WIDTH // 2) ** -0.5, 0.3125),
        "q_bias": noise(splits[6], (MODEL_WIDTH,), 0.5, 3.0, (), jnp.float32),
        "v_bias": noise(splits[7], (MODEL_WIDTH,), 0.5, 3.0, (), jnp.float32),
        "w_out": noise(splits[8], (MODEL_WIDTH, MODEL_WIDTH), (MODEL_WIDTH // 16) ** -0.5, 0.875),
        "out_bias": noise(splits[9], (MODEL_WIDTH,), 0.3, 1.75, (), jnp.float32),
        "ln2_gain": jnp.clip(1.0 + 0.18 * jax.random.normal(splits[10], (MODEL_WIDTH,), jnp.float32), 0.1, 1.9),
        "ln2_shift": noise(splits[11], (MODEL_WIDTH,), 0.3, 1.75, (), jnp.float32),
        "w_fc1": noise(splits[12], (MODEL_WIDTH, FF), MODEL_WIDTH ** -0.5, 0.21875),
        "fc1_bias": noise(splits[13], (FF,), 0.5, 3.0, (), jnp.float32),
        "w_fc2": noise(splits[14], (FF, MODEL_WIDTH), (FF // 2) ** -0.5, 0.15625),
        "fc2_bias": noise(splits[15], (MODEL_WIDTH,), 0.3, 1.75, (), jnp.float32),
        "cotangent": noise(splits[16], (TOTAL_ROWS, PACKED_ROW_LEN, MODEL_WIDTH), 1.0, 6.0, ((0, 8), (1, 4))),
    }


@jax.custom_vjp
def low(v):
    return lax.optimization_barrier(v.astype(jnp.bfloat16)).astype(jnp.float32)

@jax.custom_vjp
def low_back(v):
    return v

def low_keep(v):
    return (low(v), None)

def low_pass(kept, grad):
    return (grad,)

def back_keep(v):
    return (v, None)

def back_low(kept, grad):
    return (low(grad),)
low.defvjp(low_keep, low_pass)
low_back.defvjp(back_keep, back_low)
EPSILON = 1e-06
MASKED_SCORE = -1e+30
HIGHEST_PRECISION = lax.Precision.HIGHEST

def product(left, right):
    return jnp.dot(left, right, precision=HIGHEST_PRECISION)

def norm_rows(values, gain, shift):
    centred = values - lax.optimization_barrier(jnp.mean(values, axis=-1, keepdims=True))
    variance = lax.optimization_barrier(jnp.mean(centred * centred, axis=-1, keepdims=True))
    return centred * lax.rsqrt(variance + EPSILON) * gain + shift

def row_layer(row_tokens, row_segments, p_keys, p_values, weights):
    ln1_gain, ln1_shift, w_qkv, q_bias, v_bias, w_out, out_bias, ln2_gain, ln2_shift, w_fc1, fc1_bias, w_fc2, fc2_bias = weights
    features = row_tokens.shape[-1]
    head_count = features // HEAD_DIM
    score_scale = HEAD_DIM ** (-0.5)
    normed = low(norm_rows(row_tokens, ln1_gain, ln1_shift))
    projected = product(normed, w_qkv)
    queries = low_back(low(projected[:, :features] + q_bias))
    keys_row = low_back(low(projected[:, features:2 * features]))
    values_row = low_back(low(projected[:, 2 * features:] + v_bias))

    def by_heads(table):
        return table.reshape(table.shape[0], head_count, HEAD_DIM).transpose(1, 0, 2)
    query_heads = by_heads(queries)
    row_scores = low_back(jnp.einsum('hqd,hkd->hqk', query_heads, by_heads(keys_row), precision=HIGHEST_PRECISION) * score_scale)
    prompt_scores = low_back(jnp.einsum('hqd,hkd->hqk', query_heads, by_heads(p_keys), precision=HIGHEST_PRECISION) * score_scale)
    allowed = row_segments[:, None] == row_segments[None, :]
    row_scores = jnp.where(allowed[None], row_scores, MASKED_SCORE)
    highest = jnp.maximum(lax.optimization_barrier(jnp.max(row_scores, axis=-1, keepdims=True)), lax.optimization_barrier(jnp.max(prompt_scores, axis=-1, keepdims=True)))
    row_exp = jnp.exp(row_scores - highest)
    prompt_exp = jnp.exp(prompt_scores - highest)
    denominator = lax.optimization_barrier(jnp.sum(row_exp, axis=-1, keepdims=True)) + lax.optimization_barrier(jnp.sum(prompt_exp, axis=-1, keepdims=True))
    row_probs = low(row_exp / denominator)
    prompt_probs = low(prompt_exp / denominator)
    combined = jnp.einsum('hqk,hkd->hqd', row_probs, by_heads(values_row), precision=HIGHEST_PRECISION)
    combined = combined + jnp.einsum('hqk,hkd->hqd', prompt_probs, by_heads(p_values), precision=HIGHEST_PRECISION)
    attended = low_back(low(combined.transpose(1, 0, 2).reshape(row_tokens.shape[0], features)))
    middle = row_tokens + low_back(product(attended, w_out) + out_bias)
    normed_two = low(norm_rows(middle, ln2_gain, ln2_shift))
    hidden_pre = low_back(product(normed_two, w_fc1) + fc1_bias)
    activated = low(jax.nn.gelu(hidden_pre, approximate=False))
    return middle + low_back(product(activated, w_fc2) + fc2_bias)

def reference(tokens, segments, prompts, ln1_gain, ln1_shift, w_qkv, q_bias, v_bias, w_out, out_bias, ln2_gain, ln2_shift, w_fc1, fc1_bias, w_fc2, fc2_bias, cotangent):

    def forward(inputs, prompt_rows, *weights):
        features = inputs.shape[-1]
        complete_weight = weights[2]
        p_normed = low(norm_rows(prompt_rows, weights[0], weights[1]))
        p_projected = product(p_normed, complete_weight[:, features:])
        p_keys = low_back(low(p_projected[:, :features]))
        p_values = low_back(low(p_projected[:, features:] + weights[4]))
        layer = jax.checkpoint(row_layer)

        def scan_step(carried, element):
            return (carried, layer(element[0], element[1], p_keys, p_values, weights))
        _, results = lax.scan(scan_step, jnp.zeros((), jnp.float32), (inputs, segments))
        return results
    floats = (tokens.astype(jnp.float32), prompts, ln1_gain, ln1_shift, w_qkv.astype(jnp.float32), q_bias, v_bias, w_out.astype(jnp.float32), out_bias, ln2_gain, ln2_shift, w_fc1.astype(jnp.float32), fc1_bias, w_fc2.astype(jnp.float32), fc2_bias)
    results, pullback = jax.vjp(forward, *floats)
    grads = pullback(cotangent.astype(jnp.float32))
    return (results.astype(jnp.bfloat16), grads[0].astype(jnp.bfloat16), grads[1], grads[2], grads[3], grads[4], grads[5], grads[6], grads[7], grads[8], grads[9], grads[10], grads[11], grads[12], grads[13], grads[14])
```

```python
import functools

import jax
import jax.numpy as jnp
from jax import lax
from jax.experimental import pallas as pl
from jax.experimental.pallas import tpu as pltpu
from jax.sharding import PartitionSpec as P

HEAD_DIM = 64
IMAGE_TOKENS = (101, 197, 577)
EPSILON = 1e-06
MASKED_SCORE = -1e30
ROOT_HALF = 0.7071067811865476
ROOT_TWO_PI = 2.5066282746310002
SCALE = HEAD_DIM ** (-0.5)
GROUP = 8
PROMPT_PAD = 64
SMALL_ROWS = 64
F32 = jnp.float32
BF16 = jnp.bfloat16
MESH = pl.DeviceIdType.MESH


def dot_nn(a, b):
    return lax.dot_general(a, b, (((1,), (0,)), ((), ())), preferred_element_type=F32)


def dot_nt(a, b):
    return lax.dot_general(a, b, (((1,), (1,)), ((), ())), preferred_element_type=F32)


def dot_tn(a, b):
    return lax.dot_general(a, b, (((0,), (0,)), ((), ())), preferred_element_type=F32)


def need_table(groups, local_len):
    row_len = groups * local_len
    table = [[0] * groups for _ in range(groups)]
    for size in IMAGE_TOKENS:
        for start in range(0, row_len, size):
            first = start // local_len
            last = (min(start + size, row_len) - 1) // local_len
            for a in range(first, last + 1):
                for b in range(first, last + 1):
                    table[a][b] = 1
    return table


def norm_stats(values):
    centred = values - jnp.mean(values, axis=-1, keepdims=True)
    inverse = lax.rsqrt(jnp.mean(centred * centred, axis=-1, keepdims=True) + EPSILON)
    return centred * inverse, inverse


def norm_back(grad_out, scaled, inverse, gain):
    inner = grad_out * gain
    return inverse * (
        inner
        - jnp.mean(inner, axis=-1, keepdims=True)
        - scaled * jnp.mean(inner * scaled, axis=-1, keepdims=True)
    )


def column_sum(values):
    return jnp.sum(values, axis=0, keepdims=True)


X_COT, X_N2, X_ATT, X_NORM, X_GB, X_QKV, X_SMALL, X_FINAL, X_ACT, X_GP = 0, 1, 2, 3, 4, 5, 6, 7, 11, 15
X_COUNT = 19


def layer_kernel(
    dims,
    tokens_ref,
    seg_ref,
    prompts_ref,
    g1_ref,
    s1_ref,
    wqkv_hbm,
    qb_ref,
    vb_ref,
    wout_hbm,
    ob_ref,
    g2_ref,
    s2_ref,
    wfc1_hbm,
    b1_ref,
    wfc2_hbm,
    b2_ref,
    cot_ref,
    layer_out_ref,
    grad_input_ref,
    final_ref,
    small_ref,
    wqkv,
    wout,
    wfc1,
    wfc2,
    tokrow,
    nb,
    nbt,
    q_row,
    k_row,
    v_row,
    bias,
    o32,
    att,
    lse,
    centre,
    mid,
    xh2,
    r2,
    n2,
    n2t,
    act,
    gp,
    actp,
    gpp,
    acc_out,
    acc_dn,
    cotp,
    gb,
    gbp,
    ga_row,
    stat,
    dk,
    dv,
    dqkv,
    dqp,
    units,
    r1,
    r2u,
    r3,
    a3,
    sm,
    smp,
    s0,
    rs1,
    s1b,
    rs2,
    rs3,
    s3,
    wsem,
    tok_s,
    tok_r,
    pair_s,
    pair_r,
    ga_s,
    ga_r,
    st_s,
    st_r,
    one_s,
    one_r,
    two_s,
    two_r,
    three_s,
    three_r,
    loc_sem,
    ag1_s,
    ag1_r,
    ag2_s,
    ag2_r,
):
    groups, local_len, width, ff, prompt_count, table = dims
    row_len = groups * local_len
    head_pairs = width // (2 * HEAD_DIM)
    chunks = ff // width
    half_w = width // 2
    key_len = row_len + PROMPT_PAD
    zrows = width // groups

    b = lax.axis_index("batch")
    s = lax.axis_index("seq")
    base = (b // GROUP) * GROUP
    core = lax.rem(b, 2)
    xb = lax.rem(b // 2, 2)
    yb = lax.rem(b // 4, 2)
    h1 = xb * (1 - core) + yb * core
    h2 = yb * (1 - core) + xb * core

    def place(x, y, c):
        return base + y * 4 + x * 2 + c

    nb1 = (place(xb + (1 - core) * (1 - 2 * xb), yb + core * (1 - 2 * yb), core), s)
    nb2 = (place(xb + core * (1 - 2 * xb), yb + (1 - core) * (1 - 2 * yb), core), s)
    pair = (place(xb, yb, 1 - core), s)

    def along(d):
        return lax.rem(s + d, groups)

    def needs(a, c):
        flag = jnp.int32(0)
        for i in range(groups):
            for j in range(groups):
                if table[i][j]:
                    flag = flag + jnp.where(a == i, 1, 0) * jnp.where(c == j, 1, 0)
        return flag > 0

    def remote(src, dst, send, recv, to):
        return pltpu.make_async_remote_copy(
            src_ref=src, dst_ref=dst, send_sem=send, recv_sem=recv, device_id=to, device_id_type=MESH
        )

    barrier = pltpu.get_barrier_semaphore()
    for peer in (pair, nb1, nb2):
        pl.semaphore_signal(barrier, inc=1, device_id=peer, device_id_type=MESH)
    for d in range(1, groups):
        pl.semaphore_signal(barrier, inc=1, device_id=(b, along(d)), device_id_type=MESH)

    loads = [
        pltpu.make_async_copy(wqkv_hbm, wqkv, wsem.at[0]),
        pltpu.make_async_copy(wout_hbm, wout, wsem.at[1]),
        pltpu.make_async_copy(wfc1_hbm, wfc1, wsem.at[2]),
        pltpu.make_async_copy(wfc2_hbm, wfc2, wsem.at[3]),
    ]
    loads[0].start()
    pl.semaphore_wait(barrier, 2 + groups)

    def token_send(d):
        return remote(
            tokens_ref, tokrow.at[s], tok_s.at[d - 1], tok_r.at[s], (b, along(d))
        )

    def token_recv(j):
        return remote(tokens_ref, tokrow.at[j], tok_s.at[0], tok_r.at[j], (b, j))

    for d in range(1, groups):

        @pl.when(needs(along(d), s))
        def _(d=d):
            token_send(d).start()

    for load in loads[1:]:
        load.start()

    def pair_copy(index, src, dst):
        return remote(src, dst, pair_s.at[index], pair_r.at[index], pair)

    my_half = pl.ds(pl.multiple_of(core * half_w, 128), half_w)
    other_half = pl.ds(pl.multiple_of((1 - core) * half_w, 128), half_w)
    qkv_half = 3 * width // 2
    my_qkv = pl.ds(pl.multiple_of(core * qkv_half, 128), qkv_half)
    other_qkv = pl.ds(pl.multiple_of((1 - core) * qkv_half, 128), qkv_half)

    send_cot = pair_copy(X_COT, cot_ref, cotp)
    send_cot.start()

    gain1 = g1_ref[...]
    shift1 = s1_ref[...]

    last = s * local_len + local_len - 1
    seg_last = seg_ref[:, local_len - 1 : local_len].astype(F32)
    inv_n = jnp.full((1, 1), 1.0 / IMAGE_TOKENS[-1], F32)
    for size in IMAGE_TOKENS[:-1]:
        inv_n = jnp.where(seg_last == (last // size).astype(F32), 1.0 / size, inv_n)
    q_pos = lax.broadcasted_iota(jnp.int32, (local_len, 1), 0) + s * local_len
    k_pos = lax.broadcasted_iota(jnp.int32, (1, key_len), 1)
    q_id = jnp.floor((q_pos.astype(F32) + 0.5) * inv_n)
    k_id = jnp.floor((k_pos.astype(F32) + 0.5) * inv_n)
    k_open = jnp.where(k_pos < row_len, 0.0, jnp.where(k_pos < row_len + prompt_count, 1.0, 0.0))
    k_id = jnp.where(k_pos < row_len, k_id, -1.0)
    bias[...] = jnp.where(q_id == k_id, 0.0, MASKED_SCORE * (1.0 - k_open))

    own_rows = pl.ds(pl.multiple_of(s * local_len, local_len), local_len)

    def project(normed, rows):
        q = dot_nn(normed, wqkv[:, :width]) + qb_ref[...]
        q_row[rows, :] = (q.astype(BF16).astype(F32) * SCALE).astype(BF16)
        k_row[rows, :] = dot_nn(normed, wqkv[:, width : 2 * width]).astype(BF16)
        v_row[rows, :] = (dot_nn(normed, wqkv[:, 2 * width :]) + vb_ref[...]).astype(BF16)

    p_scaled, p_inverse = norm_stats(prompts_ref[...])
    nb[local_len : local_len + PROMPT_PAD, :] = jnp.zeros((PROMPT_PAD, width), BF16)
    nb[local_len : local_len + prompt_count, :] = (p_scaled * gain1 + shift1).astype(BF16)
    scaled1, _ = norm_stats(tokens_ref[...].astype(F32))
    nb[0:local_len, :] = (scaled1 * gain1 + shift1).astype(BF16)
    tok_block = local_len + PROMPT_PAD
    send_norm = pair_copy(X_NORM, nb.at[pl.ds(0, tok_block)], nb.at[pl.ds(tok_block, tok_block)])
    send_norm.start()

    loads[0].wait()
    project(nb[0:local_len, :], own_rows)
    p_low = nb[local_len:tok_block, :]
    k_row[row_len:key_len, :] = dot_nn(p_low, wqkv[:, width : 2 * width]).astype(BF16)
    v_row[row_len:key_len, :] = (dot_nn(p_low, wqkv[:, 2 * width :]) + vb_ref[...]).astype(BF16)

    def order(k):
        return lax.rem(s + k + jnp.where(k == 2, 1, 0) - jnp.where(k == 3, 1, 0), groups)

    def other_shard(k, carry):
        j = order(k)
        rows = pl.ds(pl.multiple_of(j * local_len, local_len), local_len)
        needed = needs(s, j)

        @pl.when(needed)
        def _():
            token_recv(j).wait_recv()
            scaled, _ = norm_stats(tokrow[j].astype(F32))
            project((scaled * gain1 + shift1).astype(BF16), rows)

        @pl.when(jnp.logical_not(needed))
        def _():
            k_row[rows, :] = jnp.zeros((local_len, width), BF16)
            v_row[rows, :] = jnp.zeros((local_len, width), BF16)

        return carry

    lax.fori_loop(1, groups, other_shard, 0)

    pair_lane = lax.broadcasted_iota(jnp.int32, (1, 2 * HEAD_DIM), 1)
    first_head = jnp.where(pair_lane < HEAD_DIM, 1.0, 0.0)
    head_mask = (first_head.astype(BF16), (1.0 - first_head).astype(BF16))
    first_head_f32 = pair_lane < HEAD_DIM
    stat_lane = lax.broadcasted_iota(jnp.int32, (local_len, 128), 1)

    def lanes_of(hp):
        return pl.ds(pl.multiple_of(hp * 2 * HEAD_DIM, 128), 2 * HEAD_DIM)

    lse[...] = jnp.zeros((local_len, 128), F32)
    centre[...] = jnp.zeros((local_len, 128), F32)

    def attend(hp, carry):
        lanes = lanes_of(hp)
        q = q_row[own_rows, lanes]
        k = k_row[:, lanes]
        v = v_row[:, lanes]
        outs = []
        for h in range(2):
            scores = dot_nt(q * head_mask[h], k) + bias[...]
            highest = jnp.max(scores, axis=-1, keepdims=True)
            weights = jnp.exp(scores - highest)
            total = jnp.sum(weights, axis=-1, keepdims=True)
            outs.append(dot_nn(weights.astype(BF16), v) / total)
            lse[...] = jnp.where(stat_lane == 2 * hp + h, highest + jnp.log(total), lse[...])
        combined = jnp.where(first_head_f32, outs[0], outs[1])
        o32[:, lanes] = combined
        att[0:local_len, lanes] = combined.astype(BF16)
        return carry

    lax.fori_loop(0, head_pairs, attend, 0)
    own = pl.ds(0, local_len)
    theirs = pl.ds(local_len, local_len)
    send_att = pair_copy(X_ATT, att.at[own], att.at[theirs])
    send_att.start()

    loads[1].wait()
    mid[...] = (
        tokens_ref[...].astype(F32) + dot_nn(att[0:local_len, :], wout[...]) + ob_ref[...]
    )
    scaled2, inverse2 = norm_stats(mid[...])
    xh2[...] = scaled2
    r2[...] = inverse2
    n2[0:local_len, :] = (scaled2 * g2_ref[...] + s2_ref[...]).astype(BF16)
    send_n2 = pair_copy(X_N2, n2.at[own], n2.at[theirs])
    send_n2.start()
    acc_out[...] = jnp.zeros((local_len, width), F32)
    acc_dn[...] = jnp.zeros((local_len, width), F32)
    n2t[:, 0:local_len] = n2[0:local_len, :].T
    loads[2].wait()
    loads[3].wait()
    send_n2.wait_recv()
    n2t[:, local_len:] = n2[local_len:, :].T
    send_cot.wait_recv()

    blk = zrows // 4

    def unit_of(p):
        return p // 2 + 4 * lax.rem(p, 2)

    def store_rows(u, grads):
        for z in range(groups):
            for a in range(2):
                for c in range(2):
                    r = z * zrows + (2 * a + c) * blk
                    units[u, a, c, z] = grads[r : r + blk, :].astype(BF16)

    def stage_one(u):
        return remote(units.at[u, 1 - h1], r1.at[u], one_s.at[u], one_r.at[u], nb1)

    def stage_two(u):
        return remote(units.at[u, h1, 1 - h2], r2u.at[u], two_s.at[u], two_r.at[u], nb2)

    def advance_one(u):
        stage_one(u).wait_recv()
        units[u, h1] = (units[u, h1].astype(F32) + r1[u].astype(F32)).astype(BF16)
        stage_two(u).start()

    def advance_two(u):
        stage_two(u).wait_recv()
        r2u[u] = (units[u, h1, h2].astype(F32) + r2u[u].astype(F32)).astype(BF16)

    def stage_three(g, d):
        t = along(d)
        src = r2u.at[t] if g == 0 else r2u.at[pl.ds(4 * g, 4), t]
        return remote(src, r3.at[g, s], three_s.at[g, d - 1], three_r.at[g, s], (b, t))

    def stage_three_recv(g, j):
        return remote(a3.at[g], r3.at[g, j], three_s.at[g, 0], three_r.at[g, j], (b, j))

    def start_three(g):
        for d in range(1, groups):
            stage_three(g, d).start()

    def keep_final(g):
        return pltpu.make_async_copy(a3.at[g], final_ref.at[g, core, h1, h2], loc_sem.at[g])

    def gather_one(g):
        return remote(a3.at[g], final_ref.at[g, core, h1, h2], ag1_s.at[g], ag1_r.at[g], nb2)

    def gather_two(g):
        return remote(
            final_ref.at[g, core, h1], final_ref.at[g, core, h1], ag2_s.at[g], ag2_r.at[g], nb1
        )

    def gather_pair(g):
        return pair_copy(X_FINAL + g, final_ref.at[g, core], final_ref.at[g, core])

    def finish_three(g):
        total = (r2u[s] if g == 0 else r2u[4 * g : 4 * g + 4, s]).astype(F32)
        for d in range(1, groups):
            j = along(d)
            stage_three_recv(g, j).wait_recv()
            total = total + r3[g, j].astype(F32)
        a3[g] = total.astype(BF16)
        keep_final(g).start()
        gather_one(g).start()

    def start_gather_two(g):
        keep_final(g).wait()
        gather_one(g).wait_recv()
        gather_two(g).start()

    def start_gather_pair(g):
        gather_two(g).wait_recv()
        gather_pair(g).start()

    sm[...] = jnp.zeros((SMALL_ROWS, width), F32)

    def send_act(j):
        return pair_copy(X_ACT + j, act.at[j, :, other_half], actp.at[j])

    def send_gp(j):
        return pair_copy(X_GP + j, gp.at[j, :, other_half], gpp.at[j])

    def mlp(i, carry):
        @pl.when(i < chunks)
        def _():
            cols = pl.ds(pl.multiple_of(i * width, 128), width)
            w1 = wfc1[:, cols]
            w2 = wfc2[cols, :]
            pre = dot_nn(n2[0:local_len, :], w1) + b1_ref[:, cols]
            phi = 0.5 * (1.0 + lax.erf(pre * ROOT_HALF))
            activated = (pre * phi).astype(BF16)
            act[i] = activated
            send_act(i).start()
            slope = phi + pre * jnp.exp(-0.5 * pre * pre) / ROOT_TWO_PI
            grad_pre = (dot_nt(cot_ref[...], w2) * slope).astype(BF16)
            gp[i] = grad_pre
            send_gp(i).start()
            sm[pl.ds(prompt_count + 7 + i, 1), :] = column_sum(grad_pre.astype(F32))
            acc_out[...] += dot_nn(activated, w2)
            acc_dn[...] += dot_nt(grad_pre, w1)

        @pl.when(i > 0)
        def _():
            j = i - 1
            send_act(j).wait_recv()
            grads2 = dot_tn(act[j, :, my_half], cot_ref[...]) + dot_tn(actp[j], cotp[...])
            rows = half_w // 4
            for a in range(2):
                for c in range(2):
                    for q in range(2):
                        for e in range(2):
                            r = (2 * a + c) * rows + e * blk
                            units[j, a, c, 2 * q + e] = grads2[
                                r : r + blk, q * half_w : (q + 1) * half_w
                            ].astype(BF16)
            stage_one(j).start()
            send_gp(j).wait_recv()
            store_rows(
                4 + j,
                dot_nn(n2t[:, 0:local_len], gp[j, :, my_half])
                + dot_nn(n2t[:, local_len:], gpp[j]),
            )
            stage_one(4 + j).start()

        return carry

    lax.fori_loop(0, chunks + 1, mlp, 0)

    grad_out = cot_ref[...].astype(F32)
    layer_out_ref[...] = (mid[...] + acc_out[...] + b2_ref[...]).astype(BF16)
    grad_n2 = acc_dn[...]
    sm[prompt_count + 11 : prompt_count + 12, :] = column_sum(grad_out)
    sm[prompt_count + 5 : prompt_count + 6, :] = column_sum(grad_n2 * xh2[...])
    sm[prompt_count + 6 : prompt_count + 7, :] = column_sum(grad_n2)
    grad_mid = grad_out + norm_back(grad_n2, xh2[...], r2[...], g2_ref[...])
    mid[...] = grad_mid
    branch = grad_mid.astype(BF16)
    gb[...] = branch
    send_gb = pair_copy(X_GB, gb.at[:, other_half], gbp)
    send_gb.start()
    sm[prompt_count + 4 : prompt_count + 5, :] = column_sum(branch.astype(F32))
    grad_att = dot_nt(branch, wout[...]).astype(BF16)
    ga_row[s] = grad_att
    product = grad_att.astype(F32) * o32[...]
    for hp in range(head_pairs):
        block = product[:, hp * 128 : (hp + 1) * 128]
        for h in range(2):
            keep = first_head_f32 if h == 0 else jnp.logical_not(first_head_f32)
            total = jnp.sum(jnp.where(keep, block, 0.0), axis=-1, keepdims=True)
            centre[...] = jnp.where(stat_lane == 2 * hp + h, total, centre[...])
    stat[s, 0:16, :] = lse[...].T[0:16, :]
    stat[s, 16:32, :] = centre[...].T[0:16, :]

    def ga_send(d):
        return remote(ga_row.at[s], ga_row.at[s], ga_s.at[d - 1], ga_r.at[s], (b, along(d)))

    def stat_send(d):
        return remote(stat.at[s], stat.at[s], st_s.at[d - 1], st_r.at[s], (b, along(d)))

    def ga_recv(j):
        return remote(ga_row.at[j], ga_row.at[j], ga_s.at[0], ga_r.at[j], (b, j))

    def stat_recv(j):
        return remote(stat.at[j], stat.at[j], st_s.at[0], st_r.at[j], (b, j))

    for d in range(1, groups):

        @pl.when(needs(along(d), s))
        def _(d=d):
            stat_send(d).start()
            ga_send(d).start()

    send_att.wait_recv()
    send_gb.wait_recv()
    store_rows(
        8, dot_tn(att[0:local_len, :], gb[:, my_half]) + dot_tn(att[local_len:, :], gbp[...])
    )
    stage_one(8).start()

    prompt_row = lax.broadcasted_iota(jnp.int32, (PROMPT_PAD, 1), 0)
    prompt_bias = jnp.where(prompt_row < prompt_count, 0.0, MASKED_SCORE)
    dqkv[local_len:tok_block, :] = jnp.zeros((PROMPT_PAD, 3 * width), BF16)

    def own_queries(hp, carry):
        lanes = lanes_of(hp)
        q = q_row[own_rows, lanes]
        k = k_row[:, lanes]
        v = v_row[:, lanes]
        g = ga_row[s, :, lanes]
        parts = []
        d_pk = jnp.zeros((PROMPT_PAD, 2 * HEAD_DIM), F32)
        d_pv = jnp.zeros((PROMPT_PAD, 2 * HEAD_DIM), F32)
        for h in range(2):
            head = 2 * hp + h
            qm = q * head_mask[h]
            gm = g * head_mask[h]
            here = stat_lane == head
            lse_col = jnp.sum(jnp.where(here, lse[...], 0.0), axis=-1, keepdims=True)
            centre_col = jnp.sum(jnp.where(here, centre[...], 0.0), axis=-1, keepdims=True)
            probs = jnp.exp(dot_nt(qm, k) + bias[...] - lse_col)
            grad_scores = (probs * (dot_nt(gm, v) - centre_col)).astype(BF16)
            parts.append(dot_nn(grad_scores, k))
            lse_line = stat[s, pl.ds(head, 1), :]
            centre_line = stat[s, pl.ds(16 + head, 1), :]
            kp = k_row[row_len:key_len, lanes]
            vp = v_row[row_len:key_len, lanes]
            probs_p = jnp.exp(dot_nt(kp, qm) + prompt_bias - lse_line)
            grads_p = (probs_p * (dot_nt(vp, gm) - centre_line)).astype(BF16)
            d_pk = d_pk + dot_nn(grads_p, qm)
            d_pv = d_pv + dot_nn(probs_p.astype(BF16), gm)
        grad_q = jnp.where(first_head_f32, parts[0], parts[1]) * SCALE
        dqkv[0:local_len, lanes] = grad_q.astype(BF16)
        k_lanes = pl.ds(pl.multiple_of(width + hp * 128, 128), 128)
        v_lanes = pl.ds(pl.multiple_of(2 * width + hp * 128, 128), 128)
        dqkv[local_len:tok_block, k_lanes] = d_pk.astype(BF16)
        dqkv[local_len:tok_block, v_lanes] = d_pv.astype(BF16)
        advance_one(unit_of(hp))
        return carry

    lax.fori_loop(0, head_pairs, own_queries, 0)
    for p in range(head_pairs, 2 * chunks):
        advance_one(unit_of(p))

    dk[...] = jnp.zeros((local_len, width), F32)
    dv[...] = jnp.zeros((local_len, width), F32)

    def own_keys(j):
        cols = pl.ds(pl.multiple_of(j * local_len, local_len), local_len)
        mask = bias[:, cols]

        def body(hp, carry):
            lanes = lanes_of(hp)
            k = k_row[own_rows, lanes]
            v = v_row[own_rows, lanes]
            q = q_row[cols, lanes]
            g = ga_row[j, :, lanes]
            d_k = dk[:, lanes]
            d_v = dv[:, lanes]
            for h in range(2):
                head = 2 * hp + h
                qm = q * head_mask[h]
                gm = g * head_mask[h]
                lse_line = stat[j, pl.ds(head, 1), :]
                centre_line = stat[j, pl.ds(16 + head, 1), :]
                probs = jnp.exp(dot_nt(k, qm) + mask - lse_line)
                grad_scores = (probs * (dot_nt(v, gm) - centre_line)).astype(BF16)
                d_k = d_k + dot_nn(grad_scores, qm)
                d_v = d_v + dot_nn(probs.astype(BF16), gm)
            dk[:, lanes] = d_k
            dv[:, lanes] = d_v
            return carry

        lax.fori_loop(0, head_pairs, body, 0)

    def key_step(k, carry):
        j = order(k)

        @pl.when(needs(s, j))
        def _():
            @pl.when(k > 0)
            def _():
                stat_recv(j).wait_recv()
                ga_recv(j).wait_recv()

            own_keys(j)

        @pl.when(k == 0)
        def _():
            advance_one(8)

        @pl.when(k < 3)
        def _():
            for e in range(3):
                advance_two(unit_of(3 * k + e) * jnp.where(3 * k + e < 8, 1, 0) + 8 * jnp.where(3 * k + e < 8, 0, 1))

        return carry

    lax.fori_loop(0, groups, key_step, 0)
    start_three(0)
    start_three(1)

    dqkv[0:local_len, width : 2 * width] = dk[...].astype(BF16)
    dqkv[0:local_len, 2 * width :] = dv[...].astype(BF16)
    send_qkv = pair_copy(X_QKV, dqkv.at[:, other_qkv], dqp)
    send_qkv.start()

    grad_normed = dot_nt(dqkv[...], wqkv[...])
    grad_tok = grad_normed[0:local_len, :]
    grad_pro = grad_normed[local_len : local_len + prompt_count, :]
    scaled1, inverse1 = norm_stats(tokens_ref[...].astype(F32))
    grad_input_ref[...] = (mid[...] + norm_back(grad_tok, scaled1, inverse1, gain1)).astype(BF16)
    p_scaled, p_inverse = norm_stats(prompts_ref[...])
    sm[0:prompt_count, :] = norm_back(grad_pro, p_scaled, p_inverse, gain1)
    sm[prompt_count : prompt_count + 1, :] = column_sum(grad_tok * scaled1) + column_sum(
        grad_pro * p_scaled
    )
    sm[prompt_count + 1 : prompt_count + 2, :] = column_sum(grad_tok) + column_sum(grad_pro)
    sm[prompt_count + 2 : prompt_count + 3, :] = column_sum(dqkv[:, :width].astype(F32))
    sm[prompt_count + 3 : prompt_count + 4, :] = column_sum(dqkv[:, 2 * width :].astype(F32))
    send_sm = pair_copy(X_SMALL, sm.at[:, other_half], smp)
    send_sm.start()

    send_norm.wait_recv()
    nbt[...] = nb[...].T
    send_qkv.wait_recv()
    for part in range(3):
        lane = pl.ds(pl.multiple_of(core * qkv_half + part * half_w, 128), half_w)
        store_rows(
            9 + part,
            dot_nn(nbt[:, 0:tok_block], dqkv[:, lane])
            + dot_nn(nbt[:, tok_block:], dqp[:, part * half_w : (part + 1) * half_w]),
        )
        stage_one(9 + part).start()

    quarter = SMALL_ROWS // 4
    send_sm.wait_recv()
    small = sm[:, my_half] + smp[...]
    for a in range(2):
        for c in range(2):
            s0[a, c] = small[(2 * a + c) * quarter : (2 * a + c + 1) * quarter, :]

    small_one = remote(s0.at[1 - h1], rs1, one_s.at[12], one_r.at[12], nb1)
    small_one.start()
    finish_three(0)
    finish_three(1)
    small_one.wait_recv()
    s1b[...] = s0[h1] + rs1[...]
    small_two = remote(s1b.at[1 - h2], rs2, two_s.at[12], two_r.at[12], nb2)
    small_two.start()
    for u in range(9, 12):
        advance_one(u)
    small_two.wait_recv()
    rs3[s] = s1b[h2] + rs2[...]

    def small_three(d):
        return remote(
            rs3.at[s], rs3.at[s], three_s.at[3, d - 1], three_r.at[3, s], (b, along(d))
        )

    def small_three_recv(j):
        return remote(rs3.at[j], rs3.at[j], three_s.at[3, 0], three_r.at[3, j], (b, j))

    for d in range(1, groups):
        small_three(d).start()
    for g in range(2):
        start_gather_two(g)
    for u in range(9, 12):
        advance_two(u)
    start_three(2)
    for d in range(1, groups):
        small_three_recv(along(d)).wait_recv()
    total = rs3[0]
    for j in range(1, groups):
        total = total + rs3[j]
    s3[...] = total
    small_keep = pltpu.make_async_copy(s3, small_ref.at[core, h1, h2], loc_sem.at[3])
    small_keep.start()
    small_gather = remote(s3, small_ref.at[core, h1, h2], ag1_s.at[3], ag1_r.at[3], nb2)
    small_gather.start()
    for g in range(2):
        start_gather_pair(g)
    finish_three(2)
    small_keep.wait()
    small_gather.wait_recv()
    small_gather_two = remote(
        small_ref.at[core, h1], small_ref.at[core, h1], ag2_s.at[3], ag2_r.at[3], nb1
    )
    small_gather_two.start()
    start_gather_two(2)
    small_gather_two.wait_recv()
    small_pair = pair_copy(X_FINAL + 3, small_ref.at[core], small_ref.at[core])
    small_pair.start()
    start_gather_pair(2)

    small_pair.wait()
    for g in range(3):
        gather_pair(g).wait()
        gather_one(g).wait_send()
        gather_two(g).wait_send()
        for d in range(1, groups):
            stage_three(g, d).wait_send()
    small_one.wait_send()
    small_two.wait_send()
    small_gather.wait_send()
    small_gather_two.wait_send()
    for d in range(1, groups):
        small_three(d).wait_send()

        @pl.when(needs(along(d), s))
        def _(d=d):
            token_send(d).wait_send()
            stat_send(d).wait_send()
            ga_send(d).wait_send()

    def drain(u, carry):
        stage_one(u).wait_send()
        stage_two(u).wait_send()
        return carry

    lax.fori_loop(0, 12, drain, 0)

    def drain_mlp(j, carry):
        send_act(j).wait_send()
        send_gp(j).wait_send()
        return carry

    lax.fori_loop(0, chunks, drain_mlp, 0)
    for copy in (send_cot, send_norm, send_att, send_n2, send_gb, send_qkv, send_sm):
        copy.wait_send()


def finish_kernel(
    width,
    prompt_count,
    layer_in,
    grad_in,
    final_ref,
    small_ref,
    layer_out_ref,
    grad_input_ref,
    gp_ref,
    g1_ref,
    s1_ref,
    wqkv_ref,
    qb_ref,
    vb_ref,
    wout_ref,
    ob_ref,
    g2_ref,
    s2_ref,
    wfc1_ref,
    b1_ref,
    wfc2_ref,
    b2_ref,
    small,
):
    layer_out_ref[...] = layer_in[...]
    grad_input_ref[...] = grad_in[...]
    half_w = width // 2
    blk = final_ref.shape[5]
    for c in range(2):
        for a in range(2):
            for e in range(2):
                for i in range(4):
                    q, r = i // 2, i % 2
                    row = c * half_w + (2 * a + e) * (half_w // 4) + r * blk
                    wfc2_ref[row : row + blk, q * half_w : (q + 1) * half_w] = final_ref[
                        0, c, a, e, i
                    ].astype(F32)
                    rows = slice((2 * a + e) * blk, (2 * a + e + 1) * blk)
                    col = i * width + c * half_w
                    wfc1_ref[rows, col : col + half_w] = final_ref[1, c, a, e, i].astype(F32)
                    if i == 0:
                        wout_ref[rows, c * half_w : (c + 1) * half_w] = final_ref[
                            2, c, a, e, 0
                        ].astype(F32)
                    else:
                        col = c * 3 * half_w + (i - 1) * half_w
                        wqkv_ref[rows, col : col + half_w] = final_ref[2, c, a, e, i].astype(F32)
    quarter = small_ref.shape[3]
    for c in range(2):
        for a in range(2):
            for e in range(2):
                r = (2 * a + e) * quarter
                small[r : r + quarter, c * half_w : (c + 1) * half_w] = small_ref[c, a, e]
    gp_ref[...] = small[0:prompt_count, :]
    for k, ref in enumerate((g1_ref, s1_ref, qb_ref, vb_ref, ob_ref, g2_ref, s2_ref)):
        ref[...] = small[prompt_count + k : prompt_count + k + 1, :]
    for k in range(b1_ref.shape[1] // width):
        r = prompt_count + 7 + k
        b1_ref[:, k * width : (k + 1) * width] = small[r : r + 1, :]
    r = prompt_count + 7 + b1_ref.shape[1] // width
    b2_ref[...] = small[r : r + 1, :]


def local(
    tokens,
    segments,
    prompts,
    ln1_gain,
    ln1_shift,
    w_qkv,
    q_bias,
    v_bias,
    w_out,
    out_bias,
    ln2_gain,
    ln2_shift,
    w_fc1,
    fc1_bias,
    w_fc2,
    fc2_bias,
    cotangent,
):
    groups = lax.axis_size("seq")
    batch = lax.axis_size("batch")
    row_count, local_len, width = tokens.shape
    ff = w_fc1.shape[1]
    prompt_count = prompts.shape[0]
    assert row_count == 1 and groups == 4 and batch % GROUP == 0 and ff == 4 * width
    table = need_table(groups, local_len)
    dims = (groups, local_len, width, ff, prompt_count, table)
    row_len = groups * local_len
    half_w = width // 2
    blk = width // groups // 4
    tok_block = local_len + PROMPT_PAD
    quarter = SMALL_ROWS // 4

    def row(v):
        return v.reshape(1, -1)

    vmem = pl.BlockSpec(memory_space=pltpu.VMEM)
    hbm = pl.BlockSpec(memory_space=pl.ANY)
    dma = pltpu.SemaphoreType.DMA
    V = pltpu.VMEM
    scratch = [
        V((width, 3 * width), BF16),
        V((width, width), BF16),
        V((width, ff), BF16),
        V((ff, width), BF16),
        V((groups, local_len, width), BF16),
        V((2 * tok_block, width), BF16),
        V((width, 2 * tok_block), BF16),
        V((row_len, width), BF16),
        V((row_len + PROMPT_PAD, width), BF16),
        V((row_len + PROMPT_PAD, width), BF16),
        V((local_len, row_len + PROMPT_PAD), F32),
        V((local_len, width), F32),
        V((2 * local_len, width), BF16),
        V((local_len, 128), F32),
        V((local_len, 128), F32),
        V((local_len, width), F32),
        V((local_len, width), F32),
        V((local_len, 1), F32),
        V((2 * local_len, width), BF16),
        V((width, 2 * local_len), BF16),
        V((4, local_len, width), BF16),
        V((4, local_len, width), BF16),
        V((4, local_len, half_w), BF16),
        V((4, local_len, half_w), BF16),
        V((local_len, width), F32),
        V((local_len, width), F32),
        V((local_len, width), BF16),
        V((local_len, width), BF16),
        V((local_len, half_w), BF16),
        V((groups, local_len, width), BF16),
        V((groups, 32, local_len), F32),
        V((local_len, width), F32),
        V((local_len, width), F32),
        V((tok_block, 3 * width), BF16),
        V((tok_block, 3 * half_w), BF16),
        V((12, 2, 2, 4, blk, half_w), BF16),
        V((12, 2, 4, blk, half_w), BF16),
        V((12, 4, blk, half_w), BF16),
        V((3, groups, 4, blk, half_w), BF16),
        V((3, 4, blk, half_w), BF16),
        V((SMALL_ROWS, width), F32),
        V((SMALL_ROWS, half_w), F32),
        V((2, 2, quarter, half_w), F32),
        V((2, quarter, half_w), F32),
        V((2, quarter, half_w), F32),
        V((quarter, half_w), F32),
        V((groups, quarter, half_w), F32),
        V((quarter, half_w), F32),
        dma((4,)),
        dma((3,)),
        dma((groups,)),
        dma((X_COUNT,)),
        dma((X_COUNT,)),
        dma((3,)),
        dma((groups,)),
        dma((3,)),
        dma((groups,)),
        dma((13,)),
        dma((13,)),
        dma((13,)),
        dma((13,)),
        dma((4, 3)),
        dma((4, groups)),
        dma((4,)),
        dma((4,)),
        dma((4,)),
        dma((4,)),
        dma((4,)),
    ]
    specs = [vmem] * 17
    for index in (5, 8, 12, 14):
        specs[index] = hbm
    layer_out, grad_input, final, small = pl.pallas_call(
        functools.partial(layer_kernel, dims),
        out_shape=(
            jax.ShapeDtypeStruct((local_len, width), BF16),
            jax.ShapeDtypeStruct((local_len, width), BF16),
            jax.ShapeDtypeStruct((3, 2, 2, 2, 4, blk, half_w), BF16),
            jax.ShapeDtypeStruct((2, 2, 2, quarter, half_w), F32),
        ),
        in_specs=specs,
        out_specs=(vmem, vmem, hbm, hbm),
        scratch_shapes=scratch,
        compiler_params=pltpu.CompilerParams(
            collective_id=0, has_side_effects=True, vmem_limit_bytes=67043328
        ),
        name="layer",
    )(
        tokens.reshape(local_len, width),
        segments,
        prompts,
        row(ln1_gain),
        row(ln1_shift),
        w_qkv,
        row(q_bias),
        row(v_bias),
        w_out,
        row(out_bias),
        row(ln2_gain),
        row(ln2_shift),
        w_fc1,
        row(fc1_bias),
        w_fc2,
        row(fc2_bias),
        cotangent.reshape(local_len, width),
    )
    if batch > GROUP:
        rings = [list(range(k, batch, GROUP)) for k in range(GROUP)]
        final, small = lax.psum((final, small), "batch", axis_index_groups=rings)
    rows_z = width // groups

    def flat(n):
        return jax.ShapeDtypeStruct((1, n), F32)

    outs = pl.pallas_call(
        functools.partial(finish_kernel, width, prompt_count),
        out_shape=(
            jax.ShapeDtypeStruct((local_len, width), BF16),
            jax.ShapeDtypeStruct((local_len, width), BF16),
            jax.ShapeDtypeStruct((prompt_count, width), F32),
            flat(width),
            flat(width),
            jax.ShapeDtypeStruct((rows_z, 3 * width), F32),
            flat(width),
            flat(width),
            jax.ShapeDtypeStruct((rows_z, width), F32),
            flat(width),
            flat(width),
            flat(width),
            jax.ShapeDtypeStruct((rows_z, ff), F32),
            flat(ff),
            jax.ShapeDtypeStruct((ff // groups, width), F32),
            flat(width),
        ),
        in_specs=[vmem] * 4,
        out_specs=tuple([vmem] * 16),
        scratch_shapes=[pltpu.VMEM((SMALL_ROWS, width), F32)],
        compiler_params=pltpu.CompilerParams(vmem_limit_bytes=40 * 1024 * 1024),
        name="finish",
    )(layer_out, grad_input, final, small)
    return tuple(
        o.reshape((1, local_len, width)) if i < 2 else (o.reshape(-1) if o.shape[0] == 1 else o)
        for i, o in enumerate(outs)
    )


def solution(mesh):
    tok = P("batch", "seq", None)
    in_specs = (tok, P("batch", "seq")) + (P(),) * 14 + (tok,)
    out_specs = (
        tok,
        tok,
        P(),
        P(),
        P(),
        P("seq", None),
        P(),
        P(),
        P("seq", None),
        P(),
        P(),
        P(),
        P("seq", None),
        P(),
        P("seq", None),
        P(),
    )
    return jax.shard_map(local, mesh=mesh, in_specs=in_specs, out_specs=out_specs, check_vma=False)
```

```python
import functools

import jax
import jax.numpy as jnp
from jax import lax
from jax.experimental import pallas as pl
from jax.experimental.pallas import tpu as pltpu
from jax.sharding import PartitionSpec as P

HEAD_DIM = 64
IMAGE_TOKENS = (101, 197, 577)
EPSILON = 1e-06
MASKED_SCORE = -1e30
ROOT_HALF = 0.7071067811865476
ROOT_TWO_PI = 2.5066282746310002
SCALE = HEAD_DIM ** (-0.5)
GROUP = 8
PROMPT_PAD = 64
SMALL_ROWS = 64
F32 = jnp.float32
BF16 = jnp.bfloat16
MESH = pl.DeviceIdType.MESH


def dot_nn(a, b):
    return lax.dot_general(a, b, (((1,), (0,)), ((), ())), preferred_element_type=F32)


def dot_nt(a, b):
    return lax.dot_general(a, b, (((1,), (1,)), ((), ())), preferred_element_type=F32)


def dot_tn(a, b):
    return lax.dot_general(a, b, (((0,), (0,)), ((), ())), preferred_element_type=F32)


def need_table(groups, local_len):
    row_len = groups * local_len
    table = [[0] * groups for _ in range(groups)]
    for size in IMAGE_TOKENS:
        for start in range(0, row_len, size):
            first = start // local_len
            last = (min(start + size, row_len) - 1) // local_len
            for a in range(first, last + 1):
                for b in range(first, last + 1):
                    table[a][b] = 1
    return table


def norm_stats(values):
    centred = values - jnp.mean(values, axis=-1, keepdims=True)
    inverse = lax.rsqrt(jnp.mean(centred * centred, axis=-1, keepdims=True) + EPSILON)
    return centred * inverse, inverse


def norm_back(grad_out, scaled, inverse, gain):
    inner = grad_out * gain
    return inverse * (
        inner
        - jnp.mean(inner, axis=-1, keepdims=True)
        - scaled * jnp.mean(inner * scaled, axis=-1, keepdims=True)
    )


def line(ref):
    return ref[...].reshape(1, -1)


def column_sum(values):
    return jnp.sum(values, axis=0, keepdims=True)


X_COT, X_N2, X_ATT, X_NORM, X_GB, X_Q, X_KV, X_SMALL, X_FINAL, X_ACT, X_GP = 0, 1, 2, 3, 4, 5, 6, 8, 9, 14, 18
X_COUNT = 22
SLOTS = ((0, 4), (4, 4), (8, 2), (10, 2))
SMALL = 4


def layer_kernel(
    dims,
    tokens_ref,
    seg_ref,
    prompts_ref,
    g1_ref,
    s1_ref,
    wqkv_hbm,
    qb_ref,
    vb_ref,
    wout_hbm,
    ob_ref,
    g2_ref,
    s2_ref,
    wfc1_hbm,
    b1_ref,
    wfc2_hbm,
    b2_ref,
    cot_ref,
    layer_out_ref,
    grad_input_ref,
    final_ref,
    small_ref,
    wqkv,
    wout,
    wfc1,
    wfc2,
    tokrow,
    nb,
    nbt,
    q_row,
    k_row,
    v_row,
    bias,
    o32,
    att,
    lse,
    centre,
    mid,
    xh2,
    r2,
    n2,
    n2t,
    act,
    gp,
    actp,
    gpp,
    b1s,
    acc_out,
    acc_dn,
    cotp,
    gb,
    gbp,
    ga_row,
    stat,
    dk,
    dv,
    dqkv,
    dqp,
    units,
    r1,
    r2u,
    r3,
    a3,
    sm,
    smp,
    s0,
    rs1,
    s1b,
    rs2,
    rs3,
    s3,
    wsem,
    tok_s,
    tok_r,
    pair_s,
    pair_r,
    ga_s,
    ga_r,
    st_s,
    st_r,
    one_s,
    one_r,
    two_s,
    two_r,
    three_s,
    three_r,
    loc_sem,
    ag1_s,
    ag1_r,
    ag2_s,
    ag2_r,
):
    groups, local_len, width, ff, prompt_count, table = dims
    row_len = groups * local_len
    head_pairs = width // (2 * HEAD_DIM)
    chunks = ff // width
    half_w = width // 2
    key_len = row_len + PROMPT_PAD
    zrows = width // groups

    b = lax.axis_index("batch")
    s = lax.axis_index("seq")
    base = (b // GROUP) * GROUP
    core = lax.rem(b, 2)
    xb = lax.rem(b // 2, 2)
    yb = lax.rem(b // 4, 2)
    h1 = xb * (1 - core) + yb * core
    h2 = yb * (1 - core) + xb * core

    def place(x, y, c):
        return base + y * 4 + x * 2 + c

    nb1 = (place(xb + (1 - core) * (1 - 2 * xb), yb + core * (1 - 2 * yb), core), s)
    nb2 = (place(xb + core * (1 - 2 * xb), yb + (1 - core) * (1 - 2 * yb), core), s)
    pair = (place(xb, yb, 1 - core), s)

    def along(d):
        return lax.rem(s + d, groups)

    def needs(a, c):
        flag = jnp.int32(0)
        for i in range(groups):
            for j in range(groups):
                if table[i][j]:
                    flag = flag + jnp.where(a == i, 1, 0) * jnp.where(c == j, 1, 0)
        return flag > 0

    def remote(src, dst, send, recv, to):
        return pltpu.make_async_remote_copy(
            src_ref=src, dst_ref=dst, send_sem=send, recv_sem=recv, device_id=to, device_id_type=MESH
        )

    barrier = pltpu.get_barrier_semaphore()
    for peer in (pair, nb1, nb2):
        pl.semaphore_signal(barrier, inc=1, device_id=peer, device_id_type=MESH)
    for d in range(1, groups):
        pl.semaphore_signal(barrier, inc=1, device_id=(b, along(d)), device_id_type=MESH)

    loads = [
        pltpu.make_async_copy(wqkv_hbm, wqkv, wsem.at[0]),
        pltpu.make_async_copy(wout_hbm, wout, wsem.at[1]),
        pltpu.make_async_copy(wfc1_hbm, wfc1, wsem.at[2]),
        pltpu.make_async_copy(wfc2_hbm, wfc2, wsem.at[3]),
    ]
    loads[0].start()
    pl.semaphore_wait(barrier, 2 + groups)

    def token_send(d):
        return remote(
            tokens_ref, tokrow.at[s], tok_s.at[d - 1], tok_r.at[s], (b, along(d))
        )

    def token_recv(j):
        return remote(tokens_ref, tokrow.at[j], tok_s.at[0], tok_r.at[j], (b, j))

    for d in range(1, groups):

        @pl.when(needs(along(d), s))
        def _(d=d):
            token_send(d).start()

    for load in loads[1:]:
        load.start()

    def pair_copy(index, src, dst):
        return remote(src, dst, pair_s.at[index], pair_r.at[index], pair)

    my_half = pl.ds(pl.multiple_of(core * half_w, 128), half_w)
    other_half = pl.ds(pl.multiple_of((1 - core) * half_w, 128), half_w)

    send_cot = pair_copy(X_COT, cot_ref, cotp)
    send_cot.start()

    gain1 = line(g1_ref)
    shift1 = line(s1_ref)
    for i in range(chunks):
        b1s[i : i + 1, :] = b1_ref[i * width : (i + 1) * width].reshape(1, width)

    last = s * local_len + local_len - 1
    seg_last = seg_ref[:, local_len - 1 : local_len].astype(F32)
    inv_n = jnp.full((1, 1), 1.0 / IMAGE_TOKENS[-1], F32)
    for size in IMAGE_TOKENS[:-1]:
        inv_n = jnp.where(seg_last == (last // size).astype(F32), 1.0 / size, inv_n)
    q_pos = lax.broadcasted_iota(jnp.int32, (local_len, 1), 0) + s * local_len
    k_pos = lax.broadcasted_iota(jnp.int32, (1, key_len), 1)
    q_id = jnp.floor((q_pos.astype(F32) + 0.5) * inv_n)
    k_id = jnp.floor((k_pos.astype(F32) + 0.5) * inv_n)
    k_open = jnp.where(k_pos < row_len, 0.0, jnp.where(k_pos < row_len + prompt_count, 1.0, 0.0))
    k_id = jnp.where(k_pos < row_len, k_id, -1.0)
    bias[...] = jnp.where(q_id == k_id, 0.0, MASKED_SCORE * (1.0 - k_open))

    own_rows = pl.ds(pl.multiple_of(s * local_len, local_len), local_len)

    def project(normed, rows):
        q = dot_nn(normed, wqkv[:, :width]) + line(qb_ref)
        q_row[rows, :] = (q.astype(BF16).astype(F32) * SCALE).astype(BF16)
        k_row[rows, :] = dot_nn(normed, wqkv[:, width : 2 * width]).astype(BF16)
        v_row[rows, :] = (dot_nn(normed, wqkv[:, 2 * width :]) + line(vb_ref)).astype(BF16)

    p_scaled, p_inverse = norm_stats(prompts_ref[...])
    nb[local_len : local_len + PROMPT_PAD, :] = jnp.zeros((PROMPT_PAD, width), BF16)
    nb[local_len : local_len + prompt_count, :] = (p_scaled * gain1 + shift1).astype(BF16)
    scaled1, _ = norm_stats(tokens_ref[...].astype(F32))
    nb[0:local_len, :] = (scaled1 * gain1 + shift1).astype(BF16)
    tok_block = local_len + PROMPT_PAD
    send_norm = pair_copy(X_NORM, nb.at[pl.ds(0, tok_block)], nb.at[pl.ds(tok_block, tok_block)])
    send_norm.start()

    loads[0].wait()
    project(nb[0:local_len, :], own_rows)
    p_low = nb[local_len:tok_block, :]
    k_row[row_len:key_len, :] = dot_nn(p_low, wqkv[:, width : 2 * width]).astype(BF16)
    v_row[row_len:key_len, :] = (dot_nn(p_low, wqkv[:, 2 * width :]) + line(vb_ref)).astype(BF16)

    def order(k):
        return lax.rem(s + k + jnp.where(k == 2, 1, 0) - jnp.where(k == 3, 1, 0), groups)

    def other_shard(k, carry):
        j = order(k)
        rows = pl.ds(pl.multiple_of(j * local_len, local_len), local_len)
        needed = needs(s, j)

        @pl.when(needed)
        def _():
            token_recv(j).wait_recv()
            scaled, _ = norm_stats(tokrow[j].astype(F32))
            project((scaled * gain1 + shift1).astype(BF16), rows)

        @pl.when(jnp.logical_not(needed))
        def _():
            k_row[rows, :] = jnp.zeros((local_len, width), BF16)
            v_row[rows, :] = jnp.zeros((local_len, width), BF16)

        return carry

    send_norm.wait_recv()
    nbt[...] = nb[...].T
    lax.fori_loop(1, groups, other_shard, 0)

    pair_lane = lax.broadcasted_iota(jnp.int32, (1, 2 * HEAD_DIM), 1)
    first_head = jnp.where(pair_lane < HEAD_DIM, 1.0, 0.0)
    head_mask = (first_head.astype(BF16), (1.0 - first_head).astype(BF16))
    first_head_f32 = pair_lane < HEAD_DIM
    stat_lane = lax.broadcasted_iota(jnp.int32, (local_len, 128), 1)

    def lanes_of(hp):
        return pl.ds(pl.multiple_of(hp * 2 * HEAD_DIM, 128), 2 * HEAD_DIM)

    lse[...] = jnp.zeros((local_len, 128), F32)
    centre[...] = jnp.zeros((local_len, 128), F32)

    def attend(hp, carry):
        lanes = lanes_of(hp)
        q = q_row[own_rows, lanes]
        k = k_row[:, lanes]
        v = v_row[:, lanes]
        outs = []
        for h in range(2):
            scores = dot_nt(q * head_mask[h], k) + bias[...]
            highest = jnp.max(scores, axis=-1, keepdims=True)
            weights = jnp.exp(scores - highest)
            total = jnp.sum(weights, axis=-1, keepdims=True)
            outs.append(dot_nn(weights.astype(BF16), v) / total)
            lse[...] = jnp.where(stat_lane == 2 * hp + h, highest + jnp.log(total), lse[...])
        combined = jnp.where(first_head_f32, outs[0], outs[1])
        o32[:, lanes] = combined
        att[0:local_len, lanes] = combined.astype(BF16)
        return carry

    lax.fori_loop(0, head_pairs, attend, 0)
    own = pl.ds(0, local_len)
    theirs = pl.ds(local_len, local_len)
    send_att = pair_copy(X_ATT, att.at[own], att.at[theirs])
    send_att.start()

    loads[1].wait()
    mid[...] = (
        tokens_ref[...].astype(F32) + dot_nn(att[0:local_len, :], wout[...]) + line(ob_ref)
    )
    scaled2, inverse2 = norm_stats(mid[...])
    xh2[...] = scaled2
    r2[...] = inverse2
    n2[0:local_len, :] = (scaled2 * line(g2_ref) + line(s2_ref)).astype(BF16)
    send_n2 = pair_copy(X_N2, n2.at[own], n2.at[theirs])
    send_n2.start()
    acc_out[...] = jnp.zeros((local_len, width), F32)
    acc_dn[...] = jnp.zeros((local_len, width), F32)
    n2t[:, 0:local_len] = n2[0:local_len, :].T
    loads[2].wait()
    loads[3].wait()
    send_n2.wait_recv()
    n2t[:, local_len:] = n2[local_len:, :].T
    send_cot.wait_recv()

    blk = zrows // 4

    def unit_of(p):
        return p // 2 + 4 * lax.rem(p, 2)

    def store_rows(u, grads):
        for z in range(groups):
            for a in range(2):
                for c in range(2):
                    r = z * zrows + (2 * a + c) * blk
                    units[u, a, c, z] = grads[r : r + blk, :].astype(BF16)

    def stage_one(u):
        return remote(units.at[u, 1 - h1], r1.at[u], one_s.at[u], one_r.at[u], nb1)

    def stage_two(u):
        return remote(units.at[u, h1, 1 - h2], r2u.at[u], two_s.at[u], two_r.at[u], nb2)

    def advance_one(u):
        stage_one(u).wait_recv()
        units[u, h1] = (units[u, h1].astype(F32) + r1[u].astype(F32)).astype(BF16)
        stage_two(u).start()

    def advance_two(u):
        stage_two(u).wait_recv()
        r2u[u] = (units[u, h1, h2].astype(F32) + r2u[u].astype(F32)).astype(BF16)

    def stage_three_fc2(u):
        return remote(
            r2u.at[u], r3.at[s, pl.ds(0, 4)], three_s.at[u, 0], three_r.at[0, s], (b, u)
        )

    def stage_three(u, d):
        t = along(d)
        return remote(r2u.at[u, t], r3.at[s, u], three_s.at[u, d - 1], three_r.at[u, s], (b, t))

    def start_three(u):
        if u < 4:

            @pl.when(s != u)
            def _():
                stage_three_fc2(u).start()

        else:
            for d in range(1, groups):
                stage_three(u, d).start()

    def drain_three(u):
        if u < 4:

            @pl.when(s != u)
            def _():
                stage_three_fc2(u).wait_send()

        else:
            for d in range(1, groups):
                stage_three(u, d).wait_send()

    def slots(g):
        return pl.ds(*SLOTS[g])

    def keep_final(g):
        return pltpu.make_async_copy(
            a3.at[slots(g)], final_ref.at[core, h1, h2, slots(g)], loc_sem.at[g]
        )

    def gather_one(g):
        return remote(
            a3.at[slots(g)],
            final_ref.at[core, h1, h2, slots(g)],
            ag1_s.at[g],
            ag1_r.at[g],
            nb2,
        )

    def gather_two(g):
        ref = final_ref.at[core, h1, :, slots(g)]
        return remote(ref, ref, ag2_s.at[g], ag2_r.at[g], nb1)

    def gather_pair(g):
        ref = final_ref.at[core, :, :, slots(g)]
        return pair_copy(X_FINAL + g, ref, ref)

    def finish_three(g):
        first, count = SLOTS[g]
        if g == 0:
            total = r2u[s].astype(F32)
            for d in range(1, groups):
                j = along(d)
                remote(
                    r2u.at[0], r3.at[j, pl.ds(0, 4)], three_s.at[0, 0], three_r.at[0, j], (b, j)
                ).wait_recv()
                total = total + r3[j, 0:4].astype(F32)
            a3[0:4] = total.astype(BF16)
        else:
            for u in range(first, first + count):
                total = r2u[u, s].astype(F32)
                for d in range(1, groups):
                    j = along(d)
                    remote(
                        r2u.at[u, 0], r3.at[j, u], three_s.at[u, 0], three_r.at[u, j], (b, j)
                    ).wait_recv()
                    total = total + r3[j, u].astype(F32)
                a3[u] = total.astype(BF16)
        keep_final(g).start()
        gather_one(g).start()

    def start_gather_two(g):
        keep_final(g).wait()
        gather_one(g).wait_recv()
        gather_two(g).start()

    def start_gather_pair(g):
        gather_two(g).wait_recv()
        gather_pair(g).start()

    def reduced(u):
        advance_two(u)
        start_three(u)

    sm[...] = jnp.zeros((SMALL_ROWS, width), F32)

    def send_act(j):
        return pair_copy(X_ACT + j, act.at[j, :, other_half], actp.at[j])

    def send_gp(j):
        return pair_copy(X_GP + j, gp.at[j, :, other_half], gpp.at[j])

    def mlp(i, carry):
        @pl.when(i < chunks)
        def _():
            cols = pl.ds(pl.multiple_of(i * width, 128), width)
            w1 = wfc1[:, cols]
            w2 = wfc2[cols, :]
            pre = dot_nn(n2[0:local_len, :], w1) + b1s[pl.ds(i, 1), :]
            phi = 0.5 * (1.0 + lax.erf(pre * ROOT_HALF))
            activated = (pre * phi).astype(BF16)
            act[i] = activated
            send_act(i).start()
            slope = phi + pre * jnp.exp(-0.5 * pre * pre) / ROOT_TWO_PI
            grad_pre = (dot_nt(cot_ref[...], w2) * slope).astype(BF16)
            gp[i] = grad_pre
            send_gp(i).start()
            sm[pl.ds(prompt_count + 7 + i, 1), :] = column_sum(grad_pre.astype(F32))
            acc_out[...] += dot_nn(activated, w2)
            acc_dn[...] += dot_nt(grad_pre, w1)

        @pl.when(i > 0)
        def _():
            j = i - 1
            send_act(j).wait_recv()
            grads2 = dot_tn(act[j, :, my_half], cot_ref[...]) + dot_tn(actp[j], cotp[...])
            rows = half_w // 4
            for a in range(2):
                for c in range(2):
                    for q in range(2):
                        for e in range(2):
                            r = (2 * a + c) * rows + e * blk
                            units[j, a, c, 2 * q + e] = grads2[
                                r : r + blk, q * half_w : (q + 1) * half_w
                            ].astype(BF16)
            stage_one(j).start()
            send_gp(j).wait_recv()
            store_rows(
                4 + j,
                dot_nn(n2t[:, 0:local_len], gp[j, :, my_half])
                + dot_nn(n2t[:, local_len:], gpp[j]),
            )
            stage_one(4 + j).start()

        return carry

    lax.fori_loop(0, chunks + 1, mlp, 0)

    grad_out = cot_ref[...].astype(F32)
    layer_out_ref[...] = (mid[...] + acc_out[...] + line(b2_ref)).astype(BF16)
    grad_n2 = acc_dn[...]
    sm[prompt_count + 11 : prompt_count + 12, :] = column_sum(grad_out)
    sm[prompt_count + 5 : prompt_count + 6, :] = column_sum(grad_n2 * xh2[...])
    sm[prompt_count + 6 : prompt_count + 7, :] = column_sum(grad_n2)
    grad_mid = grad_out + norm_back(grad_n2, xh2[...], r2[...], line(g2_ref))
    mid[...] = grad_mid
    branch = grad_mid.astype(BF16)
    gb[...] = branch
    send_gb = pair_copy(X_GB, gb.at[:, other_half], gbp)
    send_gb.start()
    sm[prompt_count + 4 : prompt_count + 5, :] = column_sum(branch.astype(F32))
    grad_att = dot_nt(branch, wout[...]).astype(BF16)
    ga_row[s] = grad_att
    product = grad_att.astype(F32) * o32[...]
    for hp in range(head_pairs):
        block = product[:, hp * 128 : (hp + 1) * 128]
        for h in range(2):
            keep = first_head_f32 if h == 0 else jnp.logical_not(first_head_f32)
            total = jnp.sum(jnp.where(keep, block, 0.0), axis=-1, keepdims=True)
            centre[...] = jnp.where(stat_lane == 2 * hp + h, total, centre[...])
    stat[s, 0:16, :] = lse[...].T[0:16, :]
    stat[s, 16:32, :] = centre[...].T[0:16, :]

    def ga_send(d):
        return remote(ga_row.at[s], ga_row.at[s], ga_s.at[d - 1], ga_r.at[s], (b, along(d)))

    def stat_send(d):
        return remote(stat.at[s], stat.at[s], st_s.at[d - 1], st_r.at[s], (b, along(d)))

    def ga_recv(j):
        return remote(ga_row.at[j], ga_row.at[j], ga_s.at[0], ga_r.at[j], (b, j))

    def stat_recv(j):
        return remote(stat.at[j], stat.at[j], st_s.at[0], st_r.at[j], (b, j))

    for d in range(1, groups):

        @pl.when(needs(along(d), s))
        def _(d=d):
            stat_send(d).start()
            ga_send(d).start()

    send_att.wait_recv()
    send_gb.wait_recv()
    store_rows(
        8, dot_tn(att[0:local_len, :], gb[:, my_half]) + dot_tn(att[local_len:, :], gbp[...])
    )
    stage_one(8).start()

    prompt_row = lax.broadcasted_iota(jnp.int32, (PROMPT_PAD, 1), 0)
    prompt_bias = jnp.where(prompt_row < prompt_count, 0.0, MASKED_SCORE)
    dqkv[local_len:tok_block, :] = jnp.zeros((PROMPT_PAD, 3 * width), BF16)

    def own_queries(hp, carry):
        lanes = lanes_of(hp)
        q = q_row[own_rows, lanes]
        k = k_row[:, lanes]
        v = v_row[:, lanes]
        g = ga_row[s, :, lanes]
        parts = []
        d_pk = jnp.zeros((PROMPT_PAD, 2 * HEAD_DIM), F32)
        d_pv = jnp.zeros((PROMPT_PAD, 2 * HEAD_DIM), F32)
        for h in range(2):
            head = 2 * hp + h
            qm = q * head_mask[h]
            gm = g * head_mask[h]
            here = stat_lane == head
            lse_col = jnp.sum(jnp.where(here, lse[...], 0.0), axis=-1, keepdims=True)
            centre_col = jnp.sum(jnp.where(here, centre[...], 0.0), axis=-1, keepdims=True)
            probs = jnp.exp(dot_nt(qm, k) + bias[...] - lse_col)
            grad_scores = (probs * (dot_nt(gm, v) - centre_col)).astype(BF16)
            parts.append(dot_nn(grad_scores, k))
            lse_line = stat[s, pl.ds(head, 1), :]
            centre_line = stat[s, pl.ds(16 + head, 1), :]
            kp = k_row[row_len:key_len, lanes]
            vp = v_row[row_len:key_len, lanes]
            probs_p = jnp.exp(dot_nt(kp, qm) + prompt_bias - lse_line)
            grads_p = (probs_p * (dot_nt(vp, gm) - centre_line)).astype(BF16)
            d_pk = d_pk + dot_nn(grads_p, qm)
            d_pv = d_pv + dot_nn(probs_p.astype(BF16), gm)
        grad_q = jnp.where(first_head_f32, parts[0], parts[1]) * SCALE
        dqkv[0:local_len, lanes] = grad_q.astype(BF16)
        k_lanes = pl.ds(pl.multiple_of(width + hp * 128, 128), 128)
        v_lanes = pl.ds(pl.multiple_of(2 * width + hp * 128, 128), 128)
        dqkv[local_len:tok_block, k_lanes] = d_pk.astype(BF16)
        dqkv[local_len:tok_block, v_lanes] = d_pv.astype(BF16)

        @pl.when(hp > 1)
        def _():
            advance_one(unit_of(hp - 2))

        return carry

    lax.fori_loop(0, head_pairs, own_queries, 0)
    q_mine = pl.ds(pl.multiple_of(core * half_w, 128), half_w)
    q_other = pl.ds(pl.multiple_of((1 - core) * half_w, 128), half_w)
    send_q = pair_copy(X_Q, dqkv.at[pl.ds(0, local_len), q_other], dqp.at[0, pl.ds(0, local_len)])
    send_q.start()

    dk[...] = jnp.zeros((local_len, width), F32)
    dv[...] = jnp.zeros((local_len, width), F32)

    def own_keys(j):
        cols = pl.ds(pl.multiple_of(j * local_len, local_len), local_len)
        mask = bias[:, cols]

        def body(hp, carry):
            lanes = lanes_of(hp)
            k = k_row[own_rows, lanes]
            v = v_row[own_rows, lanes]
            q = q_row[cols, lanes]
            g = ga_row[j, :, lanes]
            d_k = dk[:, lanes]
            d_v = dv[:, lanes]
            for h in range(2):
                head = 2 * hp + h
                qm = q * head_mask[h]
                gm = g * head_mask[h]
                lse_line = stat[j, pl.ds(head, 1), :]
                centre_line = stat[j, pl.ds(16 + head, 1), :]
                probs = jnp.exp(dot_nt(k, qm) + mask - lse_line)
                grad_scores = (probs * (dot_nt(v, gm) - centre_line)).astype(BF16)
                d_k = d_k + dot_nn(grad_scores, qm)
                d_v = d_v + dot_nn(probs.astype(BF16), gm)
            dk[:, lanes] = d_k
            dv[:, lanes] = d_v
            return carry

        lax.fori_loop(0, head_pairs, body, 0)

    def wait_row(k):
        j = order(k)

        @pl.when(needs(s, j))
        def _():
            stat_recv(j).wait_recv()
            ga_recv(j).wait_recv()

    def key_step(k, carry):
        j = order(k)

        @pl.when(needs(s, j))
        def _():
            @pl.when(k > 0)
            def _():
                wait_row(k)

            own_keys(j)

        @pl.when(k == 0)
        def _():
            advance_one(2)
            advance_two(0)
            advance_two(4)
            send_q.wait_recv()
            store_rows(
                9,
                dot_nn(nbt[:, 0:local_len], dqkv[0:local_len, q_mine])
                + dot_nn(nbt[:, tok_block : tok_block + local_len], dqp[0, 0:local_len, :]),
            )
            stage_one(9).start()

        @pl.when(k == 1)
        def _():
            advance_one(6)
            advance_two(1)
            advance_two(5)

        @pl.when(k == 2)
        def _():
            for u in (0, 4, 1, 5):
                start_three(u)
            advance_one(3)
            reduced(2)

        @pl.when(k == 3)
        def _():
            advance_one(7)
            reduced(6)

        return carry

    lax.fori_loop(0, groups, key_step, 0)

    dqkv[0:local_len, width : 2 * width] = dk[...].astype(BF16)
    dqkv[0:local_len, 2 * width :] = dv[...].astype(BF16)
    send_kv = [
        pair_copy(
            X_KV + i,
            dqkv.at[:, pl.ds(pl.multiple_of((1 + i) * width + (1 - core) * half_w, 128), half_w)],
            dqp.at[1 + i],
        )
        for i in range(2)
    ]
    for copy in send_kv:
        copy.start()
    reduced(3)
    reduced(7)
    advance_one(8)

    grad_normed = dot_nt(dqkv[...], wqkv[...])
    for i in range(2):
        send_kv[i].wait_recv()
        lane = pl.ds(pl.multiple_of((1 + i) * width + core * half_w, 128), half_w)
        store_rows(
            10 + i,
            dot_nn(nbt[:, 0:tok_block], dqkv[:, lane]) + dot_nn(nbt[:, tok_block:], dqp[1 + i]),
        )
        stage_one(10 + i).start()

    advance_one(9)
    reduced(8)
    grad_tok = grad_normed[0:local_len, :]
    grad_pro = grad_normed[local_len : local_len + prompt_count, :]
    scaled1, inverse1 = norm_stats(tokens_ref[...].astype(F32))
    grad_input_ref[...] = (mid[...] + norm_back(grad_tok, scaled1, inverse1, gain1)).astype(BF16)
    p_scaled, p_inverse = norm_stats(prompts_ref[...])
    sm[0:prompt_count, :] = norm_back(grad_pro, p_scaled, p_inverse, gain1)
    sm[prompt_count : prompt_count + 1, :] = column_sum(grad_tok * scaled1) + column_sum(
        grad_pro * p_scaled
    )
    sm[prompt_count + 1 : prompt_count + 2, :] = column_sum(grad_tok) + column_sum(grad_pro)
    sm[prompt_count + 2 : prompt_count + 3, :] = column_sum(dqkv[:, :width].astype(F32))
    sm[prompt_count + 3 : prompt_count + 4, :] = column_sum(dqkv[:, 2 * width :].astype(F32))
    send_sm = pair_copy(X_SMALL, sm.at[:, other_half], smp)
    send_sm.start()
    reduced(9)

    quarter = SMALL_ROWS // 4
    send_sm.wait_recv()
    small = sm[:, my_half] + smp[...]
    for a in range(2):
        for c in range(2):
            s0[a, c] = small[(2 * a + c) * quarter : (2 * a + c + 1) * quarter, :]

    small_one = remote(s0.at[1 - h1], rs1, one_s.at[12], one_r.at[12], nb1)
    small_one.start()
    advance_one(10)
    advance_one(11)
    small_one.wait_recv()
    s1b[...] = s0[h1] + rs1[...]
    small_two = remote(s1b.at[1 - h2], rs2, two_s.at[12], two_r.at[12], nb2)
    small_two.start()
    finish_three(0)
    reduced(10)
    reduced(11)
    small_two.wait_recv()
    rs3[s] = s1b[h2] + rs2[...]

    def small_three(d):
        return remote(
            rs3.at[s], rs3.at[s], three_s.at[12, d - 1], three_r.at[12, s], (b, along(d))
        )

    def small_three_recv(j):
        return remote(rs3.at[j], rs3.at[j], three_s.at[12, 0], three_r.at[12, j], (b, j))

    for d in range(1, groups):
        small_three(d).start()
    finish_three(1)
    start_gather_two(0)
    finish_three(2)
    start_gather_two(1)
    start_gather_pair(0)
    finish_three(3)
    start_gather_pair(1)
    for d in range(1, groups):
        small_three_recv(along(d)).wait_recv()
    total = rs3[0]
    for j in range(1, groups):
        total = total + rs3[j]
    s3[...] = total
    small_keep = pltpu.make_async_copy(s3, small_ref.at[core, h1, h2], loc_sem.at[SMALL])
    small_keep.start()
    small_gather = remote(
        s3, small_ref.at[core, h1, h2], ag1_s.at[SMALL], ag1_r.at[SMALL], nb2
    )
    small_gather.start()
    start_gather_two(2)
    start_gather_two(3)
    small_keep.wait()
    small_gather.wait_recv()
    small_gather_two = remote(
        small_ref.at[core, h1], small_ref.at[core, h1], ag2_s.at[SMALL], ag2_r.at[SMALL], nb1
    )
    small_gather_two.start()
    start_gather_pair(2)
    start_gather_pair(3)
    small_gather_two.wait_recv()
    small_pair = pair_copy(X_FINAL + SMALL, small_ref.at[core], small_ref.at[core])
    small_pair.start()

    small_pair.wait()
    for g in range(len(SLOTS)):
        gather_pair(g).wait()
        gather_one(g).wait_send()
        gather_two(g).wait_send()
    for u in range(12):
        drain_three(u)
    small_one.wait_send()
    small_two.wait_send()
    small_gather.wait_send()
    small_gather_two.wait_send()
    for d in range(1, groups):
        small_three(d).wait_send()

        @pl.when(needs(along(d), s))
        def _(d=d):
            token_send(d).wait_send()
            stat_send(d).wait_send()
            ga_send(d).wait_send()

    def drain(u, carry):
        stage_one(u).wait_send()
        stage_two(u).wait_send()
        return carry

    lax.fori_loop(0, 12, drain, 0)

    def drain_mlp(j, carry):
        send_act(j).wait_send()
        send_gp(j).wait_send()
        return carry

    lax.fori_loop(0, chunks, drain_mlp, 0)
    for copy in (send_cot, send_norm, send_att, send_n2, send_gb, send_q, *send_kv, send_sm):
        copy.wait_send()


def finish_kernel(
    width,
    prompt_count,
    ff,
    layer_in,
    grad_in,
    final_hbm,
    small_hbm,
    layer_out_ref,
    grad_input_ref,
    gp_ref,
    g1_ref,
    s1_ref,
    wqkv_ref,
    qb_ref,
    vb_ref,
    wout_ref,
    ob_ref,
    g2_ref,
    s2_ref,
    wfc1_ref,
    b1_ref,
    wfc2_ref,
    b2_ref,
    final,
    small_in,
    small,
    layer_buf,
    grad_buf,
    fc2_buf,
    fc1_buf,
    out_buf,
    qkv_buf,
    in_sem,
    out_sem,
):
    half_w = width // 2
    blk = final_hbm.shape[4]
    loads = [
        pltpu.make_async_copy(
            final_hbm.at[:, :, :, pl.ds(4 * g, 4)], final.at[g], in_sem.at[g]
        )
        for g in range(3)
    ]
    loads.append(pltpu.make_async_copy(small_hbm, small_in, in_sem.at[3]))
    loads.append(pltpu.make_async_copy(layer_in, layer_buf, in_sem.at[4]))
    loads.append(pltpu.make_async_copy(grad_in, grad_buf, in_sem.at[5]))
    for load in loads:
        load.start()
    stores = []

    def store(src, dst):
        copy = pltpu.make_async_copy(src, dst, out_sem.at[len(stores)])
        copy.start()
        stores.append(copy)

    quads = [(c, a, e) for c in range(2) for a in range(2) for e in range(2)]
    loads[0].wait()
    for c, a, e in quads:
        for i in range(4):
            q, r = i // 2, i % 2
            row = c * half_w + (2 * a + e) * (half_w // 4) + r * blk
            fc2_buf[row : row + blk, q * half_w : (q + 1) * half_w] = final[0, c, a, e, i].astype(
                F32
            )
    store(fc2_buf, wfc2_ref)
    loads[1].wait()
    for c, a, e in quads:
        rows = slice((2 * a + e) * blk, (2 * a + e + 1) * blk)
        for i in range(4):
            col = i * width + c * half_w
            fc1_buf[rows, col : col + half_w] = final[1, c, a, e, i].astype(F32)
    store(fc1_buf, wfc1_ref)
    loads[2].wait()
    for c, a, e in quads:
        rows = slice((2 * a + e) * blk, (2 * a + e + 1) * blk)
        cols = slice(c * half_w, (c + 1) * half_w)
        out_buf[rows, cols] = final[2, c, a, e, 0].astype(F32)
        for i in range(3):
            col = i * width + c * half_w
            qkv_buf[rows, col : col + half_w] = final[2, c, a, e, 1 + i].astype(F32)
    store(out_buf, wout_ref)
    store(qkv_buf, wqkv_ref)
    loads[4].wait()
    store(layer_buf, layer_out_ref)
    loads[5].wait()
    store(grad_buf, grad_input_ref)
    loads[3].wait()
    quarter = small_in.shape[3]
    for c, a, e in quads:
        r = (2 * a + e) * quarter
        small[r : r + quarter, c * half_w : (c + 1) * half_w] = small_in[c, a, e]
    gp_ref[...] = small[0:prompt_count, :]
    for k, ref in enumerate((g1_ref, s1_ref, qb_ref, vb_ref, ob_ref, g2_ref, s2_ref)):
        ref[...] = small[prompt_count + k : prompt_count + k + 1, :].reshape(width)
    for k in range(ff // width):
        r = prompt_count + 7 + k
        b1_ref[k * width : (k + 1) * width] = small[r : r + 1, :].reshape(width)
    r = prompt_count + 7 + ff // width
    b2_ref[...] = small[r : r + 1, :].reshape(width)
    for copy in stores:
        copy.wait()


def local(
    tokens,
    segments,
    prompts,
    ln1_gain,
    ln1_shift,
    w_qkv,
    q_bias,
    v_bias,
    w_out,
    out_bias,
    ln2_gain,
    ln2_shift,
    w_fc1,
    fc1_bias,
    w_fc2,
    fc2_bias,
    cotangent,
):
    groups = lax.axis_size("seq")
    batch = lax.axis_size("batch")
    row_count, local_len, width = tokens.shape
    ff = w_fc1.shape[1]
    prompt_count = prompts.shape[0]
    assert row_count == 1 and groups == 4 and batch % GROUP == 0 and ff == 4 * width
    table = need_table(groups, local_len)
    dims = (groups, local_len, width, ff, prompt_count, table)
    row_len = groups * local_len
    half_w = width // 2
    blk = width // groups // 4
    tok_block = local_len + PROMPT_PAD
    quarter = SMALL_ROWS // 4

    vmem = pl.BlockSpec(memory_space=pltpu.VMEM)
    hbm = pl.BlockSpec(memory_space=pl.ANY)
    dma = pltpu.SemaphoreType.DMA
    V = pltpu.VMEM
    scratch = [
        V((width, 3 * width), BF16),
        V((width, width), BF16),
        V((width, ff), BF16),
        V((ff, width), BF16),
        V((groups, local_len, width), BF16),
        V((2 * tok_block, width), BF16),
        V((width, 2 * tok_block), BF16),
        V((row_len, width), BF16),
        V((row_len + PROMPT_PAD, width), BF16),
        V((row_len + PROMPT_PAD, width), BF16),
        V((local_len, row_len + PROMPT_PAD), F32),
        V((local_len, width), F32),
        V((2 * local_len, width), BF16),
        V((local_len, 128), F32),
        V((local_len, 128), F32),
        V((local_len, width), F32),
        V((local_len, width), F32),
        V((local_len, 1), F32),
        V((2 * local_len, width), BF16),
        V((width, 2 * local_len), BF16),
        V((4, local_len, width), BF16),
        V((4, local_len, width), BF16),
        V((4, local_len, half_w), BF16),
        V((4, local_len, half_w), BF16),
        V((4, width), F32),
        V((local_len, width), F32),
        V((local_len, width), F32),
        V((local_len, width), BF16),
        V((local_len, width), BF16),
        V((local_len, half_w), BF16),
        V((groups, local_len, width), BF16),
        V((groups, 32, local_len), F32),
        V((local_len, width), F32),
        V((local_len, width), F32),
        V((tok_block, 3 * width), BF16),
        V((3, tok_block, half_w), BF16),
        V((12, 2, 2, 4, blk, half_w), BF16),
        V((12, 2, 4, blk, half_w), BF16),
        V((12, 4, blk, half_w), BF16),
        V((groups, 12, blk, half_w), BF16),
        V((12, blk, half_w), BF16),
        V((SMALL_ROWS, width), F32),
        V((SMALL_ROWS, half_w), F32),
        V((2, 2, quarter, half_w), F32),
        V((2, quarter, half_w), F32),
        V((2, quarter, half_w), F32),
        V((quarter, half_w), F32),
        V((groups, quarter, half_w), F32),
        V((quarter, half_w), F32),
        dma((4,)),
        dma((3,)),
        dma((groups,)),
        dma((X_COUNT,)),
        dma((X_COUNT,)),
        dma((3,)),
        dma((groups,)),
        dma((3,)),
        dma((groups,)),
        dma((13,)),
        dma((13,)),
        dma((13,)),
        dma((13,)),
        dma((13, 3)),
        dma((13, groups)),
        dma((5,)),
        dma((5,)),
        dma((5,)),
        dma((5,)),
        dma((5,)),
    ]
    specs = [vmem] * 17
    for index in (5, 8, 12, 14):
        specs[index] = hbm
    layer_out, grad_input, final, small = pl.pallas_call(
        functools.partial(layer_kernel, dims),
        out_shape=(
            jax.ShapeDtypeStruct((local_len, width), BF16),
            jax.ShapeDtypeStruct((local_len, width), BF16),
            jax.ShapeDtypeStruct((2, 2, 2, 12, blk, half_w), BF16),
            jax.ShapeDtypeStruct((2, 2, 2, quarter, half_w), F32),
        ),
        in_specs=specs,
        out_specs=(vmem, vmem, hbm, hbm),
        scratch_shapes=scratch,
        compiler_params=pltpu.CompilerParams(
            collective_id=0, has_side_effects=True, vmem_limit_bytes=67043328
        ),
        name="layer",
    )(
        tokens.reshape(local_len, width),
        segments,
        prompts,
        ln1_gain,
        ln1_shift,
        w_qkv,
        q_bias,
        v_bias,
        w_out,
        out_bias,
        ln2_gain,
        ln2_shift,
        w_fc1,
        fc1_bias,
        w_fc2,
        fc2_bias,
        cotangent.reshape(local_len, width),
    )
    if batch > GROUP:
        rings = [list(range(k, batch, GROUP)) for k in range(GROUP)]
        final, small = lax.psum((final, small), "batch", axis_index_groups=rings)
    rows_z = width // groups

    def flat(n):
        return jax.ShapeDtypeStruct((n,), F32)

    outs = pl.pallas_call(
        functools.partial(finish_kernel, width, prompt_count, ff),
        out_shape=(
            jax.ShapeDtypeStruct((local_len, width), BF16),
            jax.ShapeDtypeStruct((local_len, width), BF16),
            jax.ShapeDtypeStruct((prompt_count, width), F32),
            flat(width),
            flat(width),
            jax.ShapeDtypeStruct((rows_z, 3 * width), F32),
            flat(width),
            flat(width),
            jax.ShapeDtypeStruct((rows_z, width), F32),
            flat(width),
            flat(width),
            flat(width),
            jax.ShapeDtypeStruct((rows_z, ff), F32),
            flat(ff),
            jax.ShapeDtypeStruct((ff // groups, width), F32),
            flat(width),
        ),
        in_specs=[pl.BlockSpec(memory_space=pltpu.HBM)] * 4,
        out_specs=tuple(hbm if i in (0, 1, 5, 8, 12, 14) else vmem for i in range(16)),
        scratch_shapes=[
            V((3, 2, 2, 2, 4, blk, half_w), BF16),
            V((2, 2, 2, quarter, half_w), F32),
            V((SMALL_ROWS, width), F32),
            V((local_len, width), BF16),
            V((local_len, width), BF16),
            V((ff // groups, width), F32),
            V((rows_z, ff), F32),
            V((rows_z, width), F32),
            V((rows_z, 3 * width), F32),
            dma((6,)),
            dma((6,)),
        ],
        compiler_params=pltpu.CompilerParams(vmem_limit_bytes=67043328),
        name="finish",
    )(layer_out, grad_input, final, small)
    return tuple(o.reshape((1, local_len, width)) if i < 2 else o for i, o in enumerate(outs))


def solution(mesh):
    tok = P("batch", "seq", None)
    in_specs = (tok, P("batch", "seq")) + (P(),) * 14 + (tok,)
    out_specs = (
        tok,
        tok,
        P(),
        P(),
        P(),
        P("seq", None),
        P(),
        P(),
        P("seq", None),
        P(),
        P(),
        P(),
        P("seq", None),
        P(),
        P("seq", None),
        P(),
    )
    return jax.shard_map(local, mesh=mesh, in_specs=in_specs, out_specs=out_specs, check_vma=False)
```

```python
import functools

import jax
import jax.numpy as jnp
from jax import lax
from jax.experimental import pallas as pl
from jax.experimental.pallas import tpu as pltpu
from jax.sharding import PartitionSpec as P

HEAD_DIM = 64
IMAGE_TOKENS = (101, 197, 577)
EPSILON = 1e-06
MASKED_SCORE = -1e30
ROOT_HALF = 0.7071067811865476
ROOT_TWO_PI = 2.5066282746310002
SCALE = HEAD_DIM ** (-0.5)
GROUP = 8
PROMPT_PAD = 64
SMALL_ROWS = 64
F32 = jnp.float32
BF16 = jnp.bfloat16
MESH = pl.DeviceIdType.MESH


def dot_nn(a, b):
    return lax.dot_general(a, b, (((1,), (0,)), ((), ())), preferred_element_type=F32)


def dot_nt(a, b):
    return lax.dot_general(a, b, (((1,), (1,)), ((), ())), preferred_element_type=F32)


def dot_tn(a, b):
    return lax.dot_general(a, b, (((0,), (0,)), ((), ())), preferred_element_type=F32)


def check_window(groups, local_len):
    row_len, half_len = groups * local_len, local_len // 2
    cut = 2 * local_len
    for size in IMAGE_TOKENS:
        for first in range(0, row_len, size):
            last = min(first + size, row_len) - 1
            for shard in range(first // local_len, last // local_len + 1):
                start = 0 if shard < 2 else 3 * half_len
                inside = start <= first and last < start + 5 * half_len
                if shard == 3:
                    inside = inside and first >= cut
                given = size == IMAGE_TOKENS[-1] and shard == 2 and first == 0
                assert inside or given
                assert not given or last < cut + extra_rows(local_len)


def extra_rows(local_len):
    return -(-(IMAGE_TOKENS[-1] - 2 * local_len) // 16) * 16


def norm_stats(values):
    centred = values - jnp.mean(values, axis=-1, keepdims=True)
    inverse = lax.rsqrt(jnp.mean(centred * centred, axis=-1, keepdims=True) + EPSILON)
    return centred * inverse, inverse


def norm_back(grad_out, scaled, inverse, gain):
    inner = grad_out * gain
    return inverse * (
        inner
        - jnp.mean(inner, axis=-1, keepdims=True)
        - scaled * jnp.mean(inner * scaled, axis=-1, keepdims=True)
    )


def line(ref):
    return ref[...].reshape(1, -1)


def column_sum(values):
    return jnp.sum(values, axis=0, keepdims=True)


X_COT, X_N2, X_ATT, X_NORM, X_GB, X_Q, X_KV, X_SMALL, X_FINAL, X_ACT, X_GP, X_EXTRA = 0, 1, 2, 3, 4, 5, 6, 8, 9, 14, 18, 22
X_COUNT = 23
HALVES = ((2, 0, 0), (2, 1, 0), (1, 2, 1))
SLOTS = ((0, 4), (4, 4), (8, 2), (10, 2))
SMALL = 4


def layer_kernel(
    dims,
    tokens_ref,
    seg_ref,
    prompts_ref,
    g1_ref,
    s1_ref,
    wqkv_hbm,
    qb_ref,
    vb_ref,
    wout_hbm,
    ob_ref,
    g2_ref,
    s2_ref,
    wfc1_hbm,
    b1_ref,
    wfc2_hbm,
    b2_ref,
    cot_ref,
    layer_out_ref,
    grad_input_ref,
    final_ref,
    small_ref,
    wqkv,
    wout,
    wfc1,
    wfc2,
    tokw,
    nb,
    nbt,
    q_win,
    k_win,
    v_win,
    bias,
    o32,
    att,
    lse,
    centre,
    mid,
    xh2,
    r2,
    n2,
    n2t,
    act,
    gp,
    actp,
    gpp,
    b1s,
    acc_out,
    acc_dn,
    cotp,
    gb,
    gbp,
    ga_win,
    stat,
    dk,
    dv,
    dqkv,
    dqp,
    units,
    r1,
    r2u,
    r3,
    a3,
    sm,
    smp,
    s0,
    rs1,
    s1b,
    rs2,
    rs3,
    s3,
    bias_x,
    o32_x,
    att_x,
    lse_x,
    att_in,
    lse_in,
    xh_x,
    e_x,
    e_in,
    e_low,
    wsem,
    tok_s,
    tok_r,
    pair_s,
    pair_r,
    ga_s,
    ga_r,
    st_s,
    st_r,
    one_s,
    one_r,
    two_s,
    two_r,
    three_s,
    three_r,
    loc_sem,
    ag1_s,
    ag1_r,
    ag2_s,
    ag2_r,
    ax_s,
    ax_r,
    ex_s,
    ex_r,
):
    groups, local_len, width, ff, prompt_count = dims
    half_len = local_len // 2
    window = 5 * half_len
    cut = 2 * local_len
    extra = extra_rows(local_len)
    head_pairs = width // (2 * HEAD_DIM)
    chunks = ff // width
    half_w = width // 2
    key_len = window + PROMPT_PAD
    zrows = width // groups

    b = lax.axis_index("batch")
    s = lax.axis_index("seq")
    base = (b // GROUP) * GROUP
    core = lax.rem(b, 2)
    xb = lax.rem(b // 2, 2)
    yb = lax.rem(b // 4, 2)
    h1 = xb * (1 - core) + yb * core
    h2 = yb * (1 - core) + xb * core

    def place(x, y, c):
        return base + y * 4 + x * 2 + c

    nb1 = (place(xb + (1 - core) * (1 - 2 * xb), yb + core * (1 - 2 * yb), core), s)
    nb2 = (place(xb + core * (1 - 2 * xb), yb + (1 - core) * (1 - 2 * yb), core), s)
    pair = (place(xb, yb, 1 - core), s)

    def along(d):
        return lax.rem(s + d, groups)

    first_half = jnp.where(s < 2, 0, 3)
    start = first_half * half_len
    partner = s + 1 - 2 * lax.rem(s, 2)
    own_at = 2 * s - first_half
    partner_at = 2 * partner - first_half
    half_at = jnp.where(s < 2, 4, 0)

    def halves(at, count):
        return pl.ds(pl.multiple_of(at * half_len, half_len), count * half_len)

    own_rows = halves(own_at, 2)
    partner_rows = halves(partner_at, 2)
    half_rows = halves(half_at, 1)
    shared_rows = pl.ds(4 * half_len, extra)

    def remote(src, dst, send, recv, to):
        return pltpu.make_async_remote_copy(
            src_ref=src, dst_ref=dst, send_sem=send, recv_sem=recv, device_id=to, device_id_type=MESH
        )

    barrier = pltpu.get_barrier_semaphore()
    for peer in (pair, nb1, nb2):
        pl.semaphore_signal(barrier, inc=1, device_id=peer, device_id_type=MESH)
    for d in range(1, groups):
        pl.semaphore_signal(barrier, inc=1, device_id=(b, along(d)), device_id_type=MESH)

    loads = [
        pltpu.make_async_copy(wqkv_hbm, wqkv, wsem.at[0]),
        pltpu.make_async_copy(wout_hbm, wout, wsem.at[1]),
        pltpu.make_async_copy(wfc1_hbm, wfc1, wsem.at[2]),
        pltpu.make_async_copy(wfc2_hbm, wfc2, wsem.at[3]),
    ]
    loads[0].start()
    pl.semaphore_wait(barrier, 2 + groups)

    def token_partner(at):
        return remote(tokens_ref, tokw.at[at], tok_s.at[0], tok_r.at[0], (b, partner))

    def token_half(i, side, at, to):
        part = tokens_ref.at[pl.ds(side * half_len, half_len)]
        return remote(part, tokw.at[halves(at, 1)], tok_s.at[1 + i], tok_r.at[1], (b, to))

    def for_halves(action):
        for i, (src, dst, side) in enumerate(HALVES):

            @pl.when(s == src)
            def _(i=i, dst=dst, side=side):
                action(i, side, 4 if dst < 2 else 0, dst)

    for_halves(lambda *a: token_half(*a).start())
    token_partner(own_rows).start()

    for load in loads[1:]:
        load.start()

    def pair_copy(index, src, dst):
        return remote(src, dst, pair_s.at[index], pair_r.at[index], pair)

    my_half = pl.ds(pl.multiple_of(core * half_w, 128), half_w)
    other_half = pl.ds(pl.multiple_of((1 - core) * half_w, 128), half_w)

    send_cot = pair_copy(X_COT, cot_ref, cotp)
    send_cot.start()

    gain1 = line(g1_ref)
    shift1 = line(s1_ref)
    for i in range(chunks):
        b1s[i : i + 1, :] = b1_ref[i * width : (i + 1) * width].reshape(1, width)

    last = s * local_len + local_len - 1
    seg_last = seg_ref[:, local_len - 1 : local_len].astype(F32)
    inv_n = jnp.full((1, 1), 1.0 / IMAGE_TOKENS[-1], F32)
    is_long = jnp.ones((1, 1), F32)
    for size in IMAGE_TOKENS[:-1]:
        here = seg_last == (last // size).astype(F32)
        inv_n = jnp.where(here, 1.0 / size, inv_n)
        is_long = jnp.where(here, 0.0, is_long)
    k_pos = lax.broadcasted_iota(jnp.int32, (1, key_len), 1)
    k_open = jnp.where(k_pos < window, 0.0, jnp.where(k_pos < window + prompt_count, 1.0, 0.0))
    k_id = jnp.floor(((k_pos + start).astype(F32) + 0.5) * inv_n)
    k_id = jnp.where(k_pos < window, k_id, -1.0)

    def mask_of(q_pos):
        q_id = jnp.floor((q_pos.astype(F32) + 0.5) * inv_n)
        return jnp.where(q_id == k_id, 0.0, MASKED_SCORE * (1.0 - k_open))

    bias[...] = mask_of(lax.broadcasted_iota(jnp.int32, (local_len, 1), 0) + s * local_len)
    x_row = lax.broadcasted_iota(jnp.int32, (extra, 1), 0)
    bias_x[...] = mask_of(x_row + cut)
    shared = jnp.where(x_row + cut < IMAGE_TOKENS[-1], is_long, 0.0) > 0.5

    def project(normed, rows):
        q = dot_nn(normed, wqkv[:, :width]) + line(qb_ref)
        q_win[rows, :] = (q.astype(BF16).astype(F32) * SCALE).astype(BF16)
        k_win[rows, :] = dot_nn(normed, wqkv[:, width : 2 * width]).astype(BF16)
        v_win[rows, :] = (dot_nn(normed, wqkv[:, 2 * width :]) + line(vb_ref)).astype(BF16)

    p_scaled, p_inverse = norm_stats(prompts_ref[...])
    p_block = local_len + PROMPT_PAD
    tok_block = p_block + extra
    nb[0, local_len:p_block, :] = jnp.zeros((PROMPT_PAD, width), BF16)
    nb[0, local_len : local_len + prompt_count, :] = (p_scaled * gain1 + shift1).astype(BF16)
    scaled1, _ = norm_stats(tokens_ref[...].astype(F32))
    nb[0, 0:local_len, :] = (scaled1 * gain1 + shift1).astype(BF16)
    send_norm = pair_copy(X_NORM, nb.at[0, pl.ds(0, p_block)], nb.at[1, pl.ds(0, p_block)])
    send_norm.start()

    loads[0].wait()
    project(nb[0, 0:local_len, :], own_rows)
    p_low = nb[0, local_len:p_block, :]
    k_win[window:key_len, :] = dot_nn(p_low, wqkv[:, width : 2 * width]).astype(BF16)
    v_win[window:key_len, :] = (dot_nn(p_low, wqkv[:, 2 * width :]) + line(vb_ref)).astype(BF16)

    def project_tokens(rows):
        scaled, _ = norm_stats(tokw[rows, :].astype(F32))
        project((scaled * gain1 + shift1).astype(BF16), rows)

    token_partner(partner_rows).wait_recv()
    project_tokens(partner_rows)

    @pl.when(s < groups - 1)
    def _():
        token_half(0, 0, half_at, partner).wait_recv()
        project_tokens(half_rows)

    @pl.when(s == groups - 1)
    def _():
        empty = jnp.zeros((half_len, width), BF16)
        q_win[0:half_len, :] = empty
        k_win[0:half_len, :] = empty
        v_win[0:half_len, :] = empty
        ga_win[0:half_len, :] = empty
        stat[0] = jnp.zeros((32, half_len), F32)

    @pl.when(s < 2)
    def _():
        scaled, _ = norm_stats(tokw[shared_rows, :].astype(F32))
        xh_x[...] = scaled
        nb[0, p_block:tok_block, :] = (scaled * gain1 + shift1).astype(BF16)

    @pl.when(s >= 2)
    def _():
        xh_x[...] = jnp.zeros((extra, width), F32)
        nb[0, p_block:tok_block, :] = jnp.zeros((extra, width), BF16)

    send_extra = pair_copy(
        X_EXTRA, nb.at[0, pl.ds(p_block, extra)], nb.at[1, pl.ds(p_block, extra)]
    )
    send_extra.start()

    pair_lane = lax.broadcasted_iota(jnp.int32, (1, 2 * HEAD_DIM), 1)
    first_head = jnp.where(pair_lane < HEAD_DIM, 1.0, 0.0)
    head_mask = (first_head.astype(BF16), (1.0 - first_head).astype(BF16))
    first_head_f32 = pair_lane < HEAD_DIM
    stat_lane = lax.broadcasted_iota(jnp.int32, (local_len, 128), 1)

    def lanes_of(hp):
        return pl.ds(pl.multiple_of(hp * 2 * HEAD_DIM, 128), 2 * HEAD_DIM)

    lse[...] = jnp.zeros((local_len, 128), F32)
    centre[...] = jnp.zeros((local_len, 128), F32)

    def softmax_heads(q, lanes, mask):
        k = k_win[:, lanes]
        v = v_win[:, lanes]
        outs, logs = [], []
        for h in range(2):
            scores = dot_nt(q * head_mask[h], k) + mask[...]
            highest = jnp.max(scores, axis=-1, keepdims=True)
            weights = jnp.exp(scores - highest)
            total = jnp.sum(weights, axis=-1, keepdims=True)
            outs.append(dot_nn(weights.astype(BF16), v) / total)
            logs.append(highest + jnp.log(total))
        return jnp.where(first_head_f32, outs[0], outs[1]), logs

    x_pairs = head_pairs // 2
    x_lane = lax.broadcasted_iota(jnp.int32, (extra, 128), 1)

    def x_lanes(j):
        return pl.ds(pl.multiple_of(j * half_w, 128), half_w)

    def att_back(j):
        return remote(
            att_x.at[:, x_lanes(j)], att_in.at[:, x_lanes(j)], ax_s.at[0], ax_r.at[0, j], (b, 2)
        )

    def lse_back(j):
        return remote(lse_x, lse_in.at[j], ax_s.at[1], ax_r.at[1, j], (b, 2))

    @pl.when(s < 2)
    def _():
        lse_x[...] = jnp.zeros((extra, 128), F32)

        def attend_shared(i, carry):
            hp = s * x_pairs + i
            lanes = lanes_of(hp)
            combined, logs = softmax_heads(q_win[shared_rows, lanes], lanes, bias_x)
            o32_x[:, lanes] = combined
            att_x[:, lanes] = combined.astype(BF16)
            for h in range(2):
                lse_x[...] = jnp.where(x_lane == 2 * hp + h, logs[h], lse_x[...])
            return carry

        lax.fori_loop(0, x_pairs, attend_shared, 0)
        att_back(s).start()
        lse_back(s).start()

    def attend(hp, carry):
        lanes = lanes_of(hp)
        combined, logs = softmax_heads(q_win[own_rows, lanes], lanes, bias)
        o32[:, lanes] = combined
        att[0:local_len, lanes] = combined.astype(BF16)
        for h in range(2):
            lse[...] = jnp.where(stat_lane == 2 * hp + h, logs[h], lse[...])
        return carry

    lax.fori_loop(0, head_pairs, attend, 0)

    @pl.when(s == 2)
    def _():
        for j in range(2):
            remote(
                att_x.at[:, x_lanes(j)], att_in.at[:, x_lanes(j)], ax_s.at[0], ax_r.at[0, j], (b, j)
            ).wait_recv()
            remote(lse_x, lse_in.at[j], ax_s.at[1], ax_r.at[1, j], (b, j)).wait_recv()
        merged = jnp.where(shared, att_in[...].astype(F32), o32[0:extra, :])
        o32[0:extra, :] = merged
        att[0:extra, :] = merged.astype(BF16)
        lse[0:extra, :] = jnp.where(shared, lse_in[0] + lse_in[1], lse[0:extra, :])

    own = pl.ds(0, local_len)
    theirs = pl.ds(local_len, local_len)
    send_att = pair_copy(X_ATT, att.at[own], att.at[theirs])
    send_att.start()

    loads[1].wait()
    mid[...] = (
        tokens_ref[...].astype(F32) + dot_nn(att[0:local_len, :], wout[...]) + line(ob_ref)
    )
    scaled2, inverse2 = norm_stats(mid[...])
    xh2[...] = scaled2
    r2[...] = inverse2
    n2[0:local_len, :] = (scaled2 * line(g2_ref) + line(s2_ref)).astype(BF16)
    send_n2 = pair_copy(X_N2, n2.at[own], n2.at[theirs])
    send_n2.start()
    acc_out[...] = jnp.zeros((local_len, width), F32)
    acc_dn[...] = jnp.zeros((local_len, width), F32)
    n2t[:, 0:local_len] = n2[0:local_len, :].T
    loads[2].wait()
    loads[3].wait()
    send_n2.wait_recv()
    n2t[:, local_len:] = n2[local_len:, :].T
    send_cot.wait_recv()

    blk = zrows // 4

    def unit_of(p):
        return p // 2 + 4 * lax.rem(p, 2)

    def store_rows(u, grads):
        for z in range(groups):
            for a in range(2):
                for c in range(2):
                    r = z * zrows + (2 * a + c) * blk
                    units[u, a, c, z] = grads[r : r + blk, :].astype(BF16)

    def stage_one(u):
        return remote(units.at[u, 1 - h1], r1.at[u], one_s.at[u], one_r.at[u], nb1)

    def stage_two(u):
        return remote(units.at[u, h1, 1 - h2], r2u.at[u], two_s.at[u], two_r.at[u], nb2)

    def advance_one(u):
        stage_one(u).wait_recv()
        units[u, h1] = (units[u, h1].astype(F32) + r1[u].astype(F32)).astype(BF16)
        stage_two(u).start()

    def advance_two(u):
        stage_two(u).wait_recv()
        r2u[u] = (units[u, h1, h2].astype(F32) + r2u[u].astype(F32)).astype(BF16)

    def stage_three_fc2(u):
        return remote(
            r2u.at[u], r3.at[s, pl.ds(0, 4)], three_s.at[u, 0], three_r.at[0, s], (b, u)
        )

    def stage_three(u, d):
        t = along(d)
        return remote(r2u.at[u, t], r3.at[s, u], three_s.at[u, d - 1], three_r.at[u, s], (b, t))

    def start_three(u):
        if u < 4:

            @pl.when(s != u)
            def _():
                stage_three_fc2(u).start()

        else:
            for d in range(1, groups):
                stage_three(u, d).start()

    def drain_three(u):
        if u < 4:

            @pl.when(s != u)
            def _():
                stage_three_fc2(u).wait_send()

        else:
            for d in range(1, groups):
                stage_three(u, d).wait_send()

    def slots(g):
        return pl.ds(*SLOTS[g])

    def keep_final(g):
        return pltpu.make_async_copy(
            a3.at[slots(g)], final_ref.at[core, h1, h2, slots(g)], loc_sem.at[g]
        )

    def gather_one(g):
        return remote(
            a3.at[slots(g)],
            final_ref.at[core, h1, h2, slots(g)],
            ag1_s.at[g],
            ag1_r.at[g],
            nb2,
        )

    def gather_two(g):
        ref = final_ref.at[core, h1, :, slots(g)]
        return remote(ref, ref, ag2_s.at[g], ag2_r.at[g], nb1)

    def gather_pair(g):
        ref = final_ref.at[core, :, :, slots(g)]
        return pair_copy(X_FINAL + g, ref, ref)

    def finish_three(g):
        first, count = SLOTS[g]
        if g == 0:
            total = r2u[s].astype(F32)
            for d in range(1, groups):
                j = along(d)
                remote(
                    r2u.at[0], r3.at[j, pl.ds(0, 4)], three_s.at[0, 0], three_r.at[0, j], (b, j)
                ).wait_recv()
                total = total + r3[j, 0:4].astype(F32)
            a3[0:4] = total.astype(BF16)
        else:
            for u in range(first, first + count):
                total = r2u[u, s].astype(F32)
                for d in range(1, groups):
                    j = along(d)
                    remote(
                        r2u.at[u, 0], r3.at[j, u], three_s.at[u, 0], three_r.at[u, j], (b, j)
                    ).wait_recv()
                    total = total + r3[j, u].astype(F32)
                a3[u] = total.astype(BF16)
        keep_final(g).start()
        gather_one(g).start()

    def start_gather_two(g):
        keep_final(g).wait()
        gather_one(g).wait_recv()
        gather_two(g).start()

    def start_gather_pair(g):
        gather_two(g).wait_recv()
        gather_pair(g).start()

    def reduced(u):
        advance_two(u)
        start_three(u)

    sm[...] = jnp.zeros((SMALL_ROWS, width), F32)

    def send_act(j):
        return pair_copy(X_ACT + j, act.at[j, :, other_half], actp.at[j])

    def send_gp(j):
        return pair_copy(X_GP + j, gp.at[j, :, other_half], gpp.at[j])

    def mlp(i, carry):
        @pl.when(i < chunks)
        def _():
            cols = pl.ds(pl.multiple_of(i * width, 128), width)
            w1 = wfc1[:, cols]
            w2 = wfc2[cols, :]
            pre = dot_nn(n2[0:local_len, :], w1) + b1s[pl.ds(i, 1), :]
            phi = 0.5 * (1.0 + lax.erf(pre * ROOT_HALF))
            activated = (pre * phi).astype(BF16)
            act[i] = activated
            send_act(i).start()
            slope = phi + pre * jnp.exp(-0.5 * pre * pre) / ROOT_TWO_PI
            grad_pre = (dot_nt(cot_ref[...], w2) * slope).astype(BF16)
            gp[i] = grad_pre
            send_gp(i).start()
            sm[pl.ds(prompt_count + 7 + i, 1), :] = column_sum(grad_pre.astype(F32))
            acc_out[...] += dot_nn(activated, w2)
            acc_dn[...] += dot_nt(grad_pre, w1)

        @pl.when(i > 0)
        def _():
            j = i - 1
            send_act(j).wait_recv()
            grads2 = dot_tn(act[j, :, my_half], cot_ref[...]) + dot_tn(actp[j], cotp[...])
            rows = half_w // 4
            for a in range(2):
                for c in range(2):
                    for q in range(2):
                        for e in range(2):
                            r = (2 * a + c) * rows + e * blk
                            units[j, a, c, 2 * q + e] = grads2[
                                r : r + blk, q * half_w : (q + 1) * half_w
                            ].astype(BF16)
            stage_one(j).start()
            send_gp(j).wait_recv()
            store_rows(
                4 + j,
                dot_nn(n2t[:, 0:local_len], gp[j, :, my_half])
                + dot_nn(n2t[:, local_len:], gpp[j]),
            )
            stage_one(4 + j).start()

        return carry

    lax.fori_loop(0, chunks + 1, mlp, 0)

    grad_out = cot_ref[...].astype(F32)
    layer_out_ref[...] = (mid[...] + acc_out[...] + line(b2_ref)).astype(BF16)
    grad_n2 = acc_dn[...]
    sm[prompt_count + 11 : prompt_count + 12, :] = column_sum(grad_out)
    sm[prompt_count + 5 : prompt_count + 6, :] = column_sum(grad_n2 * xh2[...])
    sm[prompt_count + 6 : prompt_count + 7, :] = column_sum(grad_n2)
    grad_mid = grad_out + norm_back(grad_n2, xh2[...], r2[...], line(g2_ref))
    mid[...] = grad_mid
    branch = grad_mid.astype(BF16)
    gb[...] = branch
    send_gb = pair_copy(X_GB, gb.at[:, other_half], gbp)
    send_gb.start()
    sm[prompt_count + 4 : prompt_count + 5, :] = column_sum(branch.astype(F32))
    grad_att = dot_nt(branch, wout[...]).astype(BF16)
    ga_win[own_rows, :] = grad_att
    product = grad_att.astype(F32) * o32[...]
    for hp in range(head_pairs):
        block = product[:, hp * 128 : (hp + 1) * 128]
        for h in range(2):
            keep = first_head_f32 if h == 0 else jnp.logical_not(first_head_f32)
            total = jnp.sum(jnp.where(keep, block, 0.0), axis=-1, keepdims=True)
            centre[...] = jnp.where(stat_lane == 2 * hp + h, total, centre[...])
    for i in range(2):
        part = slice(i * half_len, (i + 1) * half_len)
        stat[own_at + i, 0:16, :] = lse[part, :].T[0:16, :]
        stat[own_at + i, 16:32, :] = centre[part, :].T[0:16, :]

    def ga_partner(at):
        part = ga_win.at[halves(at, 2)]
        return remote(part, part, ga_s.at[0], ga_r.at[0], (b, partner))

    def stat_partner(at):
        part = stat.at[pl.ds(at, 2)]
        return remote(part, part, st_s.at[0], st_r.at[0], (b, partner))

    def ga_half(i, side, at, to):
        return remote(
            ga_win.at[halves(own_at + side, 1)],
            ga_win.at[halves(at, 1)],
            ga_s.at[1 + i],
            ga_r.at[1],
            (b, to),
        )

    def stat_half(i, side, at, to):
        return remote(stat.at[own_at + side], stat.at[at], st_s.at[1 + i], st_r.at[1], (b, to))

    def stat_line(row, at, count):
        return jnp.concatenate([stat[at + i, pl.ds(row, 1), :] for i in range(count)], axis=1)

    for_halves(lambda *a: stat_half(*a).start())
    for_halves(lambda *a: ga_half(*a).start())
    stat_partner(own_at).start()
    ga_partner(own_at).start()

    send_att.wait_recv()
    send_gb.wait_recv()
    store_rows(
        8, dot_tn(att[0:local_len, :], gb[:, my_half]) + dot_tn(att[local_len:, :], gbp[...])
    )
    stage_one(8).start()

    prompt_row = lax.broadcasted_iota(jnp.int32, (PROMPT_PAD, 1), 0)
    prompt_bias = jnp.where(prompt_row < prompt_count, 0.0, MASKED_SCORE)
    dqkv[local_len:tok_block, :] = jnp.zeros((PROMPT_PAD + extra, 3 * width), BF16)

    def own_queries(hp, carry):
        lanes = lanes_of(hp)
        q = q_win[own_rows, lanes]
        k = k_win[:, lanes]
        v = v_win[:, lanes]
        g = ga_win[own_rows, lanes]
        parts = []
        d_pk = jnp.zeros((PROMPT_PAD, 2 * HEAD_DIM), F32)
        d_pv = jnp.zeros((PROMPT_PAD, 2 * HEAD_DIM), F32)
        for h in range(2):
            head = 2 * hp + h
            qm = q * head_mask[h]
            gm = g * head_mask[h]
            here = stat_lane == head
            lse_col = jnp.sum(jnp.where(here, lse[...], 0.0), axis=-1, keepdims=True)
            centre_col = jnp.sum(jnp.where(here, centre[...], 0.0), axis=-1, keepdims=True)
            probs = jnp.exp(dot_nt(qm, k) + bias[...] - lse_col)
            grad_scores = (probs * (dot_nt(gm, v) - centre_col)).astype(BF16)
            parts.append(dot_nn(grad_scores, k))
            lse_line = stat_line(head, own_at, 2)
            centre_line = stat_line(16 + head, own_at, 2)
            kp = k_win[window:key_len, lanes]
            vp = v_win[window:key_len, lanes]
            probs_p = jnp.exp(dot_nt(kp, qm) + prompt_bias - lse_line)
            grads_p = (probs_p * (dot_nt(vp, gm) - centre_line)).astype(BF16)
            d_pk = d_pk + dot_nn(grads_p, qm)
            d_pv = d_pv + dot_nn(probs_p.astype(BF16), gm)
        grad_q = jnp.where(first_head_f32, parts[0], parts[1]) * SCALE
        dqkv[0:local_len, lanes] = grad_q.astype(BF16)
        k_lanes = pl.ds(pl.multiple_of(width + hp * 128, 128), 128)
        v_lanes = pl.ds(pl.multiple_of(2 * width + hp * 128, 128), 128)
        dqkv[local_len:p_block, k_lanes] = d_pk.astype(BF16)
        dqkv[local_len:p_block, v_lanes] = d_pv.astype(BF16)

        @pl.when(hp > 1)
        def _():
            advance_one(unit_of(hp - 2))

        return carry

    lax.fori_loop(0, head_pairs, own_queries, 0)
    nbt[0] = nb[0].T
    send_norm.wait_recv()
    send_extra.wait_recv()
    nbt[1] = nb[1].T

    dk[...] = jnp.zeros((local_len, width), F32)
    dv[...] = jnp.zeros((local_len, width), F32)

    def own_keys(at, count):
        cols = halves(at, count)
        mask = bias[:, cols]

        def body(hp, carry):
            lanes = lanes_of(hp)
            k = k_win[own_rows, lanes]
            v = v_win[own_rows, lanes]
            q = q_win[cols, lanes]
            g = ga_win[cols, lanes]
            d_k = dk[:, lanes]
            d_v = dv[:, lanes]
            for h in range(2):
                head = 2 * hp + h
                qm = q * head_mask[h]
                gm = g * head_mask[h]
                lse_line = stat_line(head, at, count)
                centre_line = stat_line(16 + head, at, count)
                probs = jnp.exp(dot_nt(k, qm) + mask - lse_line)
                grad_scores = (probs * (dot_nt(v, gm) - centre_line)).astype(BF16)
                d_k = d_k + dot_nn(grad_scores, qm)
                d_v = d_v + dot_nn(probs.astype(BF16), gm)
            dk[:, lanes] = d_k
            dv[:, lanes] = d_v
            return carry

        lax.fori_loop(0, head_pairs, body, 0)

    def shared_back(i, carry):
        hp = s * x_pairs + i
        lanes = lanes_of(hp)
        q_x = q_win[shared_rows, lanes]
        k_x = k_win[shared_rows, lanes]
        v_x = v_win[shared_rows, lanes]
        g_x = ga_win[shared_rows, lanes]
        k = k_win[:, lanes]
        v = v_win[:, lanes]
        q = q_win[:, lanes]
        g = ga_win[:, lanes]
        product = g_x.astype(F32) * o32_x[:, lanes]
        parts = []
        d_k = jnp.zeros((extra, 2 * HEAD_DIM), F32)
        d_v = jnp.zeros((extra, 2 * HEAD_DIM), F32)
        for h in range(2):
            head = 2 * hp + h
            keep = first_head_f32 if h == 0 else jnp.logical_not(first_head_f32)
            lse_col = jnp.sum(
                jnp.where(x_lane == head, lse_x[...], 0.0), axis=-1, keepdims=True
            )
            centre_col = jnp.sum(jnp.where(keep, product, 0.0), axis=-1, keepdims=True)
            probs = jnp.exp(dot_nt(q_x * head_mask[h], k) + bias_x[...] - lse_col)
            grad_scores = (probs * (dot_nt(g_x * head_mask[h], v) - centre_col)).astype(BF16)
            parts.append(dot_nn(grad_scores, k))
            qm = q * head_mask[h]
            gm = g * head_mask[h]
            lse_line = stat_line(head, 0, 5)
            centre_line = stat_line(16 + head, 0, 5)
            probs = jnp.exp(dot_nt(k_x, qm) + bias_x[:, 0:window] - lse_line)
            grad_scores = (probs * (dot_nt(v_x, gm) - centre_line)).astype(BF16)
            d_k = d_k + dot_nn(grad_scores, qm)
            d_v = d_v + dot_nn(probs.astype(BF16), gm)
        d_q = jnp.where(first_head_f32, parts[0], parts[1]) * SCALE
        for n, part in enumerate((d_q, d_k, d_v)):
            to = pl.ds(pl.multiple_of(n * width + hp * 128, 128), 128)
            dqkv[p_block:tok_block, to] = jnp.where(shared, part, 0.0).astype(BF16)
        return carry

    own_keys(own_at, 2)
    advance_one(2)
    advance_two(0)
    advance_two(4)
    stat_partner(partner_at).wait_recv()
    ga_partner(partner_at).wait_recv()

    @pl.when(s < groups - 1)
    def _():
        stat_half(0, 0, half_at, partner).wait_recv()
        ga_half(0, 0, half_at, partner).wait_recv()

    @pl.when(s < 2)
    def _():
        lax.fori_loop(0, x_pairs, shared_back, 0)

    @pl.when(s == 2)
    def _():
        dqkv[0:extra, 0:width] = jnp.where(
            shared, 0.0, dqkv[0:extra, 0:width].astype(F32)
        ).astype(BF16)

    q_mine = pl.ds(pl.multiple_of(core * half_w, 128), half_w)
    q_other = pl.ds(pl.multiple_of((1 - core) * half_w, 128), half_w)
    send_q = pair_copy(X_Q, dqkv.at[:, q_other], dqp.at[0])
    send_q.start()
    start_three(0)
    start_three(4)
    own_keys(partner_at, 2)
    send_q.wait_recv()
    store_rows(9, dot_nn(nbt[0], dqkv[:, q_mine]) + dot_nn(nbt[1], dqp[0]))
    stage_one(9).start()
    advance_one(6)
    reduced(1)
    reduced(5)
    own_keys(half_at, 1)
    advance_one(3)
    reduced(2)
    advance_one(7)
    reduced(6)

    @pl.when(s == 2)
    def _():
        dk[0:extra, :] = jnp.where(shared, 0.0, dk[0:extra, :])
        dv[0:extra, :] = jnp.where(shared, 0.0, dv[0:extra, :])

    dqkv[0:local_len, width : 2 * width] = dk[...].astype(BF16)
    dqkv[0:local_len, 2 * width :] = dv[...].astype(BF16)
    send_kv = [
        pair_copy(
            X_KV + i,
            dqkv.at[:, pl.ds(pl.multiple_of((1 + i) * width + (1 - core) * half_w, 128), half_w)],
            dqp.at[1 + i],
        )
        for i in range(2)
    ]
    for copy in send_kv:
        copy.start()
    reduced(3)
    reduced(7)
    advance_one(8)

    grad_normed = dot_nt(dqkv[...], wqkv[...])
    grad_x = grad_normed[p_block:tok_block, :]
    e_x[...] = grad_x.astype(BF16)

    def e_back(j, to):
        return remote(e_x, e_in.at[j], ex_s.at[0], ex_r.at[j], (b, to))

    @pl.when(s < 2)
    def _():
        e_back(s, 2).start()

    for i in range(2):
        send_kv[i].wait_recv()
        lane = pl.ds(pl.multiple_of((1 + i) * width + core * half_w, 128), half_w)
        store_rows(
            10 + i,
            dot_nn(nbt[0], dqkv[:, lane]) + dot_nn(nbt[1], dqp[1 + i]),
        )
        stage_one(10 + i).start()

    advance_one(9)
    reduced(8)
    grad_tok = grad_normed[0:local_len, :]
    e_low[...] = grad_tok[0:extra, :]
    grad_pro = grad_normed[local_len : local_len + prompt_count, :]
    scaled1, inverse1 = norm_stats(tokens_ref[...].astype(F32))
    grad_input_ref[...] = (mid[...] + norm_back(grad_tok, scaled1, inverse1, gain1)).astype(BF16)
    p_scaled, p_inverse = norm_stats(prompts_ref[...])
    sm[0:prompt_count, :] = norm_back(grad_pro, p_scaled, p_inverse, gain1)
    sm[prompt_count : prompt_count + 1, :] = (
        column_sum(grad_tok * scaled1)
        + column_sum(grad_pro * p_scaled)
        + column_sum(grad_x * xh_x[...])
    )
    sm[prompt_count + 1 : prompt_count + 2, :] = (
        column_sum(grad_tok) + column_sum(grad_pro) + column_sum(grad_x)
    )
    sm[prompt_count + 2 : prompt_count + 3, :] = column_sum(dqkv[:, :width].astype(F32))
    sm[prompt_count + 3 : prompt_count + 4, :] = column_sum(dqkv[:, 2 * width :].astype(F32))
    send_sm = pair_copy(X_SMALL, sm.at[:, other_half], smp)
    send_sm.start()
    reduced(9)

    quarter = SMALL_ROWS // 4
    send_sm.wait_recv()
    small = sm[:, my_half] + smp[...]
    for a in range(2):
        for c in range(2):
            s0[a, c] = small[(2 * a + c) * quarter : (2 * a + c + 1) * quarter, :]

    small_one = remote(s0.at[1 - h1], rs1, one_s.at[12], one_r.at[12], nb1)
    small_one.start()
    advance_one(10)
    advance_one(11)
    small_one.wait_recv()
    s1b[...] = s0[h1] + rs1[...]
    small_two = remote(s1b.at[1 - h2], rs2, two_s.at[12], two_r.at[12], nb2)
    small_two.start()
    finish_three(0)
    reduced(10)
    reduced(11)
    small_two.wait_recv()
    rs3[s] = s1b[h2] + rs2[...]

    def small_three(d):
        return remote(
            rs3.at[s], rs3.at[s], three_s.at[12, d - 1], three_r.at[12, s], (b, along(d))
        )

    def small_three_recv(j):
        return remote(rs3.at[j], rs3.at[j], three_s.at[12, 0], three_r.at[12, j], (b, j))

    for d in range(1, groups):
        small_three(d).start()
    finish_three(1)
    start_gather_two(0)
    finish_three(2)
    start_gather_two(1)
    start_gather_pair(0)
    finish_three(3)
    start_gather_pair(1)
    for d in range(1, groups):
        small_three_recv(along(d)).wait_recv()
    total = rs3[0]
    for j in range(1, groups):
        total = total + rs3[j]
    s3[...] = total
    small_keep = pltpu.make_async_copy(s3, small_ref.at[core, h1, h2], loc_sem.at[SMALL])
    small_keep.start()
    small_gather = remote(
        s3, small_ref.at[core, h1, h2], ag1_s.at[SMALL], ag1_r.at[SMALL], nb2
    )
    small_gather.start()
    start_gather_two(2)

    @pl.when(s == 2)
    def _():
        for j in range(2):
            e_back(j, j).wait_recv()
        full = e_low[...] + e_in[0].astype(F32) + e_in[1].astype(F32)
        scaled, inverse = norm_stats(tokens_ref[0:extra, :].astype(F32))
        grad_input_ref[0:extra, :] = (
            mid[0:extra, :] + norm_back(full, scaled, inverse, gain1)
        ).astype(BF16)

    start_gather_two(3)
    small_keep.wait()
    small_gather.wait_recv()
    small_gather_two = remote(
        small_ref.at[core, h1], small_ref.at[core, h1], ag2_s.at[SMALL], ag2_r.at[SMALL], nb1
    )
    small_gather_two.start()
    start_gather_pair(2)
    start_gather_pair(3)
    small_gather_two.wait_recv()
    small_pair = pair_copy(X_FINAL + SMALL, small_ref.at[core], small_ref.at[core])
    small_pair.start()

    small_pair.wait()
    for g in range(len(SLOTS)):
        gather_pair(g).wait()
        gather_one(g).wait_send()
        gather_two(g).wait_send()
    for u in range(12):
        drain_three(u)
    small_one.wait_send()
    small_two.wait_send()
    small_gather.wait_send()
    small_gather_two.wait_send()
    for d in range(1, groups):
        small_three(d).wait_send()

    token_partner(own_rows).wait_send()
    stat_partner(own_at).wait_send()
    ga_partner(own_at).wait_send()
    for_halves(lambda *a: token_half(*a).wait_send())
    for_halves(lambda *a: stat_half(*a).wait_send())
    for_halves(lambda *a: ga_half(*a).wait_send())

    @pl.when(s < 2)
    def _():
        att_back(s).wait_send()
        lse_back(s).wait_send()
        e_back(s, 2).wait_send()

    def drain(u, carry):
        stage_one(u).wait_send()
        stage_two(u).wait_send()
        return carry

    lax.fori_loop(0, 12, drain, 0)

    def drain_mlp(j, carry):
        send_act(j).wait_send()
        send_gp(j).wait_send()
        return carry

    lax.fori_loop(0, chunks, drain_mlp, 0)
    for copy in (send_cot, send_norm, send_extra, send_att, send_n2, send_gb, send_q, *send_kv, send_sm):
        copy.wait_send()


def finish_kernel(
    width,
    prompt_count,
    ff,
    layer_in,
    grad_in,
    final_hbm,
    small_hbm,
    layer_out_ref,
    grad_input_ref,
    gp_ref,
    g1_ref,
    s1_ref,
    wqkv_ref,
    qb_ref,
    vb_ref,
    wout_ref,
    ob_ref,
    g2_ref,
    s2_ref,
    wfc1_ref,
    b1_ref,
    wfc2_ref,
    b2_ref,
    final,
    small_in,
    small,
    layer_buf,
    grad_buf,
    fc2_buf,
    fc1_buf,
    out_buf,
    qkv_buf,
    in_sem,
    out_sem,
):
    half_w = width // 2
    blk = final_hbm.shape[4]
    loads = [
        pltpu.make_async_copy(
            final_hbm.at[:, :, :, pl.ds(4 * g, 4)], final.at[g], in_sem.at[g]
        )
        for g in range(3)
    ]
    loads.append(pltpu.make_async_copy(small_hbm, small_in, in_sem.at[3]))
    loads.append(pltpu.make_async_copy(layer_in, layer_buf, in_sem.at[4]))
    loads.append(pltpu.make_async_copy(grad_in, grad_buf, in_sem.at[5]))
    for load in loads:
        load.start()
    stores = []

    def store(src, dst):
        copy = pltpu.make_async_copy(src, dst, out_sem.at[len(stores)])
        copy.start()
        stores.append(copy)

    quads = [(c, a, e) for c in range(2) for a in range(2) for e in range(2)]
    loads[0].wait()
    for c, a, e in quads:
        for i in range(4):
            q, r = i // 2, i % 2
            row = c * half_w + (2 * a + e) * (half_w // 4) + r * blk
            fc2_buf[row : row + blk, q * half_w : (q + 1) * half_w] = final[0, c, a, e, i].astype(
                F32
            )
    store(fc2_buf, wfc2_ref)
    loads[1].wait()
    for c, a, e in quads:
        rows = slice((2 * a + e) * blk, (2 * a + e + 1) * blk)
        for i in range(4):
            col = i * width + c * half_w
            fc1_buf[rows, col : col + half_w] = final[1, c, a, e, i].astype(F32)
    store(fc1_buf, wfc1_ref)
    loads[2].wait()
    for c, a, e in quads:
        rows = slice((2 * a + e) * blk, (2 * a + e + 1) * blk)
        cols = slice(c * half_w, (c + 1) * half_w)
        out_buf[rows, cols] = final[2, c, a, e, 0].astype(F32)
        for i in range(3):
            col = i * width + c * half_w
            qkv_buf[rows, col : col + half_w] = final[2, c, a, e, 1 + i].astype(F32)
    store(out_buf, wout_ref)
    store(qkv_buf, wqkv_ref)
    loads[4].wait()
    store(layer_buf, layer_out_ref)
    loads[5].wait()
    store(grad_buf, grad_input_ref)
    loads[3].wait()
    quarter = small_in.shape[3]
    for c, a, e in quads:
        r = (2 * a + e) * quarter
        small[r : r + quarter, c * half_w : (c + 1) * half_w] = small_in[c, a, e]
    gp_ref[...] = small[0:prompt_count, :]
    for k, ref in enumerate((g1_ref, s1_ref, qb_ref, vb_ref, ob_ref, g2_ref, s2_ref)):
        ref[...] = small[prompt_count + k : prompt_count + k + 1, :].reshape(width)
    for k in range(ff // width):
        r = prompt_count + 7 + k
        b1_ref[k * width : (k + 1) * width] = small[r : r + 1, :].reshape(width)
    r = prompt_count + 7 + ff // width
    b2_ref[...] = small[r : r + 1, :].reshape(width)
    for copy in stores:
        copy.wait()


def local(
    tokens,
    segments,
    prompts,
    ln1_gain,
    ln1_shift,
    w_qkv,
    q_bias,
    v_bias,
    w_out,
    out_bias,
    ln2_gain,
    ln2_shift,
    w_fc1,
    fc1_bias,
    w_fc2,
    fc2_bias,
    cotangent,
):
    groups = lax.axis_size("seq")
    batch = lax.axis_size("batch")
    row_count, local_len, width = tokens.shape
    ff = w_fc1.shape[1]
    prompt_count = prompts.shape[0]
    assert row_count == 1 and groups == 4 and batch % GROUP == 0 and ff == 4 * width
    check_window(groups, local_len)
    dims = (groups, local_len, width, ff, prompt_count)
    window = 5 * (local_len // 2)
    extra = extra_rows(local_len)
    half_w = width // 2
    blk = width // groups // 4
    tok_block = local_len + PROMPT_PAD + extra
    quarter = SMALL_ROWS // 4

    vmem = pl.BlockSpec(memory_space=pltpu.VMEM)
    hbm = pl.BlockSpec(memory_space=pl.ANY)
    dma = pltpu.SemaphoreType.DMA
    V = pltpu.VMEM
    scratch = [
        V((width, 3 * width), BF16),
        V((width, width), BF16),
        V((width, ff), BF16),
        V((ff, width), BF16),
        V((window, width), BF16),
        V((2, tok_block, width), BF16),
        V((2, width, tok_block), BF16),
        V((window, width), BF16),
        V((window + PROMPT_PAD, width), BF16),
        V((window + PROMPT_PAD, width), BF16),
        V((local_len, window + PROMPT_PAD), F32),
        V((local_len, width), F32),
        V((2 * local_len, width), BF16),
        V((local_len, 128), F32),
        V((local_len, 128), F32),
        V((local_len, width), F32),
        V((local_len, width), F32),
        V((local_len, 1), F32),
        V((2 * local_len, width), BF16),
        V((width, 2 * local_len), BF16),
        V((4, local_len, width), BF16),
        V((4, local_len, width), BF16),
        V((4, local_len, half_w), BF16),
        V((4, local_len, half_w), BF16),
        V((4, width), F32),
        V((local_len, width), F32),
        V((local_len, width), F32),
        V((local_len, width), BF16),
        V((local_len, width), BF16),
        V((local_len, half_w), BF16),
        V((window, width), BF16),
        V((5, 32, local_len // 2), F32),
        V((local_len, width), F32),
        V((local_len, width), F32),
        V((tok_block, 3 * width), BF16),
        V((3, tok_block, half_w), BF16),
        V((12, 2, 2, 4, blk, half_w), BF16),
        V((12, 2, 4, blk, half_w), BF16),
        V((12, 4, blk, half_w), BF16),
        V((groups, 12, blk, half_w), BF16),
        V((12, blk, half_w), BF16),
        V((SMALL_ROWS, width), F32),
        V((SMALL_ROWS, half_w), F32),
        V((2, 2, quarter, half_w), F32),
        V((2, quarter, half_w), F32),
        V((2, quarter, half_w), F32),
        V((quarter, half_w), F32),
        V((groups, quarter, half_w), F32),
        V((quarter, half_w), F32),
        V((extra, window + PROMPT_PAD), F32),
        V((extra, width), F32),
        V((extra, width), BF16),
        V((extra, 128), F32),
        V((extra, width), BF16),
        V((2, extra, 128), F32),
        V((extra, width), F32),
        V((extra, width), BF16),
        V((2, extra, width), BF16),
        V((extra, width), F32),
        dma((4,)),
        dma((4,)),
        dma((2,)),
        dma((X_COUNT,)),
        dma((X_COUNT,)),
        dma((4,)),
        dma((2,)),
        dma((4,)),
        dma((2,)),
        dma((13,)),
        dma((13,)),
        dma((13,)),
        dma((13,)),
        dma((13, 3)),
        dma((13, groups)),
        dma((5,)),
        dma((5,)),
        dma((5,)),
        dma((5,)),
        dma((5,)),
        dma((2,)),
        dma((2, 2)),
        dma((1,)),
        dma((2,)),
    ]
    specs = [vmem] * 17
    for index in (5, 8, 12, 14):
        specs[index] = hbm
    layer_out, grad_input, final, small = pl.pallas_call(
        functools.partial(layer_kernel, dims),
        out_shape=(
            jax.ShapeDtypeStruct((local_len, width), BF16),
            jax.ShapeDtypeStruct((local_len, width), BF16),
            jax.ShapeDtypeStruct((2, 2, 2, 12, blk, half_w), BF16),
            jax.ShapeDtypeStruct((2, 2, 2, quarter, half_w), F32),
        ),
        in_specs=specs,
        out_specs=(vmem, vmem, hbm, hbm),
        scratch_shapes=scratch,
        compiler_params=pltpu.CompilerParams(
            collective_id=0, has_side_effects=True, vmem_limit_bytes=67043328
        ),
        name="layer",
    )(
        tokens.reshape(local_len, width),
        segments,
        prompts,
        ln1_gain,
        ln1_shift,
        w_qkv,
        q_bias,
        v_bias,
        w_out,
        out_bias,
        ln2_gain,
        ln2_shift,
        w_fc1,
        fc1_bias,
        w_fc2,
        fc2_bias,
        cotangent.reshape(local_len, width),
    )
    if batch > GROUP:
        rings = [list(range(k, batch, GROUP)) for k in range(GROUP)]
        final, small = lax.psum((final, small), "batch", axis_index_groups=rings)
    rows_z = width // groups

    def flat(n):
        return jax.ShapeDtypeStruct((n,), F32)

    outs = pl.pallas_call(
        functools.partial(finish_kernel, width, prompt_count, ff),
        out_shape=(
            jax.ShapeDtypeStruct((local_len, width), BF16),
            jax.ShapeDtypeStruct((local_len, width), BF16),
            jax.ShapeDtypeStruct((prompt_count, width), F32),
            flat(width),
            flat(width),
            jax.ShapeDtypeStruct((rows_z, 3 * width), F32),
            flat(width),
            flat(width),
            jax.ShapeDtypeStruct((rows_z, width), F32),
            flat(width),
            flat(width),
            flat(width),
            jax.ShapeDtypeStruct((rows_z, ff), F32),
            flat(ff),
            jax.ShapeDtypeStruct((ff // groups, width), F32),
            flat(width),
        ),
        in_specs=[pl.BlockSpec(memory_space=pltpu.HBM)] * 4,
        out_specs=tuple(hbm if i in (0, 1, 5, 8, 12, 14) else vmem for i in range(16)),
        scratch_shapes=[
            V((3, 2, 2, 2, 4, blk, half_w), BF16),
            V((2, 2, 2, quarter, half_w), F32),
            V((SMALL_ROWS, width), F32),
            V((local_len, width), BF16),
            V((local_len, width), BF16),
            V((ff // groups, width), F32),
            V((rows_z, ff), F32),
            V((rows_z, width), F32),
            V((rows_z, 3 * width), F32),
            dma((6,)),
            dma((6,)),
        ],
        compiler_params=pltpu.CompilerParams(vmem_limit_bytes=67043328),
        name="finish",
    )(layer_out, grad_input, final, small)
    return tuple(o.reshape((1, local_len, width)) if i < 2 else o for i, o in enumerate(outs))


def solution(mesh):
    tok = P("batch", "seq", None)
    in_specs = (tok, P("batch", "seq")) + (P(),) * 14 + (tok,)
    out_specs = (
        tok,
        tok,
        P(),
        P(),
        P(),
        P("seq", None),
        P(),
        P(),
        P("seq", None),
        P(),
        P(),
        P(),
        P("seq", None),
        P(),
        P("seq", None),
        P(),
    )
    return jax.shard_map(local, mesh=mesh, in_specs=in_specs, out_specs=out_specs, check_vma=False)
```

```python
import functools

import jax
import jax.numpy as jnp
from jax import lax
from jax.experimental import pallas as pl
from jax.experimental.pallas import tpu as pltpu
from jax.sharding import PartitionSpec as P

HEAD_DIM = 64
IMAGE_TOKENS = (101, 197, 577)
EPSILON = 1e-06
MASKED_SCORE = -1e30
ROOT_HALF = 0.7071067811865476
ROOT_TWO_PI = 2.5066282746310002
SCALE = HEAD_DIM ** (-0.5)
GROUP = 8
PROMPT_PAD = 64
SMALL_ROWS = 64
F32 = jnp.float32
BF16 = jnp.bfloat16
MESH = pl.DeviceIdType.MESH


def dot_nn(a, b):
    return lax.dot_general(a, b, (((1,), (0,)), ((), ())), preferred_element_type=F32)


def dot_nt(a, b):
    return lax.dot_general(a, b, (((1,), (1,)), ((), ())), preferred_element_type=F32)


def dot_tn(a, b):
    return lax.dot_general(a, b, (((0,), (0,)), ((), ())), preferred_element_type=F32)


def check_window(groups, local_len):
    row_len, half_len = groups * local_len, local_len // 2
    cut = 2 * local_len
    for size in IMAGE_TOKENS:
        for first in range(0, row_len, size):
            last = min(first + size, row_len) - 1
            for shard in range(first // local_len, last // local_len + 1):
                start = 0 if shard < 2 else 3 * half_len
                inside = start <= first and last < start + 5 * half_len
                if shard == 3:
                    inside = inside and first >= cut
                given = size == IMAGE_TOKENS[-1] and shard == 2 and first == 0
                assert inside or given
                assert not given or last < cut + extra_rows(local_len)


def extra_rows(local_len):
    return -(-(IMAGE_TOKENS[-1] - 2 * local_len) // 16) * 16


def half_rows_needed(local_len, src, dst):
    if src < dst:
        return local_len // 2
    top = 0
    for size in IMAGE_TOKENS:
        end = ((dst + 1) * local_len - 1) // size * size + size
        top = max(top, end - 2 * local_len)
    return min(-(-top // 16) * 16, local_len // 2)


def norm_stats(values):
    centred = values - jnp.mean(values, axis=-1, keepdims=True)
    inverse = lax.rsqrt(jnp.mean(centred * centred, axis=-1, keepdims=True) + EPSILON)
    return centred * inverse, inverse


def norm_back(grad_out, scaled, inverse, gain):
    inner = grad_out * gain
    return inverse * (
        inner
        - jnp.mean(inner, axis=-1, keepdims=True)
        - scaled * jnp.mean(inner * scaled, axis=-1, keepdims=True)
    )


def line(ref):
    return ref[...].reshape(1, -1)


def column_sum(values):
    return jnp.sum(values, axis=0, keepdims=True)


X_COT, X_N2, X_ATT, X_NORM, X_GB, X_Q, X_KV, X_SMALL, X_FINAL, X_ACT, X_GP, X_EXTRA = 0, 1, 2, 3, 4, 5, 6, 8, 9, 14, 18, 22
X_COUNT = 23
HALVES = ((2, 0, 0), (2, 1, 0), (1, 2, 1))
SLOTS = ((0, 4), (4, 4), (8, 2), (10, 2))
SMALL = 4


def layer_kernel(
    dims,
    tokens_ref,
    seg_ref,
    prompts_ref,
    g1_ref,
    s1_ref,
    wqkv_hbm,
    qb_ref,
    vb_ref,
    wout_hbm,
    ob_ref,
    g2_ref,
    s2_ref,
    wfc1_hbm,
    b1_ref,
    wfc2_hbm,
    b2_ref,
    cot_ref,
    layer_out_ref,
    grad_input_ref,
    final_ref,
    small_ref,
    wqkv,
    wout,
    wfc1,
    wfc2,
    tokw,
    nb,
    nbt,
    q_win,
    k_win,
    v_win,
    bias,
    o32,
    att,
    lse,
    centre,
    mid,
    n2,
    n2t,
    act,
    gp,
    actp,
    gpp,
    b1s,
    acc_out,
    acc_dn,
    cotp,
    gb,
    gbp,
    ga_win,
    stat,
    dqkv,
    dqp,
    units,
    r1,
    r2u,
    r3,
    a3,
    sm,
    smp,
    s0,
    rs1,
    s1b,
    rs2,
    rs3,
    s3,
    bias_x,
    o32_x,
    att_x,
    lse_x,
    att_in,
    lse_in,
    xh_x,
    e_x,
    e_in,
    e_low,
    dact,
    wsem,
    tok_s,
    tok_r,
    pair_s,
    pair_r,
    ga_s,
    ga_r,
    st_s,
    st_r,
    one_s,
    one_r,
    two_s,
    two_r,
    three_s,
    three_r,
    loc_sem,
    ag1_s,
    ag1_r,
    ag2_s,
    ag2_r,
    ax_s,
    ax_r,
    ex_s,
    ex_r,
):
    groups, local_len, width, ff, prompt_count = dims
    half_len = local_len // 2
    window = 5 * half_len
    cut = 2 * local_len
    extra = extra_rows(local_len)
    head_pairs = width // (2 * HEAD_DIM)
    chunks = ff // width
    half_w = width // 2
    key_len = window + PROMPT_PAD
    zrows = width // groups

    b = lax.axis_index("batch")
    s = lax.axis_index("seq")
    base = (b // GROUP) * GROUP
    core = lax.rem(b, 2)
    xb = lax.rem(b // 2, 2)
    yb = lax.rem(b // 4, 2)
    h1 = xb * (1 - core) + yb * core
    h2 = yb * (1 - core) + xb * core

    def place(x, y, c):
        return base + y * 4 + x * 2 + c

    nb1 = (place(xb + (1 - core) * (1 - 2 * xb), yb + core * (1 - 2 * yb), core), s)
    nb2 = (place(xb + core * (1 - 2 * xb), yb + (1 - core) * (1 - 2 * yb), core), s)
    pair = (place(xb, yb, 1 - core), s)

    def along(d):
        return lax.rem(s + d, groups)

    first_half = jnp.where(s < 2, 0, 3)
    start = first_half * half_len
    partner = s + 1 - 2 * lax.rem(s, 2)
    own_at = 2 * s - first_half
    partner_at = 2 * partner - first_half
    half_at = jnp.where(s < 2, 4, 0)

    def halves(at, count):
        return pl.ds(pl.multiple_of(at * half_len, half_len), count * half_len)

    own_rows = halves(own_at, 2)
    partner_rows = halves(partner_at, 2)
    half_rows = halves(half_at, 1)
    shared_rows = pl.ds(4 * half_len, extra)

    def remote(src, dst, send, recv, to):
        return pltpu.make_async_remote_copy(
            src_ref=src, dst_ref=dst, send_sem=send, recv_sem=recv, device_id=to, device_id_type=MESH
        )

    barrier = pltpu.get_barrier_semaphore()
    for peer in (pair, nb1, nb2):
        pl.semaphore_signal(barrier, inc=1, device_id=peer, device_id_type=MESH)
    for d in range(1, groups):
        pl.semaphore_signal(barrier, inc=1, device_id=(b, along(d)), device_id_type=MESH)

    loads = [
        pltpu.make_async_copy(wqkv_hbm, wqkv, wsem.at[0]),
        pltpu.make_async_copy(wout_hbm, wout, wsem.at[1]),
        pltpu.make_async_copy(wfc1_hbm, wfc1, wsem.at[2]),
        pltpu.make_async_copy(wfc2_hbm, wfc2, wsem.at[3]),
    ]
    loads[0].start()
    pl.semaphore_wait(barrier, 2 + groups)

    def token_partner(side, at):
        part = tokens_ref.at[pl.ds(side * half_len, half_len)]
        return remote(
            part, tokw.at[halves(at + side, 1)], tok_s.at[side], tok_r.at[side], (b, partner)
        )

    def token_half(i, side, at, to):
        count = half_rows_needed(local_len, HALVES[i][0], HALVES[i][1])
        return remote(
            tokens_ref.at[pl.ds(side * half_len, count)],
            tokw.at[pl.ds(at * half_len, count)],
            tok_s.at[2 + i],
            tok_r.at[2],
            (b, to),
        )

    def for_halves(action):
        for i, (src, dst, side) in enumerate(HALVES):

            @pl.when(s == src)
            def _(i=i, dst=dst, side=side):
                action(i, side, 4 if dst < 2 else 0, dst)

    def for_half_in(action):
        for i, (src, dst, side) in enumerate(HALVES):

            @pl.when(s == dst)
            def _(i=i, src=src, side=side, dst=dst):
                action(i, side, 4 if dst < 2 else 0, src)

    for_halves(lambda *a: token_half(*a).start())
    for side in range(2):
        token_partner(side, own_at).start()

    for load in loads[1:]:
        load.start()

    def pair_copy(index, src, dst):
        return remote(src, dst, pair_s.at[index], pair_r.at[index], pair)

    my_half = pl.ds(pl.multiple_of(core * half_w, 128), half_w)
    other_half = pl.ds(pl.multiple_of((1 - core) * half_w, 128), half_w)

    send_cot = pair_copy(X_COT, cot_ref, cotp)
    send_cot.start()

    gain1 = line(g1_ref)
    shift1 = line(s1_ref)
    for i in range(chunks):
        b1s[i : i + 1, :] = b1_ref[i * width : (i + 1) * width].reshape(1, width)

    last = s * local_len + local_len - 1
    seg_last = seg_ref[:, local_len - 1 : local_len].astype(F32)
    inv_n = jnp.full((1, 1), 1.0 / IMAGE_TOKENS[-1], F32)
    is_long = jnp.ones((1, 1), F32)
    for size in IMAGE_TOKENS[:-1]:
        here = seg_last == (last // size).astype(F32)
        inv_n = jnp.where(here, 1.0 / size, inv_n)
        is_long = jnp.where(here, 0.0, is_long)
    k_pos = lax.broadcasted_iota(jnp.int32, (1, key_len), 1)
    k_open = jnp.where(k_pos < window, 0.0, jnp.where(k_pos < window + prompt_count, 1.0, 0.0))
    k_id = jnp.floor(((k_pos + start).astype(F32) + 0.5) * inv_n)
    k_id = jnp.where(k_pos < window, k_id, -1.0)

    def mask_of(q_pos):
        q_id = jnp.floor((q_pos.astype(F32) + 0.5) * inv_n)
        return jnp.where(q_id == k_id, 0.0, MASKED_SCORE * (1.0 - k_open))

    bias[...] = mask_of(lax.broadcasted_iota(jnp.int32, (local_len, 1), 0) + s * local_len)
    x_row = lax.broadcasted_iota(jnp.int32, (extra, 1), 0)
    bias_x[...] = mask_of(x_row + cut)
    shared = jnp.where(x_row + cut < IMAGE_TOKENS[-1], is_long, 0.0) > 0.5

    def project_q(normed, rows):
        q = dot_nn(normed, wqkv[:, :width]) + line(qb_ref)
        q_win[rows, :] = (q.astype(BF16).astype(F32) * SCALE).astype(BF16)

    def project(normed, rows):
        k_win[rows, :] = dot_nn(normed, wqkv[:, width : 2 * width]).astype(BF16)
        v_win[rows, :] = (dot_nn(normed, wqkv[:, 2 * width :]) + line(vb_ref)).astype(BF16)

    p_scaled, p_inverse = norm_stats(prompts_ref[...])
    p_block = local_len + PROMPT_PAD
    tok_block = p_block + extra
    nb[0, local_len:p_block, :] = jnp.zeros((PROMPT_PAD, width), BF16)
    nb[0, local_len : local_len + prompt_count, :] = (p_scaled * gain1 + shift1).astype(BF16)
    scaled1, _ = norm_stats(tokens_ref[...].astype(F32))
    nb[0, 0:local_len, :] = (scaled1 * gain1 + shift1).astype(BF16)
    send_norm = pair_copy(X_NORM, nb.at[0, pl.ds(0, p_block)], nb.at[1, pl.ds(0, p_block)])
    send_norm.start()

    tail = half_rows_needed(local_len, 2, 0)
    tail_rows = pl.ds(4 * half_len + tail, half_len - tail)

    @pl.when(s == 0)
    def _():
        tokw[tail_rows, :] = jnp.zeros((half_len - tail, width), BF16)
        ga_win[tail_rows, :] = jnp.zeros((half_len - tail, width), BF16)

    tail_one = half_rows_needed(local_len, 2, 1)
    tail_one_rows = pl.ds(4 * half_len + tail_one, half_len - tail_one)

    @pl.when(s == 1)
    def _():
        tokw[tail_one_rows, :] = jnp.zeros((half_len - tail_one, width), BF16)
        ga_win[tail_one_rows, :] = jnp.zeros((half_len - tail_one, width), BF16)

    loads[0].wait()
    project_q(nb[0, 0:local_len, :], own_rows)
    project(nb[0, 0:local_len, :], own_rows)
    p_low = nb[0, local_len:p_block, :]
    k_win[window:key_len, :] = dot_nn(p_low, wqkv[:, width : 2 * width]).astype(BF16)
    v_win[window:key_len, :] = (dot_nn(p_low, wqkv[:, 2 * width :]) + line(vb_ref)).astype(BF16)

    def normed_tokens(rows):
        scaled, _ = norm_stats(tokw[rows, :].astype(F32))
        return (scaled * gain1 + shift1).astype(BF16)

    loads[3].wait()

    held = chunks - 1

    def grad_act(i, carry):
        rows = pl.ds(pl.multiple_of(i * width, 128), width)
        dact[lax.rem(i, held)] = dot_nt(cot_ref[...], wfc2[rows, :])
        return carry

    lax.fori_loop(0, held, grad_act, 0)

    def partner_piece(side):
        token_partner(side, partner_at).wait_recv()
        rows = halves(partner_at + side, 1)
        normed = normed_tokens(rows)
        tokw[rows, :] = normed
        project(normed, rows)

    partner_piece(0)
    for_half_in(lambda *a: token_half(*a).wait_recv())

    @pl.when(s < groups - 1)
    def _():
        normed = normed_tokens(half_rows)
        project_q(normed, half_rows)
        project(normed, half_rows)

    partner_piece(1)

    @pl.when(s == groups - 1)
    def _():
        empty = jnp.zeros((half_len, width), BF16)
        q_win[0:half_len, :] = empty
        k_win[0:half_len, :] = empty
        v_win[0:half_len, :] = empty
        ga_win[0:half_len, :] = empty
        stat[0] = jnp.zeros((32, half_len), F32)

    @pl.when(s < 2)
    def _():
        scaled, _ = norm_stats(tokw[shared_rows, :].astype(F32))
        xh_x[...] = scaled
        nb[0, p_block:tok_block, :] = (scaled * gain1 + shift1).astype(BF16)

    @pl.when(s >= 2)
    def _():
        xh_x[...] = jnp.zeros((extra, width), F32)
        nb[0, p_block:tok_block, :] = jnp.zeros((extra, width), BF16)

    send_extra = pair_copy(
        X_EXTRA, nb.at[0, pl.ds(p_block, extra)], nb.at[1, pl.ds(p_block, extra)]
    )
    send_extra.start()

    pair_lane = lax.broadcasted_iota(jnp.int32, (1, 2 * HEAD_DIM), 1)
    first_head = jnp.where(pair_lane < HEAD_DIM, 1.0, 0.0)
    head_mask = (first_head.astype(BF16), (1.0 - first_head).astype(BF16))
    first_head_f32 = pair_lane < HEAD_DIM
    stat_lane = lax.broadcasted_iota(jnp.int32, (local_len, 128), 1)

    def lanes_of(hp):
        return pl.ds(pl.multiple_of(hp * 2 * HEAD_DIM, 128), 2 * HEAD_DIM)

    lse[...] = jnp.zeros((local_len, 128), F32)
    centre[...] = jnp.zeros((local_len, 128), F32)

    def softmax_heads(q, lanes, mask):
        k = k_win[:, lanes]
        v = v_win[:, lanes]
        outs, logs = [], []
        for h in range(2):
            scores = dot_nt(q * head_mask[h], k) + mask[...]
            highest = jnp.max(scores, axis=-1, keepdims=True)
            weights = jnp.exp(scores - highest)
            total = jnp.sum(weights, axis=-1, keepdims=True)
            outs.append(dot_nn(weights.astype(BF16), v) / total)
            logs.append(highest + jnp.log(total))
        return jnp.where(first_head_f32, outs[0], outs[1]), logs

    x_pairs = head_pairs // 2
    x_lane = lax.broadcasted_iota(jnp.int32, (extra, 128), 1)

    def x_lanes(j):
        return pl.ds(pl.multiple_of(j * half_w, 128), half_w)

    def att_back(j):
        return remote(
            att_x.at[:, x_lanes(j)], att_in.at[:, x_lanes(j)], ax_s.at[0], ax_r.at[0, j], (b, 2)
        )

    def lse_back(j):
        return remote(lse_x, lse_in.at[j], ax_s.at[1], ax_r.at[1, j], (b, 2))

    @pl.when(s < 2)
    def _():
        lse_x[...] = jnp.zeros((extra, 128), F32)

        def attend_shared(i, carry):
            hp = s * x_pairs + i
            lanes = lanes_of(hp)
            combined, logs = softmax_heads(q_win[shared_rows, lanes], lanes, bias_x)
            o32_x[:, lanes] = combined
            att_x[:, lanes] = combined.astype(BF16)
            for h in range(2):
                lse_x[...] = jnp.where(x_lane == 2 * hp + h, logs[h], lse_x[...])
            return carry

        lax.fori_loop(0, x_pairs, attend_shared, 0)
        att_back(s).start()
        lse_back(s).start()

    def attend(hp, carry):
        lanes = lanes_of(hp)
        combined, logs = softmax_heads(q_win[own_rows, lanes], lanes, bias)
        o32[:, lanes] = combined
        att[0:local_len, lanes] = combined.astype(BF16)
        for h in range(2):
            lse[...] = jnp.where(stat_lane == 2 * hp + h, logs[h], lse[...])
        return carry

    lax.fori_loop(0, head_pairs, attend, 0)

    @pl.when(s == 2)
    def _():
        for j in range(2):
            remote(
                att_x.at[:, x_lanes(j)], att_in.at[:, x_lanes(j)], ax_s.at[0], ax_r.at[0, j], (b, j)
            ).wait_recv()
            remote(lse_x, lse_in.at[j], ax_s.at[1], ax_r.at[1, j], (b, j)).wait_recv()
        merged = jnp.where(shared, att_in[...].astype(F32), o32[0:extra, :])
        o32[0:extra, :] = merged
        att[0:extra, :] = merged.astype(BF16)
        lse[0:extra, :] = jnp.where(shared, lse_in[0] + lse_in[1], lse[0:extra, :])

    own = pl.ds(0, local_len)
    theirs = pl.ds(local_len, local_len)
    send_att = pair_copy(X_ATT, att.at[own], att.at[theirs])
    send_att.start()

    loads[1].wait()
    mid[...] = (
        tokens_ref[...].astype(F32) + dot_nn(att[0:local_len, :], wout[...]) + line(ob_ref)
    )
    scaled2, _ = norm_stats(mid[...])
    n2[0:local_len, :] = (scaled2 * line(g2_ref) + line(s2_ref)).astype(BF16)
    send_n2 = pair_copy(X_N2, n2.at[own], n2.at[theirs])
    send_n2.start()
    acc_out[...] = jnp.zeros((local_len, width), F32)
    acc_dn[...] = jnp.zeros((local_len, width), F32)
    loads[2].wait()

    blk = zrows // 4

    def unit_of(p):
        return p // 2 + 4 * lax.rem(p, 2)

    def store_rows(u, grads):
        for z in range(groups):
            for a in range(2):
                for c in range(2):
                    r = z * zrows + (2 * a + c) * blk
                    units[u, a, c, z] = grads[r : r + blk, :].astype(BF16)

    def stage_one(u):
        return remote(units.at[u, 1 - h1], r1.at[u], one_s.at[u], one_r.at[u], nb1)

    def stage_two(u):
        return remote(units.at[u, h1, 1 - h2], r2u.at[u], two_s.at[u], two_r.at[u], nb2)

    def advance_one(u):
        stage_one(u).wait_recv()
        units[u, h1] = (units[u, h1].astype(F32) + r1[u].astype(F32)).astype(BF16)
        stage_two(u).start()

    def advance_two(u):
        stage_two(u).wait_recv()
        r2u[u] = (units[u, h1, h2].astype(F32) + r2u[u].astype(F32)).astype(BF16)

    def stage_three_fc2(u):
        return remote(
            r2u.at[u], r3.at[s, pl.ds(0, 4)], three_s.at[u, 0], three_r.at[0, s], (b, u)
        )

    def stage_three(u, d):
        t = along(d)
        return remote(r2u.at[u, t], r3.at[s, u], three_s.at[u, d - 1], three_r.at[u, s], (b, t))

    def start_three(u):
        if u < 4:

            @pl.when(s != u)
            def _():
                stage_three_fc2(u).start()

        else:
            for d in range(1, groups):
                stage_three(u, d).start()

    def drain_three(u):
        if u < 4:

            @pl.when(s != u)
            def _():
                stage_three_fc2(u).wait_send()

        else:
            for d in range(1, groups):
                stage_three(u, d).wait_send()

    def slots(g):
        return pl.ds(*SLOTS[g])

    def keep_final(g):
        return pltpu.make_async_copy(
            a3.at[slots(g)], final_ref.at[core, h1, h2, slots(g)], loc_sem.at[g]
        )

    def gather_one(g):
        return remote(
            a3.at[slots(g)],
            final_ref.at[core, h1, h2, slots(g)],
            ag1_s.at[g],
            ag1_r.at[g],
            nb2,
        )

    def gather_two(g):
        ref = final_ref.at[core, h1, :, slots(g)]
        return remote(ref, ref, ag2_s.at[g], ag2_r.at[g], nb1)

    def gather_pair(g):
        ref = final_ref.at[core, :, :, slots(g)]
        return pair_copy(X_FINAL + g, ref, ref)

    def finish_three(g):
        first, count = SLOTS[g]
        if g == 0:
            total = r2u[s].astype(F32)
            for d in range(1, groups):
                j = along(d)
                remote(
                    r2u.at[0], r3.at[j, pl.ds(0, 4)], three_s.at[0, 0], three_r.at[0, j], (b, j)
                ).wait_recv()
                total = total + r3[j, 0:4].astype(F32)
            a3[0:4] = total.astype(BF16)
        else:
            for u in range(first, first + count):
                total = r2u[u, s].astype(F32)
                for d in range(1, groups):
                    j = along(d)
                    remote(
                        r2u.at[u, 0], r3.at[j, u], three_s.at[u, 0], three_r.at[u, j], (b, j)
                    ).wait_recv()
                    total = total + r3[j, u].astype(F32)
                a3[u] = total.astype(BF16)
        keep_final(g).start()
        gather_one(g).start()

    def start_gather_two(g):
        keep_final(g).wait()
        gather_one(g).wait_recv()
        gather_two(g).start()

    def start_gather_pair(g):
        gather_two(g).wait_recv()
        gather_pair(g).start()

    def reduced(u):
        advance_two(u)
        start_three(u)

    sm[...] = jnp.zeros((SMALL_ROWS, width), F32)

    def send_act(j):
        return pair_copy(X_ACT + j, act.at[j, :, other_half], actp.at[j])

    def send_gp(j):
        return pair_copy(X_GP + j, gp.at[j, :, other_half], gpp.at[j])

    def hidden(i):
        cols = pl.ds(pl.multiple_of(i * width, 128), width)
        w1 = wfc1[:, cols]
        w2 = wfc2[cols, :]
        pre = dot_nn(n2[0:local_len, :], w1) + b1s[pl.ds(i, 1), :]
        phi = 0.5 * (1.0 + lax.erf(pre * ROOT_HALF))
        activated = (pre * phi).astype(BF16)
        act[i] = activated
        send_act(i).start()
        slope = phi + pre * jnp.exp(-0.5 * pre * pre) / ROOT_TWO_PI
        grad_pre = (dact[lax.rem(i, held)] * slope).astype(BF16)
        gp[i] = grad_pre
        send_gp(i).start()
        sm[pl.ds(prompt_count + 7 + i, 1), :] = column_sum(grad_pre.astype(F32))
        acc_out[...] += dot_nn(activated, w2)
        acc_dn[...] += dot_nt(grad_pre, w1)

    def grad_fc2(j):
        send_act(j).wait_recv()
        grads2 = dot_tn(act[j, :, my_half], cot_ref[...]) + dot_tn(actp[j], cotp[...])
        rows = half_w // 4
        for a in range(2):
            for c in range(2):
                for q in range(2):
                    for e in range(2):
                        r = (2 * a + c) * rows + e * blk
                        units[j, a, c, 2 * q + e] = grads2[
                            r : r + blk, q * half_w : (q + 1) * half_w
                        ].astype(BF16)
        stage_one(j).start()

    def grad_fc1(j):
        send_gp(j).wait_recv()
        store_rows(
            4 + j,
            dot_nn(n2t[:, 0:local_len], gp[j, :, my_half]) + dot_nn(n2t[:, local_len:], gpp[j]),
        )
        stage_one(4 + j).start()

    def mlp(i, carry):
        @pl.when(i < chunks)
        def _():
            hidden(i)

        @pl.when(i == 1)
        def _():
            grad_act(held, 0)
            n2t[:, 0:local_len] = n2[0:local_len, :].T
            send_n2.wait_recv()
            n2t[:, local_len:] = n2[local_len:, :].T
            send_cot.wait_recv()

        @pl.when(i > 0)
        def _():
            grad_fc2(i - 1)
            grad_fc1(i - 1)

        return carry

    lax.fori_loop(0, chunks + 1, mlp, 0)

    grad_out = cot_ref[...].astype(F32)
    layer_out_ref[...] = (mid[...] + acc_out[...] + line(b2_ref)).astype(BF16)
    grad_n2 = acc_dn[...]
    scaled2, inverse2 = norm_stats(mid[...])
    sm[prompt_count + 11 : prompt_count + 12, :] = column_sum(grad_out)
    sm[prompt_count + 5 : prompt_count + 6, :] = column_sum(grad_n2 * scaled2)
    sm[prompt_count + 6 : prompt_count + 7, :] = column_sum(grad_n2)
    grad_mid = grad_out + norm_back(grad_n2, scaled2, inverse2, line(g2_ref))
    mid[...] = grad_mid
    branch = grad_mid.astype(BF16)
    gb[...] = branch
    send_gb = pair_copy(X_GB, gb.at[:, other_half], gbp)
    send_gb.start()
    sm[prompt_count + 4 : prompt_count + 5, :] = column_sum(branch.astype(F32))
    grad_att = dot_nt(branch, wout[...]).astype(BF16)
    ga_win[own_rows, :] = grad_att
    product = grad_att.astype(F32) * o32[...]
    for hp in range(head_pairs):
        block = product[:, hp * 128 : (hp + 1) * 128]
        for h in range(2):
            keep = first_head_f32 if h == 0 else jnp.logical_not(first_head_f32)
            total = jnp.sum(jnp.where(keep, block, 0.0), axis=-1, keepdims=True)
            centre[...] = jnp.where(stat_lane == 2 * hp + h, total, centre[...])
    for i in range(2):
        part = slice(i * half_len, (i + 1) * half_len)
        stat[own_at + i, 0:16, :] = lse[part, :].T[0:16, :]
        stat[own_at + i, 16:32, :] = centre[part, :].T[0:16, :]

    def ga_partner(at):
        part = ga_win.at[halves(at, 2)]
        return remote(part, part, ga_s.at[0], ga_r.at[0], (b, partner))

    def stat_partner(at):
        part = stat.at[pl.ds(at, 2)]
        return remote(part, part, st_s.at[0], st_r.at[0], (b, partner))

    def ga_half(i, side, at, to):
        count = half_rows_needed(local_len, HALVES[i][0], HALVES[i][1])
        rows = pl.ds(pl.multiple_of((own_at + side) * half_len, half_len), count)
        return remote(
            ga_win.at[rows],
            ga_win.at[pl.ds(at * half_len, count)],
            ga_s.at[1 + i],
            ga_r.at[1],
            (b, to),
        )

    def stat_half(i, side, at, to):
        return remote(stat.at[own_at + side], stat.at[at], st_s.at[1 + i], st_r.at[1], (b, to))

    def stat_line(row, at, count):
        return jnp.concatenate([stat[at + i, pl.ds(row, 1), :] for i in range(count)], axis=1)

    for_halves(lambda *a: stat_half(*a).start())
    for_halves(lambda *a: ga_half(*a).start())
    stat_partner(own_at).start()
    ga_partner(own_at).start()

    send_att.wait_recv()
    send_gb.wait_recv()
    store_rows(
        8, dot_tn(att[0:local_len, :], gb[:, my_half]) + dot_tn(att[local_len:, :], gbp[...])
    )
    stage_one(8).start()

    prompt_row = lax.broadcasted_iota(jnp.int32, (PROMPT_PAD, 1), 0)
    prompt_bias = jnp.where(prompt_row < prompt_count, 0.0, MASKED_SCORE)
    dqkv[local_len:tok_block, :] = jnp.zeros((PROMPT_PAD + extra, 3 * width), BF16)

    def own_queries(hp, carry):
        lanes = lanes_of(hp)
        q = q_win[own_rows, lanes]
        k = k_win[:, lanes]
        v = v_win[:, lanes]
        g = ga_win[own_rows, lanes]
        parts = []
        d_pk = jnp.zeros((PROMPT_PAD, 2 * HEAD_DIM), F32)
        d_pv = jnp.zeros((PROMPT_PAD, 2 * HEAD_DIM), F32)
        for h in range(2):
            head = 2 * hp + h
            qm = q * head_mask[h]
            gm = g * head_mask[h]
            here = stat_lane == head
            lse_col = jnp.sum(jnp.where(here, lse[...], 0.0), axis=-1, keepdims=True)
            centre_col = jnp.sum(jnp.where(here, centre[...], 0.0), axis=-1, keepdims=True)
            probs = jnp.exp(dot_nt(qm, k) + bias[...] - lse_col)
            grad_scores = (probs * (dot_nt(gm, v) - centre_col)).astype(BF16)
            parts.append(dot_nn(grad_scores, k))
            lse_line = stat_line(head, own_at, 2)
            centre_line = stat_line(16 + head, own_at, 2)
            kp = k_win[window:key_len, lanes]
            vp = v_win[window:key_len, lanes]
            probs_p = jnp.exp(dot_nt(kp, qm) + prompt_bias - lse_line)
            grads_p = (probs_p * (dot_nt(vp, gm) - centre_line)).astype(BF16)
            d_pk = d_pk + dot_nn(grads_p, qm)
            d_pv = d_pv + dot_nn(probs_p.astype(BF16), gm)
        grad_q = jnp.where(first_head_f32, parts[0], parts[1]) * SCALE
        dqkv[0:local_len, lanes] = grad_q.astype(BF16)
        k_lanes = pl.ds(pl.multiple_of(width + hp * 128, 128), 128)
        v_lanes = pl.ds(pl.multiple_of(2 * width + hp * 128, 128), 128)
        dqkv[local_len:p_block, k_lanes] = d_pk.astype(BF16)
        dqkv[local_len:p_block, v_lanes] = d_pv.astype(BF16)

        @pl.when(hp > 1)
        def _():
            advance_one(unit_of(hp - 2))

        return carry

    lax.fori_loop(0, head_pairs, own_queries, 0)
    project_q(tokw[partner_rows, :], partner_rows)
    nbt[0] = nb[0].T
    send_norm.wait_recv()
    send_extra.wait_recv()
    nbt[1] = nb[1].T

    dk, dv = acc_out, acc_dn
    dk[...] = jnp.zeros((local_len, width), F32)
    dv[...] = jnp.zeros((local_len, width), F32)

    def own_keys(at, count):
        cols = halves(at, count)
        mask = bias[:, cols]

        def body(hp, carry):
            lanes = lanes_of(hp)
            k = k_win[own_rows, lanes]
            v = v_win[own_rows, lanes]
            q = q_win[cols, lanes]
            g = ga_win[cols, lanes]
            d_k = dk[:, lanes]
            d_v = dv[:, lanes]
            for h in range(2):
                head = 2 * hp + h
                qm = q * head_mask[h]
                gm = g * head_mask[h]
                lse_line = stat_line(head, at, count)
                centre_line = stat_line(16 + head, at, count)
                probs = jnp.exp(dot_nt(k, qm) + mask - lse_line)
                grad_scores = (probs * (dot_nt(v, gm) - centre_line)).astype(BF16)
                d_k = d_k + dot_nn(grad_scores, qm)
                d_v = d_v + dot_nn(probs.astype(BF16), gm)
            dk[:, lanes] = d_k
            dv[:, lanes] = d_v
            return carry

        lax.fori_loop(0, head_pairs, body, 0)

    def shared_back(i, carry):
        hp = s * x_pairs + i
        lanes = lanes_of(hp)
        q_x = q_win[shared_rows, lanes]
        k_x = k_win[shared_rows, lanes]
        v_x = v_win[shared_rows, lanes]
        g_x = ga_win[shared_rows, lanes]
        k = k_win[:, lanes]
        v = v_win[:, lanes]
        q = q_win[:, lanes]
        g = ga_win[:, lanes]
        product = g_x.astype(F32) * o32_x[:, lanes]
        parts = []
        d_k = jnp.zeros((extra, 2 * HEAD_DIM), F32)
        d_v = jnp.zeros((extra, 2 * HEAD_DIM), F32)
        for h in range(2):
            head = 2 * hp + h
            keep = first_head_f32 if h == 0 else jnp.logical_not(first_head_f32)
            lse_col = jnp.sum(
                jnp.where(x_lane == head, lse_x[...], 0.0), axis=-1, keepdims=True
            )
            centre_col = jnp.sum(jnp.where(keep, product, 0.0), axis=-1, keepdims=True)
            probs = jnp.exp(dot_nt(q_x * head_mask[h], k) + bias_x[...] - lse_col)
            grad_scores = (probs * (dot_nt(g_x * head_mask[h], v) - centre_col)).astype(BF16)
            parts.append(dot_nn(grad_scores, k))
            qm = q * head_mask[h]
            gm = g * head_mask[h]
            lse_line = stat_line(head, 0, 5)
            centre_line = stat_line(16 + head, 0, 5)
            probs = jnp.exp(dot_nt(k_x, qm) + bias_x[:, 0:window] - lse_line)
            grad_scores = (probs * (dot_nt(v_x, gm) - centre_line)).astype(BF16)
            d_k = d_k + dot_nn(grad_scores, qm)
            d_v = d_v + dot_nn(probs.astype(BF16), gm)
        d_q = jnp.where(first_head_f32, parts[0], parts[1]) * SCALE
        for n, part in enumerate((d_q, d_k, d_v)):
            to = pl.ds(pl.multiple_of(n * width + hp * 128, 128), 128)
            dqkv[p_block:tok_block, to] = jnp.where(shared, part, 0.0).astype(BF16)
        return carry

    own_keys(own_at, 2)
    advance_one(2)
    advance_two(0)
    advance_two(4)
    stat_partner(partner_at).wait_recv()
    ga_partner(partner_at).wait_recv()

    for_half_in(lambda *a: stat_half(*a).wait_recv())
    for_half_in(lambda *a: ga_half(*a).wait_recv())

    @pl.when(s < 2)
    def _():
        lax.fori_loop(0, x_pairs, shared_back, 0)

    @pl.when(s == 2)
    def _():
        dqkv[0:extra, 0:width] = jnp.where(
            shared, 0.0, dqkv[0:extra, 0:width].astype(F32)
        ).astype(BF16)

    q_mine = pl.ds(pl.multiple_of(core * half_w, 128), half_w)
    q_other = pl.ds(pl.multiple_of((1 - core) * half_w, 128), half_w)
    send_q = pair_copy(X_Q, dqkv.at[:, q_other], dqp.at[0])
    send_q.start()
    start_three(0)
    start_three(4)
    own_keys(partner_at, 2)
    send_q.wait_recv()
    store_rows(9, dot_nn(nbt[0], dqkv[:, q_mine]) + dot_nn(nbt[1], dqp[0]))
    stage_one(9).start()
    advance_one(6)
    reduced(1)
    reduced(5)
    own_keys(half_at, 1)
    advance_one(3)
    reduced(2)
    advance_one(7)
    reduced(6)

    @pl.when(s == 2)
    def _():
        dk[0:extra, :] = jnp.where(shared, 0.0, dk[0:extra, :])
        dv[0:extra, :] = jnp.where(shared, 0.0, dv[0:extra, :])

    dqkv[0:local_len, width : 2 * width] = dk[...].astype(BF16)
    dqkv[0:local_len, 2 * width :] = dv[...].astype(BF16)
    send_kv = [
        pair_copy(
            X_KV + i,
            dqkv.at[:, pl.ds(pl.multiple_of((1 + i) * width + (1 - core) * half_w, 128), half_w)],
            dqp.at[1 + i],
        )
        for i in range(2)
    ]
    for copy in send_kv:
        copy.start()
    reduced(3)
    reduced(7)
    advance_one(8)

    grad_normed = dot_nt(dqkv[...], wqkv[...])
    grad_x = grad_normed[p_block:tok_block, :]
    e_x[...] = grad_x.astype(BF16)

    def e_back(j, to):
        return remote(e_x, e_in.at[j], ex_s.at[0], ex_r.at[j], (b, to))

    @pl.when(s < 2)
    def _():
        e_back(s, 2).start()

    for i in range(2):
        send_kv[i].wait_recv()
        lane = pl.ds(pl.multiple_of((1 + i) * width + core * half_w, 128), half_w)
        store_rows(
            10 + i,
            dot_nn(nbt[0], dqkv[:, lane]) + dot_nn(nbt[1], dqp[1 + i]),
        )
        stage_one(10 + i).start()

    advance_one(9)
    reduced(8)
    grad_tok = grad_normed[0:local_len, :]
    e_low[...] = grad_tok[0:extra, :]
    grad_pro = grad_normed[local_len : local_len + prompt_count, :]
    scaled1, inverse1 = norm_stats(tokens_ref[...].astype(F32))
    grad_input_ref[...] = (mid[...] + norm_back(grad_tok, scaled1, inverse1, gain1)).astype(BF16)
    p_scaled, p_inverse = norm_stats(prompts_ref[...])
    sm[0:prompt_count, :] = norm_back(grad_pro, p_scaled, p_inverse, gain1)
    sm[prompt_count : prompt_count + 1, :] = (
        column_sum(grad_tok * scaled1)
        + column_sum(grad_pro * p_scaled)
        + column_sum(grad_x * xh_x[...])
    )
    sm[prompt_count + 1 : prompt_count + 2, :] = (
        column_sum(grad_tok) + column_sum(grad_pro) + column_sum(grad_x)
    )
    sm[prompt_count + 2 : prompt_count + 3, :] = column_sum(dqkv[:, :width].astype(F32))
    sm[prompt_count + 3 : prompt_count + 4, :] = column_sum(dqkv[:, 2 * width :].astype(F32))
    send_sm = pair_copy(X_SMALL, sm.at[:, other_half], smp)
    send_sm.start()
    reduced(9)

    quarter = SMALL_ROWS // 4
    send_sm.wait_recv()
    small = sm[:, my_half] + smp[...]
    for a in range(2):
        for c in range(2):
            s0[a, c] = small[(2 * a + c) * quarter : (2 * a + c + 1) * quarter, :]

    small_one = remote(s0.at[1 - h1], rs1, one_s.at[12], one_r.at[12], nb1)
    small_one.start()
    advance_one(10)
    advance_one(11)
    small_one.wait_recv()
    s1b[...] = s0[h1] + rs1[...]
    small_two = remote(s1b.at[1 - h2], rs2, two_s.at[12], two_r.at[12], nb2)
    small_two.start()
    finish_three(0)
    reduced(10)
    reduced(11)
    small_two.wait_recv()
    rs3[s] = s1b[h2] + rs2[...]

    def small_three(d):
        return remote(
            rs3.at[s], rs3.at[s], three_s.at[12, d - 1], three_r.at[12, s], (b, along(d))
        )

    def small_three_recv(j):
        return remote(rs3.at[j], rs3.at[j], three_s.at[12, 0], three_r.at[12, j], (b, j))

    for d in range(1, groups):
        small_three(d).start()
    finish_three(1)
    start_gather_two(0)
    finish_three(2)
    start_gather_two(1)
    start_gather_pair(0)
    finish_three(3)
    start_gather_pair(1)
    for d in range(1, groups):
        small_three_recv(along(d)).wait_recv()
    total = rs3[0]
    for j in range(1, groups):
        total = total + rs3[j]
    s3[...] = total
    small_keep = pltpu.make_async_copy(s3, small_ref.at[core, h1, h2], loc_sem.at[SMALL])
    small_keep.start()
    small_gather = remote(
        s3, small_ref.at[core, h1, h2], ag1_s.at[SMALL], ag1_r.at[SMALL], nb2
    )
    small_gather.start()
    start_gather_two(2)

    @pl.when(s == 2)
    def _():
        for j in range(2):
            e_back(j, j).wait_recv()
        full = e_low[...] + e_in[0].astype(F32) + e_in[1].astype(F32)
        scaled, inverse = norm_stats(tokens_ref[0:extra, :].astype(F32))
        grad_input_ref[0:extra, :] = (
            mid[0:extra, :] + norm_back(full, scaled, inverse, gain1)
        ).astype(BF16)

    start_gather_two(3)
    small_keep.wait()
    small_gather.wait_recv()
    small_gather_two = remote(
        small_ref.at[core, h1], small_ref.at[core, h1], ag2_s.at[SMALL], ag2_r.at[SMALL], nb1
    )
    small_gather_two.start()
    start_gather_pair(2)
    start_gather_pair(3)
    small_gather_two.wait_recv()
    small_pair = pair_copy(X_FINAL + SMALL, small_ref.at[core], small_ref.at[core])
    small_pair.start()

    small_pair.wait()
    for g in range(len(SLOTS)):
        gather_pair(g).wait()
        gather_one(g).wait_send()
        gather_two(g).wait_send()
    for u in range(12):
        drain_three(u)
    small_one.wait_send()
    small_two.wait_send()
    small_gather.wait_send()
    small_gather_two.wait_send()
    for d in range(1, groups):
        small_three(d).wait_send()

    for side in range(2):
        token_partner(side, own_at).wait_send()
    stat_partner(own_at).wait_send()
    ga_partner(own_at).wait_send()
    for_halves(lambda *a: token_half(*a).wait_send())
    for_halves(lambda *a: stat_half(*a).wait_send())
    for_halves(lambda *a: ga_half(*a).wait_send())

    @pl.when(s < 2)
    def _():
        att_back(s).wait_send()
        lse_back(s).wait_send()
        e_back(s, 2).wait_send()

    def drain(u, carry):
        stage_one(u).wait_send()
        stage_two(u).wait_send()
        return carry

    lax.fori_loop(0, 12, drain, 0)

    def drain_mlp(j, carry):
        send_act(j).wait_send()
        send_gp(j).wait_send()
        return carry

    lax.fori_loop(0, chunks, drain_mlp, 0)
    for copy in (send_cot, send_norm, send_extra, send_att, send_n2, send_gb, send_q, *send_kv, send_sm):
        copy.wait_send()


def finish_kernel(
    width,
    prompt_count,
    ff,
    layer_in,
    grad_in,
    final_hbm,
    small_hbm,
    layer_out_ref,
    grad_input_ref,
    gp_ref,
    g1_ref,
    s1_ref,
    wqkv_ref,
    qb_ref,
    vb_ref,
    wout_ref,
    ob_ref,
    g2_ref,
    s2_ref,
    wfc1_ref,
    b1_ref,
    wfc2_ref,
    b2_ref,
    final,
    small_in,
    small,
    layer_buf,
    grad_buf,
    fc2_buf,
    fc1_buf,
    out_buf,
    qkv_buf,
    gp_buf,
    b1_buf,
    b2_buf,
    *rest,
):
    vec_bufs, (in_sem, out_sem) = rest[:7], rest[7:]
    half_w = width // 2
    blk = final_hbm.shape[4]
    small_loads = pltpu.make_async_copy(small_hbm, small_in, in_sem.at[3])
    small_loads.start()
    loads = [
        pltpu.make_async_copy(
            final_hbm.at[:, :, :, pl.ds(4 * g, 4)], final.at[g], in_sem.at[g]
        )
        for g in range(3)
    ]
    loads.append(pltpu.make_async_copy(layer_in, layer_buf, in_sem.at[4]))
    loads.append(pltpu.make_async_copy(grad_in, grad_buf, in_sem.at[5]))
    for load in loads:
        load.start()
    stores = []

    def store(src, dst):
        copy = pltpu.make_async_copy(src, dst, out_sem.at[len(stores)])
        copy.start()
        stores.append(copy)

    quads = [(c, a, e) for c in range(2) for a in range(2) for e in range(2)]
    small_loads.wait()
    quarter = small_in.shape[3]
    for c, a, e in quads:
        r = (2 * a + e) * quarter
        small[r : r + quarter, c * half_w : (c + 1) * half_w] = small_in[c, a, e]
    gp_buf[...] = small[0:prompt_count, :]
    store(gp_buf, gp_ref)
    vectors = (g1_ref, s1_ref, qb_ref, vb_ref, ob_ref, g2_ref, s2_ref)
    for k, (buf, ref) in enumerate(zip(vec_bufs, vectors)):
        buf[...] = small[prompt_count + k : prompt_count + k + 1, :].reshape(width)
        store(buf, ref)
    for k in range(ff // width):
        r = prompt_count + 7 + k
        b1_buf[k * width : (k + 1) * width] = small[r : r + 1, :].reshape(width)
    store(b1_buf, b1_ref)
    r = prompt_count + 7 + ff // width
    b2_buf[...] = small[r : r + 1, :].reshape(width)
    store(b2_buf, b2_ref)
    loads[0].wait()
    for c, a, e in quads:
        for i in range(4):
            q, r = i // 2, i % 2
            row = c * half_w + (2 * a + e) * (half_w // 4) + r * blk
            fc2_buf[row : row + blk, q * half_w : (q + 1) * half_w] = final[0, c, a, e, i].astype(
                F32
            )
    store(fc2_buf, wfc2_ref)
    loads[1].wait()
    for c, a, e in quads:
        rows = slice((2 * a + e) * blk, (2 * a + e + 1) * blk)
        for i in range(4):
            col = i * width + c * half_w
            fc1_buf[rows, col : col + half_w] = final[1, c, a, e, i].astype(F32)
    store(fc1_buf, wfc1_ref)
    loads[2].wait()
    for c, a, e in quads:
        rows = slice((2 * a + e) * blk, (2 * a + e + 1) * blk)
        cols = slice(c * half_w, (c + 1) * half_w)
        out_buf[rows, cols] = final[2, c, a, e, 0].astype(F32)
        for i in range(3):
            col = i * width + c * half_w
            qkv_buf[rows, col : col + half_w] = final[2, c, a, e, 1 + i].astype(F32)
    store(out_buf, wout_ref)
    store(qkv_buf, wqkv_ref)
    loads[3].wait()
    store(layer_buf, layer_out_ref)
    loads[4].wait()
    store(grad_buf, grad_input_ref)
    for copy in stores:
        copy.wait()


def local(
    tokens,
    segments,
    prompts,
    ln1_gain,
    ln1_shift,
    w_qkv,
    q_bias,
    v_bias,
    w_out,
    out_bias,
    ln2_gain,
    ln2_shift,
    w_fc1,
    fc1_bias,
    w_fc2,
    fc2_bias,
    cotangent,
):
    groups = lax.axis_size("seq")
    batch = lax.axis_size("batch")
    row_count, local_len, width = tokens.shape
    ff = w_fc1.shape[1]
    prompt_count = prompts.shape[0]
    assert row_count == 1 and groups == 4 and batch % GROUP == 0 and ff == 4 * width
    check_window(groups, local_len)
    dims = (groups, local_len, width, ff, prompt_count)
    window = 5 * (local_len // 2)
    extra = extra_rows(local_len)
    half_w = width // 2
    blk = width // groups // 4
    tok_block = local_len + PROMPT_PAD + extra
    quarter = SMALL_ROWS // 4

    vmem = pl.BlockSpec(memory_space=pltpu.VMEM)
    hbm = pl.BlockSpec(memory_space=pl.ANY)
    dma = pltpu.SemaphoreType.DMA
    V = pltpu.VMEM
    scratch = [
        V((width, 3 * width), BF16),
        V((width, width), BF16),
        V((width, ff), BF16),
        V((ff, width), BF16),
        V((window, width), BF16),
        V((2, tok_block, width), BF16),
        V((2, width, tok_block), BF16),
        V((window, width), BF16),
        V((window + PROMPT_PAD, width), BF16),
        V((window + PROMPT_PAD, width), BF16),
        V((local_len, window + PROMPT_PAD), F32),
        V((local_len, width), F32),
        V((2 * local_len, width), BF16),
        V((local_len, 128), F32),
        V((local_len, 128), F32),
        V((local_len, width), F32),
        V((2 * local_len, width), BF16),
        V((width, 2 * local_len), BF16),
        V((4, local_len, width), BF16),
        V((4, local_len, width), BF16),
        V((4, local_len, half_w), BF16),
        V((4, local_len, half_w), BF16),
        V((4, width), F32),
        V((local_len, width), F32),
        V((local_len, width), F32),
        V((local_len, width), BF16),
        V((local_len, width), BF16),
        V((local_len, half_w), BF16),
        V((window, width), BF16),
        V((5, 32, local_len // 2), F32),
        V((tok_block, 3 * width), BF16),
        V((3, tok_block, half_w), BF16),
        V((12, 2, 2, 4, blk, half_w), BF16),
        V((12, 2, 4, blk, half_w), BF16),
        V((12, 4, blk, half_w), BF16),
        V((groups, 12, blk, half_w), BF16),
        V((12, blk, half_w), BF16),
        V((SMALL_ROWS, width), F32),
        V((SMALL_ROWS, half_w), F32),
        V((2, 2, quarter, half_w), F32),
        V((2, quarter, half_w), F32),
        V((2, quarter, half_w), F32),
        V((quarter, half_w), F32),
        V((groups, quarter, half_w), F32),
        V((quarter, half_w), F32),
        V((extra, window + PROMPT_PAD), F32),
        V((extra, width), F32),
        V((extra, width), BF16),
        V((extra, 128), F32),
        V((extra, width), BF16),
        V((2, extra, 128), F32),
        V((extra, width), F32),
        V((extra, width), BF16),
        V((2, extra, width), BF16),
        V((extra, width), F32),
        V((3, local_len, width), F32),
        dma((4,)),
        dma((5,)),
        dma((3,)),
        dma((X_COUNT,)),
        dma((X_COUNT,)),
        dma((4,)),
        dma((2,)),
        dma((4,)),
        dma((2,)),
        dma((13,)),
        dma((13,)),
        dma((13,)),
        dma((13,)),
        dma((13, 3)),
        dma((13, groups)),
        dma((5,)),
        dma((5,)),
        dma((5,)),
        dma((5,)),
        dma((5,)),
        dma((2,)),
        dma((2, 2)),
        dma((1,)),
        dma((2,)),
    ]
    specs = [vmem] * 17
    for index in (5, 8, 12, 14):
        specs[index] = hbm
    layer_out, grad_input, final, small = pl.pallas_call(
        functools.partial(layer_kernel, dims),
        out_shape=(
            jax.ShapeDtypeStruct((local_len, width), BF16),
            jax.ShapeDtypeStruct((local_len, width), BF16),
            jax.ShapeDtypeStruct((2, 2, 2, 12, blk, half_w), BF16),
            jax.ShapeDtypeStruct((2, 2, 2, quarter, half_w), F32),
        ),
        in_specs=specs,
        out_specs=(vmem, vmem, hbm, hbm),
        scratch_shapes=scratch,
        compiler_params=pltpu.CompilerParams(
            collective_id=0, has_side_effects=True, vmem_limit_bytes=67043328
        ),
        name="layer",
    )(
        tokens.reshape(local_len, width),
        segments,
        prompts,
        ln1_gain,
        ln1_shift,
        w_qkv,
        q_bias,
        v_bias,
        w_out,
        out_bias,
        ln2_gain,
        ln2_shift,
        w_fc1,
        fc1_bias,
        w_fc2,
        fc2_bias,
        cotangent.reshape(local_len, width),
    )
    if batch > GROUP:
        rings = [list(range(k, batch, GROUP)) for k in range(GROUP)]
        final, small = lax.psum((final, small), "batch", axis_index_groups=rings)
    rows_z = width // groups

    def flat(n):
        return jax.ShapeDtypeStruct((n,), F32)

    outs = pl.pallas_call(
        functools.partial(finish_kernel, width, prompt_count, ff),
        out_shape=(
            jax.ShapeDtypeStruct((local_len, width), BF16),
            jax.ShapeDtypeStruct((local_len, width), BF16),
            jax.ShapeDtypeStruct((prompt_count, width), F32),
            flat(width),
            flat(width),
            jax.ShapeDtypeStruct((rows_z, 3 * width), F32),
            flat(width),
            flat(width),
            jax.ShapeDtypeStruct((rows_z, width), F32),
            flat(width),
            flat(width),
            flat(width),
            jax.ShapeDtypeStruct((rows_z, ff), F32),
            flat(ff),
            jax.ShapeDtypeStruct((ff // groups, width), F32),
            flat(width),
        ),
        in_specs=[pl.BlockSpec(memory_space=pltpu.HBM)] * 4,
        out_specs=(hbm,) * 16,
        scratch_shapes=[
            V((3, 2, 2, 2, 4, blk, half_w), BF16),
            V((2, 2, 2, quarter, half_w), F32),
            V((SMALL_ROWS, width), F32),
            V((local_len, width), BF16),
            V((local_len, width), BF16),
            V((ff // groups, width), F32),
            V((rows_z, ff), F32),
            V((rows_z, width), F32),
            V((rows_z, 3 * width), F32),
            V((prompt_count, width), F32),
            V((ff,), F32),
            V((width,), F32),
            *[V((width,), F32) for _ in range(7)],
            dma((6,)),
            dma((16,)),
        ],
        compiler_params=pltpu.CompilerParams(vmem_limit_bytes=67043328),
        name="finish",
    )(layer_out, grad_input, final, small)
    return tuple(o.reshape((1, local_len, width)) if i < 2 else o for i, o in enumerate(outs))


def solution(mesh):
    tok = P("batch", "seq", None)
    in_specs = (tok, P("batch", "seq")) + (P(),) * 14 + (tok,)
    out_specs = (
        tok,
        tok,
        P(),
        P(),
        P(),
        P("seq", None),
        P(),
        P(),
        P("seq", None),
        P(),
        P(),
        P(),
        P("seq", None),
        P(),
        P("seq", None),
        P(),
    )
    return jax.shard_map(local, mesh=mesh, in_specs=in_specs, out_specs=out_specs, check_vma=False)
```

```python
import functools

import jax
import jax.numpy as jnp
from jax import lax
from jax.experimental import pallas as pl
from jax.experimental.pallas import tpu as pltpu
from jax.sharding import PartitionSpec as P

HEAD_DIM = 64
IMAGE_TOKENS = (101, 197, 577)
EPSILON = 1e-06
MASKED_SCORE = -1e30
ROOT_HALF = 0.7071067811865476
ROOT_TWO_PI = 2.5066282746310002
SCALE = HEAD_DIM ** (-0.5)
GROUP = 8
PROMPT_PAD = 64
SMALL_ROWS = 64
F32 = jnp.float32
BF16 = jnp.bfloat16
MESH = pl.DeviceIdType.MESH


def dot_nn(a, b):
    return lax.dot_general(a, b, (((1,), (0,)), ((), ())), preferred_element_type=F32)


def dot_nt(a, b):
    return lax.dot_general(a, b, (((1,), (1,)), ((), ())), preferred_element_type=F32)


def dot_tn(a, b):
    return lax.dot_general(a, b, (((0,), (0,)), ((), ())), preferred_element_type=F32)


def check_window(groups, local_len):
    row_len, half_len = groups * local_len, local_len // 2
    cut = 2 * local_len
    for size in IMAGE_TOKENS:
        for first in range(0, row_len, size):
            last = min(first + size, row_len) - 1
            for shard in range(first // local_len, last // local_len + 1):
                start = 0 if shard < 2 else 3 * half_len
                inside = start <= first and last < start + 5 * half_len
                if shard == 3:
                    inside = inside and first >= cut
                given = size == IMAGE_TOKENS[-1] and shard == 2 and first == 0
                assert inside or given
                assert not given or last < cut + extra_rows(local_len)


def extra_rows(local_len):
    return -(-(IMAGE_TOKENS[-1] - 2 * local_len) // 16) * 16


def half_rows_needed(local_len, src, dst):
    if src < dst:
        return local_len // 2
    top = 0
    for size in IMAGE_TOKENS:
        end = ((dst + 1) * local_len - 1) // size * size + size
        top = max(top, end - 2 * local_len)
    return min(-(-top // 16) * 16, local_len // 2)


def norm_stats(values):
    centred = values - jnp.mean(values, axis=-1, keepdims=True)
    inverse = lax.rsqrt(jnp.mean(centred * centred, axis=-1, keepdims=True) + EPSILON)
    return centred * inverse, inverse


def norm_back(grad_out, scaled, inverse, gain):
    inner = grad_out * gain
    return inverse * (
        inner
        - jnp.mean(inner, axis=-1, keepdims=True)
        - scaled * jnp.mean(inner * scaled, axis=-1, keepdims=True)
    )


def line(ref):
    return ref[...].reshape(1, -1)


def column_sum(values):
    return jnp.sum(values, axis=0, keepdims=True)


X_COT, X_N2, X_ATT, X_NORM, X_GB, X_Q, X_KV, X_SMALL, X_FINAL, X_ACT, X_GP, X_EXTRA = 0, 1, 2, 3, 4, 5, 6, 8, 9, 14, 18, 22
X_COUNT = 23
HALVES = ((2, 0, 0), (2, 1, 0), (1, 2, 1))
SLOTS = ((0, 4), (4, 4), (8, 2), (10, 2))
SMALL = 4


def layer_kernel(
    dims,
    tokens_ref,
    seg_ref,
    prompts_ref,
    g1_ref,
    s1_ref,
    wqkv_hbm,
    qb_ref,
    vb_ref,
    wout_hbm,
    ob_ref,
    g2_ref,
    s2_ref,
    wfc1_hbm,
    b1_ref,
    wfc2_hbm,
    b2_ref,
    cot_ref,
    layer_out_ref,
    grad_input_ref,
    final_ref,
    small_ref,
    wqkv,
    wout,
    wfc1,
    wfc2,
    tokw,
    nb,
    nbt,
    q_win,
    k_win,
    v_win,
    bias,
    o32,
    att,
    lse,
    centre,
    mid,
    n2,
    n2t,
    act,
    gp,
    actp,
    gpp,
    b1s,
    acc_out,
    acc_dn,
    cotp,
    gb,
    gbp,
    ga_win,
    stat,
    dqkv,
    dqp,
    units,
    r1,
    r2u,
    r3,
    a3,
    sm,
    smp,
    s0,
    rs1,
    s1b,
    rs2,
    rs3,
    s3,
    bias_x,
    o32_x,
    att_x,
    lse_x,
    att_in,
    lse_in,
    xh_x,
    e_x,
    e_in,
    e_low,
    dact,
    wsem,
    tok_s,
    tok_r,
    pair_s,
    pair_r,
    ga_s,
    ga_r,
    st_s,
    st_r,
    one_s,
    one_r,
    two_s,
    two_r,
    three_s,
    three_r,
    loc_sem,
    ag1_s,
    ag1_r,
    ag2_s,
    ag2_r,
    ax_s,
    ax_r,
    ex_s,
    ex_r,
):
    groups, local_len, width, ff, prompt_count = dims
    half_len = local_len // 2
    window = 5 * half_len
    cut = 2 * local_len
    extra = extra_rows(local_len)
    head_pairs = width // (2 * HEAD_DIM)
    chunks = ff // width
    half_w = width // 2
    key_len = window + PROMPT_PAD
    zrows = width // groups

    b = lax.axis_index("batch")
    s = lax.axis_index("seq")
    base = (b // GROUP) * GROUP
    core = lax.rem(b, 2)
    xb = lax.rem(b // 2, 2)
    yb = lax.rem(b // 4, 2)
    h1 = xb * (1 - core) + yb * core
    h2 = yb * (1 - core) + xb * core

    def place(x, y, c):
        return base + y * 4 + x * 2 + c

    nb1 = (place(xb + (1 - core) * (1 - 2 * xb), yb + core * (1 - 2 * yb), core), s)
    nb2 = (place(xb + core * (1 - 2 * xb), yb + (1 - core) * (1 - 2 * yb), core), s)
    pair = (place(xb, yb, 1 - core), s)

    def along(d):
        return lax.rem(s + d, groups)

    first_half = jnp.where(s < 2, 0, 3)
    start = first_half * half_len
    partner = s + 1 - 2 * lax.rem(s, 2)
    own_at = 2 * s - first_half
    partner_at = 2 * partner - first_half
    half_at = jnp.where(s < 2, 4, 0)

    def halves(at, count):
        return pl.ds(pl.multiple_of(at * half_len, half_len), count * half_len)

    own_rows = halves(own_at, 2)
    partner_rows = halves(partner_at, 2)
    half_rows = halves(half_at, 1)
    shared_rows = pl.ds(4 * half_len, extra)

    def remote(src, dst, send, recv, to):
        return pltpu.make_async_remote_copy(
            src_ref=src, dst_ref=dst, send_sem=send, recv_sem=recv, device_id=to, device_id_type=MESH
        )

    barrier = pltpu.get_barrier_semaphore()
    for peer in (pair, nb1, nb2):
        pl.semaphore_signal(barrier, inc=1, device_id=peer, device_id_type=MESH)
    for d in range(1, groups):
        pl.semaphore_signal(barrier, inc=1, device_id=(b, along(d)), device_id_type=MESH)

    loads = [
        pltpu.make_async_copy(wqkv_hbm, wqkv, wsem.at[0]),
        pltpu.make_async_copy(wout_hbm, wout, wsem.at[1]),
        pltpu.make_async_copy(wfc1_hbm, wfc1, wsem.at[2]),
        pltpu.make_async_copy(wfc2_hbm, wfc2, wsem.at[3]),
    ]
    loads[0].start()
    pl.semaphore_wait(barrier, 2 + groups)

    def token_partner(side, at):
        part = tokens_ref.at[pl.ds(side * half_len, half_len)]
        return remote(
            part, tokw.at[halves(at + side, 1)], tok_s.at[side], tok_r.at[side], (b, partner)
        )

    def token_half(i, side, at, to):
        count = half_rows_needed(local_len, HALVES[i][0], HALVES[i][1])
        return remote(
            tokens_ref.at[pl.ds(side * half_len, count)],
            tokw.at[pl.ds(at * half_len, count)],
            tok_s.at[2 + i],
            tok_r.at[2],
            (b, to),
        )

    def for_halves(action):
        for i, (src, dst, side) in enumerate(HALVES):

            @pl.when(s == src)
            def _(i=i, dst=dst, side=side):
                action(i, side, 4 if dst < 2 else 0, dst)

    def for_half_in(action):
        for i, (src, dst, side) in enumerate(HALVES):

            @pl.when(s == dst)
            def _(i=i, src=src, side=side, dst=dst):
                action(i, side, 4 if dst < 2 else 0, src)

    for_halves(lambda *a: token_half(*a).start())
    for side in range(2):
        token_partner(side, own_at).start()

    for load in loads[1:]:
        load.start()

    def pair_copy(index, src, dst):
        return remote(src, dst, pair_s.at[index], pair_r.at[index], pair)

    my_half = pl.ds(pl.multiple_of(core * half_w, 128), half_w)
    other_half = pl.ds(pl.multiple_of((1 - core) * half_w, 128), half_w)

    send_cot = pair_copy(X_COT, cot_ref, cotp)
    send_cot.start()

    gain1 = line(g1_ref)
    shift1 = line(s1_ref)
    for i in range(chunks):
        b1s[i : i + 1, :] = b1_ref[i * width : (i + 1) * width].reshape(1, width)

    last = s * local_len + local_len - 1
    seg_last = seg_ref[:, local_len - 1 : local_len].astype(F32)
    inv_n = jnp.full((1, 1), 1.0 / IMAGE_TOKENS[-1], F32)
    is_long = jnp.ones((1, 1), F32)
    for size in IMAGE_TOKENS[:-1]:
        here = seg_last == (last // size).astype(F32)
        inv_n = jnp.where(here, 1.0 / size, inv_n)
        is_long = jnp.where(here, 0.0, is_long)
    k_pos = lax.broadcasted_iota(jnp.int32, (1, key_len), 1)
    k_open = jnp.where(k_pos < window, 0.0, jnp.where(k_pos < window + prompt_count, 1.0, 0.0))
    k_id = jnp.floor(((k_pos + start).astype(F32) + 0.5) * inv_n)
    k_id = jnp.where(k_pos < window, k_id, -1.0)

    def mask_of(q_pos):
        q_id = jnp.floor((q_pos.astype(F32) + 0.5) * inv_n)
        return jnp.where(q_id == k_id, 0.0, MASKED_SCORE * (1.0 - k_open))

    bias[...] = mask_of(lax.broadcasted_iota(jnp.int32, (local_len, 1), 0) + s * local_len)
    x_row = lax.broadcasted_iota(jnp.int32, (extra, 1), 0)
    bias_x[...] = mask_of(x_row + cut)
    shared = jnp.where(x_row + cut < IMAGE_TOKENS[-1], is_long, 0.0) > 0.5

    def project_q(normed, rows):
        q = dot_nn(normed, wqkv[:, :width]) + line(qb_ref)
        q_win[rows, :] = (q.astype(BF16).astype(F32) * SCALE).astype(BF16)

    def project(normed, rows):
        k_win[rows, :] = dot_nn(normed, wqkv[:, width : 2 * width]).astype(BF16)
        v_win[rows, :] = (dot_nn(normed, wqkv[:, 2 * width :]) + line(vb_ref)).astype(BF16)

    p_scaled, p_inverse = norm_stats(prompts_ref[...])
    p_block = local_len + PROMPT_PAD
    tok_block = p_block + extra
    nb[0, local_len:p_block, :] = jnp.zeros((PROMPT_PAD, width), BF16)
    nb[0, local_len : local_len + prompt_count, :] = (p_scaled * gain1 + shift1).astype(BF16)
    scaled1, _ = norm_stats(tokens_ref[...].astype(F32))
    nb[0, 0:local_len, :] = (scaled1 * gain1 + shift1).astype(BF16)
    send_norm = pair_copy(X_NORM, nb.at[0, pl.ds(0, p_block)], nb.at[1, pl.ds(0, p_block)])
    send_norm.start()

    tail = half_rows_needed(local_len, 2, 0)
    tail_rows = pl.ds(4 * half_len + tail, half_len - tail)

    @pl.when(s == 0)
    def _():
        tokw[tail_rows, :] = jnp.zeros((half_len - tail, width), BF16)
        ga_win[tail_rows, :] = jnp.zeros((half_len - tail, width), BF16)

    tail_one = half_rows_needed(local_len, 2, 1)
    tail_one_rows = pl.ds(4 * half_len + tail_one, half_len - tail_one)

    @pl.when(s == 1)
    def _():
        tokw[tail_one_rows, :] = jnp.zeros((half_len - tail_one, width), BF16)
        ga_win[tail_one_rows, :] = jnp.zeros((half_len - tail_one, width), BF16)

    loads[0].wait()
    project_q(nb[0, 0:local_len, :], own_rows)
    project(nb[0, 0:local_len, :], own_rows)
    p_low = nb[0, local_len:p_block, :]
    k_win[window:key_len, :] = dot_nn(p_low, wqkv[:, width : 2 * width]).astype(BF16)
    v_win[window:key_len, :] = (dot_nn(p_low, wqkv[:, 2 * width :]) + line(vb_ref)).astype(BF16)

    def normed_tokens(rows):
        scaled, _ = norm_stats(tokw[rows, :].astype(F32))
        return (scaled * gain1 + shift1).astype(BF16)

    loads[3].wait()

    held = chunks - 1

    def grad_act(i, carry):
        rows = pl.ds(pl.multiple_of(i * width, 128), width)
        dact[lax.rem(i, held)] = dot_nt(cot_ref[...], wfc2[rows, :])
        return carry

    lax.fori_loop(0, held, grad_act, 0)

    def partner_piece(side):
        token_partner(side, partner_at).wait_recv()
        rows = halves(partner_at + side, 1)
        normed = normed_tokens(rows)
        tokw[rows, :] = normed
        project(normed, rows)

    partner_piece(0)
    for_half_in(lambda *a: token_half(*a).wait_recv())

    @pl.when(s < groups - 1)
    def _():
        normed = normed_tokens(half_rows)
        project_q(normed, half_rows)
        project(normed, half_rows)

    partner_piece(1)

    @pl.when(s == groups - 1)
    def _():
        empty = jnp.zeros((half_len, width), BF16)
        q_win[0:half_len, :] = empty
        k_win[0:half_len, :] = empty
        v_win[0:half_len, :] = empty
        ga_win[0:half_len, :] = empty
        stat[0] = jnp.zeros((32, half_len), F32)

    @pl.when(s < 2)
    def _():
        scaled, _ = norm_stats(tokw[shared_rows, :].astype(F32))
        xh_x[...] = scaled
        nb[0, p_block:tok_block, :] = (scaled * gain1 + shift1).astype(BF16)

    @pl.when(s >= 2)
    def _():
        xh_x[...] = jnp.zeros((extra, width), F32)
        nb[0, p_block:tok_block, :] = jnp.zeros((extra, width), BF16)

    send_extra = pair_copy(
        X_EXTRA, nb.at[0, pl.ds(p_block, extra)], nb.at[1, pl.ds(p_block, extra)]
    )
    send_extra.start()

    pair_lane = lax.broadcasted_iota(jnp.int32, (1, 2 * HEAD_DIM), 1)
    first_head = jnp.where(pair_lane < HEAD_DIM, 1.0, 0.0)
    head_mask = (first_head.astype(BF16), (1.0 - first_head).astype(BF16))
    first_head_f32 = pair_lane < HEAD_DIM
    stat_lane = lax.broadcasted_iota(jnp.int32, (local_len, 128), 1)

    def lanes_of(hp):
        return pl.ds(pl.multiple_of(hp * 2 * HEAD_DIM, 128), 2 * HEAD_DIM)

    lse[...] = jnp.zeros((local_len, 128), F32)
    centre[...] = jnp.zeros((local_len, 128), F32)

    def softmax_heads(q, lanes, mask):
        k = k_win[:, lanes]
        v = v_win[:, lanes]
        outs, logs = [], []
        for h in range(2):
            scores = dot_nt(q * head_mask[h], k) + mask[...]
            highest = jnp.max(scores, axis=-1, keepdims=True)
            weights = jnp.exp(scores - highest)
            total = jnp.sum(weights, axis=-1, keepdims=True)
            outs.append(dot_nn(weights.astype(BF16), v) / total)
            logs.append(highest + jnp.log(total))
        return jnp.where(first_head_f32, outs[0], outs[1]), logs

    x_pairs = head_pairs // 2
    x_lane = lax.broadcasted_iota(jnp.int32, (extra, 128), 1)

    def x_lanes(j):
        return pl.ds(pl.multiple_of(j * half_w, 128), half_w)

    def att_back(j):
        return remote(
            att_x.at[:, x_lanes(j)], att_in.at[:, x_lanes(j)], ax_s.at[0], ax_r.at[0, j], (b, 2)
        )

    def lse_back(j):
        return remote(lse_x, lse_in.at[j], ax_s.at[1], ax_r.at[1, j], (b, 2))

    @pl.when(s < 2)
    def _():
        lse_x[...] = jnp.zeros((extra, 128), F32)

        def attend_shared(i, carry):
            hp = s * x_pairs + i
            lanes = lanes_of(hp)
            combined, logs = softmax_heads(q_win[shared_rows, lanes], lanes, bias_x)
            o32_x[:, lanes] = combined
            att_x[:, lanes] = combined.astype(BF16)
            for h in range(2):
                lse_x[...] = jnp.where(x_lane == 2 * hp + h, logs[h], lse_x[...])
            return carry

        lax.fori_loop(0, x_pairs, attend_shared, 0)
        att_back(s).start()
        lse_back(s).start()

    def attend(hp, carry):
        lanes = lanes_of(hp)
        combined, logs = softmax_heads(q_win[own_rows, lanes], lanes, bias)
        o32[:, lanes] = combined
        att[0:local_len, lanes] = combined.astype(BF16)
        for h in range(2):
            lse[...] = jnp.where(stat_lane == 2 * hp + h, logs[h], lse[...])
        return carry

    lax.fori_loop(0, head_pairs, attend, 0)

    @pl.when(s == 2)
    def _():
        for j in range(2):
            remote(
                att_x.at[:, x_lanes(j)], att_in.at[:, x_lanes(j)], ax_s.at[0], ax_r.at[0, j], (b, j)
            ).wait_recv()
            remote(lse_x, lse_in.at[j], ax_s.at[1], ax_r.at[1, j], (b, j)).wait_recv()
        merged = jnp.where(shared, att_in[...].astype(F32), o32[0:extra, :])
        o32[0:extra, :] = merged
        att[0:extra, :] = merged.astype(BF16)
        lse[0:extra, :] = jnp.where(shared, lse_in[0] + lse_in[1], lse[0:extra, :])

    own = pl.ds(0, local_len)
    theirs = pl.ds(local_len, local_len)
    send_att = pair_copy(X_ATT, att.at[own], att.at[theirs])
    send_att.start()

    loads[1].wait()
    mid[...] = (
        tokens_ref[...].astype(F32) + dot_nn(att[0:local_len, :], wout[...]) + line(ob_ref)
    )
    scaled2, _ = norm_stats(mid[...])
    n2[0:local_len, :] = (scaled2 * line(g2_ref) + line(s2_ref)).astype(BF16)
    send_n2 = pair_copy(X_N2, n2.at[own], n2.at[theirs])
    send_n2.start()
    acc_out[...] = jnp.zeros((local_len, width), F32)
    acc_dn[...] = jnp.zeros((local_len, width), F32)
    loads[2].wait()

    blk = zrows // 4

    def unit_of(p):
        return p // 2 + 4 * lax.rem(p, 2)

    def store_rows(u, grads):
        for z in range(groups):
            for a in range(2):
                for c in range(2):
                    r = z * zrows + (2 * a + c) * blk
                    units[u, a, c, z] = grads[r : r + blk, :].astype(BF16)

    def stage_one(u):
        return remote(units.at[u, 1 - h1], r1.at[u], one_s.at[u], one_r.at[u], nb1)

    def stage_two(u):
        return remote(units.at[u, h1, 1 - h2], r2u.at[u], two_s.at[u], two_r.at[u], nb2)

    def advance_one(u):
        stage_one(u).wait_recv()
        units[u, h1] = (units[u, h1].astype(F32) + r1[u].astype(F32)).astype(BF16)
        stage_two(u).start()

    def advance_two(u):
        stage_two(u).wait_recv()
        r2u[u] = (units[u, h1, h2].astype(F32) + r2u[u].astype(F32)).astype(BF16)

    def stage_three_fc2(u):
        return remote(
            r2u.at[u], r3.at[s, pl.ds(0, 4)], three_s.at[u, 0], three_r.at[0, s], (b, u)
        )

    def stage_three(u, d):
        t = along(d)
        return remote(r2u.at[u, t], r3.at[s, u], three_s.at[u, d - 1], three_r.at[u, s], (b, t))

    def start_three(u):
        if u < 4:

            @pl.when(s != u)
            def _():
                stage_three_fc2(u).start()

        else:
            for d in range(1, groups):
                stage_three(u, d).start()

    def drain_three(u):
        if u < 4:

            @pl.when(s != u)
            def _():
                stage_three_fc2(u).wait_send()

        else:
            for d in range(1, groups):
                stage_three(u, d).wait_send()

    def slots(g):
        return pl.ds(*SLOTS[g])

    def keep_final(g):
        return pltpu.make_async_copy(
            a3.at[slots(g)], final_ref.at[core, h1, h2, slots(g)], loc_sem.at[g]
        )

    def gather_one(g):
        return remote(
            a3.at[slots(g)],
            final_ref.at[core, h1, h2, slots(g)],
            ag1_s.at[g],
            ag1_r.at[g],
            nb2,
        )

    def gather_two(g):
        ref = final_ref.at[core, h1, :, slots(g)]
        return remote(ref, ref, ag2_s.at[g], ag2_r.at[g], nb1)

    def gather_pair(g):
        ref = final_ref.at[core, :, :, slots(g)]
        return pair_copy(X_FINAL + g, ref, ref)

    def finish_three(g):
        first, count = SLOTS[g]
        if g == 0:
            total = r2u[s].astype(F32)
            for d in range(1, groups):
                j = along(d)
                remote(
                    r2u.at[0], r3.at[j, pl.ds(0, 4)], three_s.at[0, 0], three_r.at[0, j], (b, j)
                ).wait_recv()
                total = total + r3[j, 0:4].astype(F32)
            a3[0:4] = total.astype(BF16)
        else:
            for u in range(first, first + count):
                total = r2u[u, s].astype(F32)
                for d in range(1, groups):
                    j = along(d)
                    remote(
                        r2u.at[u, 0], r3.at[j, u], three_s.at[u, 0], three_r.at[u, j], (b, j)
                    ).wait_recv()
                    total = total + r3[j, u].astype(F32)
                a3[u] = total.astype(BF16)
        keep_final(g).start()
        gather_one(g).start()

    def start_gather_two(g):
        keep_final(g).wait()
        gather_one(g).wait_recv()
        gather_two(g).start()

    def start_gather_pair(g):
        gather_two(g).wait_recv()
        gather_pair(g).start()

    def reduced(u):
        advance_two(u)
        start_three(u)

    sm[...] = jnp.zeros((SMALL_ROWS, width), F32)

    def send_act(j):
        return pair_copy(X_ACT + j, act.at[j, :, other_half], actp.at[j])

    def send_gp(j):
        return pair_copy(X_GP + j, gp.at[j, :, other_half], gpp.at[j])

    def hidden(i):
        cols = pl.ds(pl.multiple_of(i * width, 128), width)
        w1 = wfc1[:, cols]
        w2 = wfc2[cols, :]
        pre = dot_nn(n2[0:local_len, :], w1) + b1s[pl.ds(i, 1), :]
        phi = 0.5 * (1.0 + lax.erf(pre * ROOT_HALF))
        activated = (pre * phi).astype(BF16)
        act[i] = activated
        send_act(i).start()
        slope = phi + pre * jnp.exp(-0.5 * pre * pre) / ROOT_TWO_PI
        grad_pre = (dact[lax.rem(i, held)] * slope).astype(BF16)
        gp[i] = grad_pre
        send_gp(i).start()
        sm[pl.ds(prompt_count + 7 + i, 1), :] = column_sum(grad_pre.astype(F32))
        acc_out[...] += dot_nn(activated, w2)
        acc_dn[...] += dot_nt(grad_pre, w1)

    def grad_fc2(j):
        send_act(j).wait_recv()
        grads2 = dot_tn(act[j, :, my_half], cot_ref[...]) + dot_tn(actp[j], cotp[...])
        rows = half_w // 4
        for a in range(2):
            for c in range(2):
                for q in range(2):
                    for e in range(2):
                        r = (2 * a + c) * rows + e * blk
                        units[j, a, c, 2 * q + e] = grads2[
                            r : r + blk, q * half_w : (q + 1) * half_w
                        ].astype(BF16)
        stage_one(j).start()

    def grad_fc1(j):
        send_gp(j).wait_recv()
        store_rows(
            4 + j,
            dot_nn(n2t[:, 0:local_len], gp[j, :, my_half]) + dot_nn(n2t[:, local_len:], gpp[j]),
        )
        stage_one(4 + j).start()

    def mlp(i, carry):
        @pl.when(i < chunks)
        def _():
            hidden(i)

        @pl.when(i == 1)
        def _():
            grad_act(held, 0)
            n2t[:, 0:local_len] = n2[0:local_len, :].T
            send_n2.wait_recv()
            n2t[:, local_len:] = n2[local_len:, :].T
            send_cot.wait_recv()

        @pl.when(i > 0)
        def _():
            grad_fc2(i - 1)
            grad_fc1(i - 1)

        return carry

    lax.fori_loop(0, chunks + 1, mlp, 0)

    grad_out = cot_ref[...].astype(F32)
    layer_out_ref[...] = (mid[...] + acc_out[...] + line(b2_ref)).astype(BF16)
    grad_n2 = acc_dn[...]
    scaled2, inverse2 = norm_stats(mid[...])
    sm[prompt_count + 11 : prompt_count + 12, :] = column_sum(grad_out)
    sm[prompt_count + 5 : prompt_count + 6, :] = column_sum(grad_n2 * scaled2)
    sm[prompt_count + 6 : prompt_count + 7, :] = column_sum(grad_n2)
    grad_mid = grad_out + norm_back(grad_n2, scaled2, inverse2, line(g2_ref))
    mid[...] = grad_mid
    branch = grad_mid.astype(BF16)
    gb[...] = branch
    send_gb = pair_copy(X_GB, gb.at[:, other_half], gbp)
    send_gb.start()
    sm[prompt_count + 4 : prompt_count + 5, :] = column_sum(branch.astype(F32))
    grad_att = dot_nt(branch, wout[...]).astype(BF16)
    ga_win[own_rows, :] = grad_att
    product = grad_att.astype(F32) * o32[...]
    for hp in range(head_pairs):
        block = product[:, hp * 128 : (hp + 1) * 128]
        for h in range(2):
            keep = first_head_f32 if h == 0 else jnp.logical_not(first_head_f32)
            total = jnp.sum(jnp.where(keep, block, 0.0), axis=-1, keepdims=True)
            centre[...] = jnp.where(stat_lane == 2 * hp + h, total, centre[...])
    for i in range(2):
        part = slice(i * half_len, (i + 1) * half_len)
        stat[own_at + i, 0:16, :] = lse[part, :].T[0:16, :]
        stat[own_at + i, 16:32, :] = centre[part, :].T[0:16, :]

    def ga_partner(at):
        part = ga_win.at[halves(at, 2)]
        return remote(part, part, ga_s.at[0], ga_r.at[0], (b, partner))

    def stat_partner(at):
        part = stat.at[pl.ds(at, 2)]
        return remote(part, part, st_s.at[0], st_r.at[0], (b, partner))

    def ga_half(i, side, at, to):
        count = half_rows_needed(local_len, HALVES[i][0], HALVES[i][1])
        rows = pl.ds(pl.multiple_of((own_at + side) * half_len, half_len), count)
        return remote(
            ga_win.at[rows],
            ga_win.at[pl.ds(at * half_len, count)],
            ga_s.at[1 + i],
            ga_r.at[1],
            (b, to),
        )

    def stat_half(i, side, at, to):
        return remote(stat.at[own_at + side], stat.at[at], st_s.at[1 + i], st_r.at[1], (b, to))

    def stat_line(row, at, count):
        return jnp.concatenate([stat[at + i, pl.ds(row, 1), :] for i in range(count)], axis=1)

    for_halves(lambda *a: stat_half(*a).start())
    for_halves(lambda *a: ga_half(*a).start())
    stat_partner(own_at).start()
    ga_partner(own_at).start()

    send_att.wait_recv()
    send_gb.wait_recv()
    store_rows(
        8, dot_tn(att[0:local_len, :], gb[:, my_half]) + dot_tn(att[local_len:, :], gbp[...])
    )
    stage_one(8).start()

    prompt_row = lax.broadcasted_iota(jnp.int32, (PROMPT_PAD, 1), 0)
    prompt_bias = jnp.where(prompt_row < prompt_count, 0.0, MASKED_SCORE)
    dqkv[local_len:tok_block, :] = jnp.zeros((PROMPT_PAD + extra, 3 * width), BF16)

    def own_queries(hp, carry):
        lanes = lanes_of(hp)
        q = q_win[own_rows, lanes]
        k = k_win[:, lanes]
        v = v_win[:, lanes]
        g = ga_win[own_rows, lanes]
        parts = []
        d_pk = jnp.zeros((PROMPT_PAD, 2 * HEAD_DIM), F32)
        d_pv = jnp.zeros((PROMPT_PAD, 2 * HEAD_DIM), F32)
        for h in range(2):
            head = 2 * hp + h
            qm = q * head_mask[h]
            gm = g * head_mask[h]
            here = stat_lane == head
            lse_col = jnp.sum(jnp.where(here, lse[...], 0.0), axis=-1, keepdims=True)
            centre_col = jnp.sum(jnp.where(here, centre[...], 0.0), axis=-1, keepdims=True)
            probs = jnp.exp(dot_nt(qm, k) + bias[...] - lse_col)
            grad_scores = (probs * (dot_nt(gm, v) - centre_col)).astype(BF16)
            parts.append(dot_nn(grad_scores, k))
            lse_line = stat_line(head, own_at, 2)
            centre_line = stat_line(16 + head, own_at, 2)
            kp = k_win[window:key_len, lanes]
            vp = v_win[window:key_len, lanes]
            probs_p = jnp.exp(dot_nt(kp, qm) + prompt_bias - lse_line)
            grads_p = (probs_p * (dot_nt(vp, gm) - centre_line)).astype(BF16)
            d_pk = d_pk + dot_nn(grads_p, qm)
            d_pv = d_pv + dot_nn(probs_p.astype(BF16), gm)
        grad_q = jnp.where(first_head_f32, parts[0], parts[1]) * SCALE
        dqkv[0:local_len, lanes] = grad_q.astype(BF16)
        k_lanes = pl.ds(pl.multiple_of(width + hp * 128, 128), 128)
        v_lanes = pl.ds(pl.multiple_of(2 * width + hp * 128, 128), 128)
        dqkv[local_len:p_block, k_lanes] = d_pk.astype(BF16)
        dqkv[local_len:p_block, v_lanes] = d_pv.astype(BF16)

        @pl.when(hp > 1)
        def _():
            advance_one(unit_of(hp - 2))

        return carry

    lax.fori_loop(0, head_pairs, own_queries, 0)
    project_q(tokw[partner_rows, :], partner_rows)
    nbt[0] = nb[0].T
    send_norm.wait_recv()
    send_extra.wait_recv()
    nbt[1] = nb[1].T

    dk, dv = acc_out, acc_dn
    dk[...] = jnp.zeros((local_len, width), F32)
    dv[...] = jnp.zeros((local_len, width), F32)

    def own_keys(at, count):
        cols = halves(at, count)
        mask = bias[:, cols]

        def body(hp, carry):
            lanes = lanes_of(hp)
            k = k_win[own_rows, lanes]
            v = v_win[own_rows, lanes]
            q = q_win[cols, lanes]
            g = ga_win[cols, lanes]
            d_k = dk[:, lanes]
            d_v = dv[:, lanes]
            for h in range(2):
                head = 2 * hp + h
                qm = q * head_mask[h]
                gm = g * head_mask[h]
                lse_line = stat_line(head, at, count)
                centre_line = stat_line(16 + head, at, count)
                probs = jnp.exp(dot_nt(k, qm) + mask - lse_line)
                grad_scores = (probs * (dot_nt(v, gm) - centre_line)).astype(BF16)
                d_k = d_k + dot_nn(grad_scores, qm)
                d_v = d_v + dot_nn(probs.astype(BF16), gm)
            dk[:, lanes] = d_k
            dv[:, lanes] = d_v
            return carry

        lax.fori_loop(0, head_pairs, body, 0)

    def shared_back(i, carry):
        hp = s * x_pairs + i
        lanes = lanes_of(hp)
        q_x = q_win[shared_rows, lanes]
        k_x = k_win[shared_rows, lanes]
        v_x = v_win[shared_rows, lanes]
        g_x = ga_win[shared_rows, lanes]
        k = k_win[:, lanes]
        v = v_win[:, lanes]
        q = q_win[:, lanes]
        g = ga_win[:, lanes]
        product = g_x.astype(F32) * o32_x[:, lanes]
        parts = []
        d_k = jnp.zeros((extra, 2 * HEAD_DIM), F32)
        d_v = jnp.zeros((extra, 2 * HEAD_DIM), F32)
        for h in range(2):
            head = 2 * hp + h
            keep = first_head_f32 if h == 0 else jnp.logical_not(first_head_f32)
            lse_col = jnp.sum(
                jnp.where(x_lane == head, lse_x[...], 0.0), axis=-1, keepdims=True
            )
            centre_col = jnp.sum(jnp.where(keep, product, 0.0), axis=-1, keepdims=True)
            probs = jnp.exp(dot_nt(q_x * head_mask[h], k) + bias_x[...] - lse_col)
            grad_scores = (probs * (dot_nt(g_x * head_mask[h], v) - centre_col)).astype(BF16)
            parts.append(dot_nn(grad_scores, k))
            qm = q * head_mask[h]
            gm = g * head_mask[h]
            lse_line = stat_line(head, 0, 5)
            centre_line = stat_line(16 + head, 0, 5)
            probs = jnp.exp(dot_nt(k_x, qm) + bias_x[:, 0:window] - lse_line)
            grad_scores = (probs * (dot_nt(v_x, gm) - centre_line)).astype(BF16)
            d_k = d_k + dot_nn(grad_scores, qm)
            d_v = d_v + dot_nn(probs.astype(BF16), gm)
        d_q = jnp.where(first_head_f32, parts[0], parts[1]) * SCALE
        for n, part in enumerate((d_q, d_k, d_v)):
            to = pl.ds(pl.multiple_of(n * width + hp * 128, 128), 128)
            dqkv[p_block:tok_block, to] = jnp.where(shared, part, 0.0).astype(BF16)
        return carry

    own_keys(own_at, 2)
    advance_one(2)
    advance_two(0)
    advance_two(4)
    stat_partner(partner_at).wait_recv()
    ga_partner(partner_at).wait_recv()

    for_half_in(lambda *a: stat_half(*a).wait_recv())
    for_half_in(lambda *a: ga_half(*a).wait_recv())

    @pl.when(s < 2)
    def _():
        lax.fori_loop(0, x_pairs, shared_back, 0)

    @pl.when(s == 2)
    def _():
        dqkv[0:extra, 0:width] = jnp.where(
            shared, 0.0, dqkv[0:extra, 0:width].astype(F32)
        ).astype(BF16)

    q_mine = pl.ds(pl.multiple_of(core * half_w, 128), half_w)
    q_other = pl.ds(pl.multiple_of((1 - core) * half_w, 128), half_w)
    send_q = pair_copy(X_Q, dqkv.at[:, q_other], dqp.at[0])
    send_q.start()
    start_three(0)
    start_three(4)
    own_keys(partner_at, 2)
    send_q.wait_recv()
    store_rows(9, dot_nn(nbt[0], dqkv[:, q_mine]) + dot_nn(nbt[1], dqp[0]))
    stage_one(9).start()
    advance_one(6)
    reduced(1)
    reduced(5)
    own_keys(half_at, 1)
    advance_one(3)
    reduced(2)
    advance_one(7)
    reduced(6)

    @pl.when(s == 2)
    def _():
        dk[0:extra, :] = jnp.where(shared, 0.0, dk[0:extra, :])
        dv[0:extra, :] = jnp.where(shared, 0.0, dv[0:extra, :])

    dqkv[0:local_len, width : 2 * width] = dk[...].astype(BF16)
    dqkv[0:local_len, 2 * width :] = dv[...].astype(BF16)
    send_kv = [
        pair_copy(
            X_KV + i,
            dqkv.at[:, pl.ds(pl.multiple_of((1 + i) * width + (1 - core) * half_w, 128), half_w)],
            dqp.at[1 + i],
        )
        for i in range(2)
    ]
    for copy in send_kv:
        copy.start()
    advance_one(8)

    def grad_kv(i):
        send_kv[i].wait_recv()
        lane = pl.ds(pl.multiple_of((1 + i) * width + core * half_w, 128), half_w)
        store_rows(
            10 + i,
            dot_nn(nbt[0], dqkv[:, lane]) + dot_nn(nbt[1], dqp[1 + i]),
        )
        stage_one(10 + i).start()

    grad_kv(0)
    grad_kv(1)
    reduced(3)
    reduced(7)
    grad_normed = dot_nt(dqkv[...], wqkv[...])
    grad_x = grad_normed[p_block:tok_block, :]
    e_x[...] = grad_x.astype(BF16)

    def e_back(j, to):
        return remote(e_x, e_in.at[j], ex_s.at[0], ex_r.at[j], (b, to))

    @pl.when(s < 2)
    def _():
        e_back(s, 2).start()

    advance_one(9)
    reduced(8)
    grad_tok = grad_normed[0:local_len, :]
    e_low[...] = grad_tok[0:extra, :]
    grad_pro = grad_normed[local_len : local_len + prompt_count, :]
    scaled1, inverse1 = norm_stats(tokens_ref[...].astype(F32))
    grad_input_ref[...] = (mid[...] + norm_back(grad_tok, scaled1, inverse1, gain1)).astype(BF16)
    p_scaled, p_inverse = norm_stats(prompts_ref[...])
    sm[0:prompt_count, :] = norm_back(grad_pro, p_scaled, p_inverse, gain1)
    sm[prompt_count : prompt_count + 1, :] = (
        column_sum(grad_tok * scaled1)
        + column_sum(grad_pro * p_scaled)
        + column_sum(grad_x * xh_x[...])
    )
    sm[prompt_count + 1 : prompt_count + 2, :] = (
        column_sum(grad_tok) + column_sum(grad_pro) + column_sum(grad_x)
    )
    sm[prompt_count + 2 : prompt_count + 3, :] = column_sum(dqkv[:, :width].astype(F32))
    sm[prompt_count + 3 : prompt_count + 4, :] = column_sum(dqkv[:, 2 * width :].astype(F32))
    send_sm = pair_copy(X_SMALL, sm.at[:, other_half], smp)
    send_sm.start()
    reduced(9)

    quarter = SMALL_ROWS // 4
    send_sm.wait_recv()
    small = sm[:, my_half] + smp[...]
    for a in range(2):
        for c in range(2):
            s0[a, c] = small[(2 * a + c) * quarter : (2 * a + c + 1) * quarter, :]

    small_one = remote(s0.at[1 - h1], rs1, one_s.at[12], one_r.at[12], nb1)
    small_one.start()
    advance_one(10)
    advance_one(11)
    small_one.wait_recv()
    s1b[...] = s0[h1] + rs1[...]
    small_two = remote(s1b.at[1 - h2], rs2, two_s.at[12], two_r.at[12], nb2)
    small_two.start()
    finish_three(0)
    reduced(10)
    reduced(11)
    small_two.wait_recv()
    rs3[s] = s1b[h2] + rs2[...]

    def small_three(d):
        return remote(
            rs3.at[s], rs3.at[s], three_s.at[12, d - 1], three_r.at[12, s], (b, along(d))
        )

    def small_three_recv(j):
        return remote(rs3.at[j], rs3.at[j], three_s.at[12, 0], three_r.at[12, j], (b, j))

    for d in range(1, groups):
        small_three(d).start()
    finish_three(1)
    start_gather_two(0)
    finish_three(2)
    start_gather_two(1)
    start_gather_pair(0)
    finish_three(3)
    start_gather_pair(1)
    for d in range(1, groups):
        small_three_recv(along(d)).wait_recv()
    total = rs3[0]
    for j in range(1, groups):
        total = total + rs3[j]
    s3[...] = total
    small_keep = pltpu.make_async_copy(s3, small_ref.at[core, h1, h2], loc_sem.at[SMALL])
    small_keep.start()
    small_gather = remote(
        s3, small_ref.at[core, h1, h2], ag1_s.at[SMALL], ag1_r.at[SMALL], nb2
    )
    small_gather.start()
    start_gather_two(2)

    @pl.when(s == 2)
    def _():
        for j in range(2):
            e_back(j, j).wait_recv()
        full = e_low[...] + e_in[0].astype(F32) + e_in[1].astype(F32)
        scaled, inverse = norm_stats(tokens_ref[0:extra, :].astype(F32))
        grad_input_ref[0:extra, :] = (
            mid[0:extra, :] + norm_back(full, scaled, inverse, gain1)
        ).astype(BF16)

    start_gather_two(3)
    small_keep.wait()
    small_gather.wait_recv()
    small_gather_two = remote(
        small_ref.at[core, h1], small_ref.at[core, h1], ag2_s.at[SMALL], ag2_r.at[SMALL], nb1
    )
    small_gather_two.start()
    start_gather_pair(2)
    start_gather_pair(3)
    small_gather_two.wait_recv()
    small_pair = pair_copy(X_FINAL + SMALL, small_ref.at[core], small_ref.at[core])
    small_pair.start()

    small_pair.wait()
    for g in range(len(SLOTS)):
        gather_pair(g).wait()
        gather_one(g).wait_send()
        gather_two(g).wait_send()
    for u in range(12):
        drain_three(u)
    small_one.wait_send()
    small_two.wait_send()
    small_gather.wait_send()
    small_gather_two.wait_send()
    for d in range(1, groups):
        small_three(d).wait_send()

    for side in range(2):
        token_partner(side, own_at).wait_send()
    stat_partner(own_at).wait_send()
    ga_partner(own_at).wait_send()
    for_halves(lambda *a: token_half(*a).wait_send())
    for_halves(lambda *a: stat_half(*a).wait_send())
    for_halves(lambda *a: ga_half(*a).wait_send())

    @pl.when(s < 2)
    def _():
        att_back(s).wait_send()
        lse_back(s).wait_send()
        e_back(s, 2).wait_send()

    def drain(u, carry):
        stage_one(u).wait_send()
        stage_two(u).wait_send()
        return carry

    lax.fori_loop(0, 12, drain, 0)

    def drain_mlp(j, carry):
        send_act(j).wait_send()
        send_gp(j).wait_send()
        return carry

    lax.fori_loop(0, chunks, drain_mlp, 0)
    for copy in (send_cot, send_norm, send_extra, send_att, send_n2, send_gb, send_q, *send_kv, send_sm):
        copy.wait_send()


def finish_kernel(
    width,
    prompt_count,
    ff,
    layer_in,
    grad_in,
    final_hbm,
    small_hbm,
    layer_out_ref,
    grad_input_ref,
    gp_ref,
    g1_ref,
    s1_ref,
    wqkv_ref,
    qb_ref,
    vb_ref,
    wout_ref,
    ob_ref,
    g2_ref,
    s2_ref,
    wfc1_ref,
    b1_ref,
    wfc2_ref,
    b2_ref,
    final,
    small_in,
    small,
    layer_buf,
    grad_buf,
    fc2_buf,
    fc1_buf,
    out_buf,
    qkv_buf,
    gp_buf,
    b1_buf,
    b2_buf,
    *rest,
):
    vec_bufs, (in_sem, out_sem) = rest[:7], rest[7:]
    half_w = width // 2
    blk = final_hbm.shape[4]
    small_loads = pltpu.make_async_copy(small_hbm, small_in, in_sem.at[3])
    small_loads.start()
    loads = [
        pltpu.make_async_copy(
            final_hbm.at[:, :, :, pl.ds(4 * g, 4)], final.at[g], in_sem.at[g]
        )
        for g in range(3)
    ]
    loads.append(pltpu.make_async_copy(layer_in, layer_buf, in_sem.at[4]))
    loads.append(pltpu.make_async_copy(grad_in, grad_buf, in_sem.at[5]))
    for load in loads:
        load.start()
    stores = []

    def store(src, dst):
        copy = pltpu.make_async_copy(src, dst, out_sem.at[len(stores)])
        copy.start()
        stores.append(copy)

    quads = [(c, a, e) for c in range(2) for a in range(2) for e in range(2)]
    small_loads.wait()
    quarter = small_in.shape[3]
    for c, a, e in quads:
        r = (2 * a + e) * quarter
        small[r : r + quarter, c * half_w : (c + 1) * half_w] = small_in[c, a, e]
    gp_buf[...] = small[0:prompt_count, :]
    store(gp_buf, gp_ref)
    vectors = (g1_ref, s1_ref, qb_ref, vb_ref, ob_ref, g2_ref, s2_ref)
    for k, (buf, ref) in enumerate(zip(vec_bufs, vectors)):
        buf[...] = small[prompt_count + k : prompt_count + k + 1, :].reshape(width)
        store(buf, ref)
    for k in range(ff // width):
        r = prompt_count + 7 + k
        b1_buf[k * width : (k + 1) * width] = small[r : r + 1, :].reshape(width)
    store(b1_buf, b1_ref)
    r = prompt_count + 7 + ff // width
    b2_buf[...] = small[r : r + 1, :].reshape(width)
    store(b2_buf, b2_ref)
    loads[0].wait()
    for c, a, e in quads:
        for i in range(4):
            q, r = i // 2, i % 2
            row = c * half_w + (2 * a + e) * (half_w // 4) + r * blk
            fc2_buf[row : row + blk, q * half_w : (q + 1) * half_w] = final[0, c, a, e, i].astype(
                F32
            )
    store(fc2_buf, wfc2_ref)
    loads[1].wait()
    for c, a, e in quads:
        rows = slice((2 * a + e) * blk, (2 * a + e + 1) * blk)
        for i in range(4):
            col = i * width + c * half_w
            fc1_buf[rows, col : col + half_w] = final[1, c, a, e, i].astype(F32)
    store(fc1_buf, wfc1_ref)
    loads[2].wait()
    for c, a, e in quads:
        rows = slice((2 * a + e) * blk, (2 * a + e + 1) * blk)
        cols = slice(c * half_w, (c + 1) * half_w)
        out_buf[rows, cols] = final[2, c, a, e, 0].astype(F32)
        for i in range(3):
            col = i * width + c * half_w
            qkv_buf[rows, col : col + half_w] = final[2, c, a, e, 1 + i].astype(F32)
    store(out_buf, wout_ref)
    store(qkv_buf, wqkv_ref)
    loads[3].wait()
    store(layer_buf, layer_out_ref)
    loads[4].wait()
    store(grad_buf, grad_input_ref)
    for copy in stores:
        copy.wait()


def local(
    tokens,
    segments,
    prompts,
    ln1_gain,
    ln1_shift,
    w_qkv,
    q_bias,
    v_bias,
    w_out,
    out_bias,
    ln2_gain,
    ln2_shift,
    w_fc1,
    fc1_bias,
    w_fc2,
    fc2_bias,
    cotangent,
):
    groups = lax.axis_size("seq")
    batch = lax.axis_size("batch")
    row_count, local_len, width = tokens.shape
    ff = w_fc1.shape[1]
    prompt_count = prompts.shape[0]
    assert row_count == 1 and groups == 4 and batch % GROUP == 0 and ff == 4 * width
    check_window(groups, local_len)
    dims = (groups, local_len, width, ff, prompt_count)
    window = 5 * (local_len // 2)
    extra = extra_rows(local_len)
    half_w = width // 2
    blk = width // groups // 4
    tok_block = local_len + PROMPT_PAD + extra
    quarter = SMALL_ROWS // 4

    vmem = pl.BlockSpec(memory_space=pltpu.VMEM)
    hbm = pl.BlockSpec(memory_space=pl.ANY)
    dma = pltpu.SemaphoreType.DMA
    V = pltpu.VMEM
    scratch = [
        V((width, 3 * width), BF16),
        V((width, width), BF16),
        V((width, ff), BF16),
        V((ff, width), BF16),
        V((window, width), BF16),
        V((2, tok_block, width), BF16),
        V((2, width, tok_block), BF16),
        V((window, width), BF16),
        V((window + PROMPT_PAD, width), BF16),
        V((window + PROMPT_PAD, width), BF16),
        V((local_len, window + PROMPT_PAD), F32),
        V((local_len, width), F32),
        V((2 * local_len, width), BF16),
        V((local_len, 128), F32),
        V((local_len, 128), F32),
        V((local_len, width), F32),
        V((2 * local_len, width), BF16),
        V((width, 2 * local_len), BF16),
        V((4, local_len, width), BF16),
        V((4, local_len, width), BF16),
        V((4, local_len, half_w), BF16),
        V((4, local_len, half_w), BF16),
        V((4, width), F32),
        V((local_len, width), F32),
        V((local_len, width), F32),
        V((local_len, width), BF16),
        V((local_len, width), BF16),
        V((local_len, half_w), BF16),
        V((window, width), BF16),
        V((5, 32, local_len // 2), F32),
        V((tok_block, 3 * width), BF16),
        V((3, tok_block, half_w), BF16),
        V((12, 2, 2, 4, blk, half_w), BF16),
        V((12, 2, 4, blk, half_w), BF16),
        V((12, 4, blk, half_w), BF16),
        V((groups, 12, blk, half_w), BF16),
        V((12, blk, half_w), BF16),
        V((SMALL_ROWS, width), F32),
        V((SMALL_ROWS, half_w), F32),
        V((2, 2, quarter, half_w), F32),
        V((2, quarter, half_w), F32),
        V((2, quarter, half_w), F32),
        V((quarter, half_w), F32),
        V((groups, quarter, half_w), F32),
        V((quarter, half_w), F32),
        V((extra, window + PROMPT_PAD), F32),
        V((extra, width), F32),
        V((extra, width), BF16),
        V((extra, 128), F32),
        V((extra, width), BF16),
        V((2, extra, 128), F32),
        V((extra, width), F32),
        V((extra, width), BF16),
        V((2, extra, width), BF16),
        V((extra, width), F32),
        V((3, local_len, width), F32),
        dma((4,)),
        dma((5,)),
        dma((3,)),
        dma((X_COUNT,)),
        dma((X_COUNT,)),
        dma((4,)),
        dma((2,)),
        dma((4,)),
        dma((2,)),
        dma((13,)),
        dma((13,)),
        dma((13,)),
        dma((13,)),
        dma((13, 3)),
        dma((13, groups)),
        dma((5,)),
        dma((5,)),
        dma((5,)),
        dma((5,)),
        dma((5,)),
        dma((2,)),
        dma((2, 2)),
        dma((1,)),
        dma((2,)),
    ]
    specs = [vmem] * 17
    for index in (5, 8, 12, 14):
        specs[index] = hbm
    layer_out, grad_input, final, small = pl.pallas_call(
        functools.partial(layer_kernel, dims),
        out_shape=(
            jax.ShapeDtypeStruct((local_len, width), BF16),
            jax.ShapeDtypeStruct((local_len, width), BF16),
            jax.ShapeDtypeStruct((2, 2, 2, 12, blk, half_w), BF16),
            jax.ShapeDtypeStruct((2, 2, 2, quarter, half_w), F32),
        ),
        in_specs=specs,
        out_specs=(vmem, vmem, hbm, hbm),
        scratch_shapes=scratch,
        compiler_params=pltpu.CompilerParams(
            collective_id=0, has_side_effects=True, vmem_limit_bytes=67043328
        ),
        name="layer",
    )(
        tokens.reshape(local_len, width),
        segments,
        prompts,
        ln1_gain,
        ln1_shift,
        w_qkv,
        q_bias,
        v_bias,
        w_out,
        out_bias,
        ln2_gain,
        ln2_shift,
        w_fc1,
        fc1_bias,
        w_fc2,
        fc2_bias,
        cotangent.reshape(local_len, width),
    )
    if batch > GROUP:
        rings = [list(range(k, batch, GROUP)) for k in range(GROUP)]
        final, small = lax.psum((final, small), "batch", axis_index_groups=rings)
    rows_z = width // groups

    def flat(n):
        return jax.ShapeDtypeStruct((n,), F32)

    outs = pl.pallas_call(
        functools.partial(finish_kernel, width, prompt_count, ff),
        out_shape=(
            jax.ShapeDtypeStruct((local_len, width), BF16),
            jax.ShapeDtypeStruct((local_len, width), BF16),
            jax.ShapeDtypeStruct((prompt_count, width), F32),
            flat(width),
            flat(width),
            jax.ShapeDtypeStruct((rows_z, 3 * width), F32),
            flat(width),
            flat(width),
            jax.ShapeDtypeStruct((rows_z, width), F32),
            flat(width),
            flat(width),
            flat(width),
            jax.ShapeDtypeStruct((rows_z, ff), F32),
            flat(ff),
            jax.ShapeDtypeStruct((ff // groups, width), F32),
            flat(width),
        ),
        in_specs=[pl.BlockSpec(memory_space=pltpu.HBM)] * 4,
        out_specs=(hbm,) * 16,
        scratch_shapes=[
            V((3, 2, 2, 2, 4, blk, half_w), BF16),
            V((2, 2, 2, quarter, half_w), F32),
            V((SMALL_ROWS, width), F32),
            V((local_len, width), BF16),
            V((local_len, width), BF16),
            V((ff // groups, width), F32),
            V((rows_z, ff), F32),
            V((rows_z, width), F32),
            V((rows_z, 3 * width), F32),
            V((prompt_count, width), F32),
            V((ff,), F32),
            V((width,), F32),
            *[V((width,), F32) for _ in range(7)],
            dma((6,)),
            dma((16,)),
        ],
        compiler_params=pltpu.CompilerParams(vmem_limit_bytes=67043328),
        name="finish",
    )(layer_out, grad_input, final, small)
    return tuple(o.reshape((1, local_len, width)) if i < 2 else o for i, o in enumerate(outs))


def solution(mesh):
    tok = P("batch", "seq", None)
    in_specs = (tok, P("batch", "seq")) + (P(),) * 14 + (tok,)
    out_specs = (
        tok,
        tok,
        P(),
        P(),
        P(),
        P("seq", None),
        P(),
        P(),
        P("seq", None),
        P(),
        P(),
        P(),
        P("seq", None),
        P(),
        P("seq", None),
        P(),
    )
    return jax.shard_map(local, mesh=mesh, in_specs=in_specs, out_specs=out_specs, check_vma=False)
```

```python
import functools

import jax
import jax.numpy as jnp
from jax import lax
from jax.experimental import pallas as pl
from jax.experimental.pallas import tpu as pltpu
from jax.sharding import PartitionSpec as P

HEAD_DIM = 64
IMAGE_TOKENS = (101, 197, 577)
EPSILON = 1e-06
MASKED_SCORE = -1e30
ROOT_HALF = 0.7071067811865476
ROOT_TWO_PI = 2.5066282746310002
SCALE = HEAD_DIM ** (-0.5)
GROUP = 8
PROMPT_PAD = 64
SMALL_ROWS = 64
F32 = jnp.float32
BF16 = jnp.bfloat16
MESH = pl.DeviceIdType.MESH


def dot_nn(a, b):
    return lax.dot_general(a, b, (((1,), (0,)), ((), ())), preferred_element_type=F32)


def dot_nt(a, b):
    return lax.dot_general(a, b, (((1,), (1,)), ((), ())), preferred_element_type=F32)


def dot_tn(a, b):
    return lax.dot_general(a, b, (((0,), (0,)), ((), ())), preferred_element_type=F32)


def check_window(groups, local_len):
    row_len, half_len = groups * local_len, local_len // 2
    cut = 2 * local_len
    for size in IMAGE_TOKENS:
        for first in range(0, row_len, size):
            last = min(first + size, row_len) - 1
            for shard in range(first // local_len, last // local_len + 1):
                start = 0 if shard < 2 else 3 * half_len
                inside = start <= first and last < start + 5 * half_len
                if shard == 3:
                    inside = inside and first >= cut
                given = size == IMAGE_TOKENS[-1] and shard == 2 and first == 0
                assert inside or given
                assert not given or last < cut + extra_rows(local_len)


def extra_rows(local_len):
    return -(-(IMAGE_TOKENS[-1] - 2 * local_len) // 16) * 16


def half_rows_needed(local_len, src, dst):
    if src < dst:
        return local_len // 2
    top = 0
    for size in IMAGE_TOKENS:
        end = ((dst + 1) * local_len - 1) // size * size + size
        top = max(top, end - 2 * local_len)
    return min(-(-top // 16) * 16, local_len // 2)


def norm_stats(values):
    centred = values - jnp.mean(values, axis=-1, keepdims=True)
    inverse = lax.rsqrt(jnp.mean(centred * centred, axis=-1, keepdims=True) + EPSILON)
    return centred * inverse, inverse


def norm_back(grad_out, scaled, inverse, gain):
    inner = grad_out * gain
    return inverse * (
        inner
        - jnp.mean(inner, axis=-1, keepdims=True)
        - scaled * jnp.mean(inner * scaled, axis=-1, keepdims=True)
    )


def line(ref):
    return ref[...].reshape(1, -1)


def column_sum(values):
    return jnp.sum(values, axis=0, keepdims=True)


X_COT, X_N2, X_ATT, X_NORM, X_GB, X_Q, X_KV, X_SMALL, X_FINAL, X_ACT, X_GP, X_EXTRA = 0, 1, 2, 3, 4, 5, 6, 8, 9, 14, 18, 22
X_COUNT = 23
HALVES = ((2, 0, 0), (2, 1, 0), (1, 2, 1))
SLOTS = ((0, 4), (4, 4), (8, 2), (10, 2))
SMALL = 4


def layer_kernel(
    dims,
    tokens_ref,
    seg_ref,
    prompts_ref,
    g1_ref,
    s1_ref,
    wqkv_hbm,
    qb_ref,
    vb_ref,
    wout_hbm,
    ob_ref,
    g2_ref,
    s2_ref,
    wfc1_hbm,
    b1_ref,
    wfc2_hbm,
    b2_ref,
    cot_ref,
    layer_out_ref,
    grad_input_ref,
    final_ref,
    small_ref,
    wqkv,
    wout,
    wfc1,
    wfc2,
    tokw,
    nb,
    nbt,
    q_win,
    k_win,
    v_win,
    bias,
    o32,
    att,
    lse,
    centre,
    mid,
    n2,
    n2t,
    act,
    gp,
    actp,
    gpp,
    b1s,
    acc_out,
    acc_dn,
    cotp,
    gb,
    gbp,
    ga_win,
    stat,
    dqkv,
    dqp,
    units,
    r1,
    r2u,
    r3,
    a3,
    sm,
    smp,
    s0,
    rs1,
    s1b,
    rs2,
    rs3,
    s3,
    bias_x,
    o32_x,
    att_x,
    lse_x,
    att_in,
    lse_in,
    xh_x,
    e_x,
    e_in,
    e_low,
    dact,
    wsem,
    tok_s,
    tok_r,
    pair_s,
    pair_r,
    ga_s,
    ga_r,
    st_s,
    st_r,
    one_s,
    one_r,
    two_s,
    two_r,
    three_s,
    three_r,
    loc_sem,
    ag1_s,
    ag1_r,
    ag2_s,
    ag2_r,
    ax_s,
    ax_r,
    ex_s,
    ex_r,
):
    groups, local_len, width, ff, prompt_count = dims
    half_len = local_len // 2
    window = 5 * half_len
    cut = 2 * local_len
    extra = extra_rows(local_len)
    head_pairs = width // (2 * HEAD_DIM)
    chunks = ff // width
    half_w = width // 2
    key_len = window + PROMPT_PAD
    zrows = width // groups

    b = lax.axis_index("batch")
    s = lax.axis_index("seq")
    base = (b // GROUP) * GROUP
    core = lax.rem(b, 2)
    xb = lax.rem(b // 2, 2)
    yb = lax.rem(b // 4, 2)
    h1 = xb * (1 - core) + yb * core
    h2 = yb * (1 - core) + xb * core

    def place(x, y, c):
        return base + y * 4 + x * 2 + c

    nb1 = (place(xb + (1 - core) * (1 - 2 * xb), yb + core * (1 - 2 * yb), core), s)
    nb2 = (place(xb + core * (1 - 2 * xb), yb + (1 - core) * (1 - 2 * yb), core), s)
    pair = (place(xb, yb, 1 - core), s)

    def along(d):
        return lax.rem(s + d, groups)

    first_half = jnp.where(s < 2, 0, 3)
    start = first_half * half_len
    partner = s + 1 - 2 * lax.rem(s, 2)
    own_at = 2 * s - first_half
    partner_at = 2 * partner - first_half
    half_at = jnp.where(s < 2, 4, 0)

    def halves(at, count):
        return pl.ds(pl.multiple_of(at * half_len, half_len), count * half_len)

    own_rows = halves(own_at, 2)
    partner_rows = halves(partner_at, 2)
    half_rows = halves(half_at, 1)
    shared_rows = pl.ds(4 * half_len, extra)

    def remote(src, dst, send, recv, to):
        return pltpu.make_async_remote_copy(
            src_ref=src, dst_ref=dst, send_sem=send, recv_sem=recv, device_id=to, device_id_type=MESH
        )

    barrier = pltpu.get_barrier_semaphore()
    for peer in (pair, nb1, nb2):
        pl.semaphore_signal(barrier, inc=1, device_id=peer, device_id_type=MESH)
    for d in range(1, groups):
        pl.semaphore_signal(barrier, inc=1, device_id=(b, along(d)), device_id_type=MESH)

    loads = [
        pltpu.make_async_copy(wqkv_hbm, wqkv, wsem.at[0]),
        pltpu.make_async_copy(wout_hbm, wout, wsem.at[1]),
        pltpu.make_async_copy(wfc1_hbm, wfc1, wsem.at[2]),
        pltpu.make_async_copy(wfc2_hbm, wfc2, wsem.at[3]),
    ]
    loads[0].start()
    pl.semaphore_wait(barrier, 2 + groups)

    def token_partner(side, at):
        part = tokens_ref.at[pl.ds(side * half_len, half_len)]
        return remote(
            part, tokw.at[halves(at + side, 1)], tok_s.at[side], tok_r.at[side], (b, partner)
        )

    def token_half(i, side, at, to):
        count = half_rows_needed(local_len, HALVES[i][0], HALVES[i][1])
        return remote(
            tokens_ref.at[pl.ds(side * half_len, count)],
            tokw.at[pl.ds(at * half_len, count)],
            tok_s.at[2 + i],
            tok_r.at[2],
            (b, to),
        )

    def for_halves(action):
        for i, (src, dst, side) in enumerate(HALVES):

            @pl.when(s == src)
            def _(i=i, dst=dst, side=side):
                action(i, side, 4 if dst < 2 else 0, dst)

    def for_half_in(action):
        for i, (src, dst, side) in enumerate(HALVES):

            @pl.when(s == dst)
            def _(i=i, src=src, side=side, dst=dst):
                action(i, side, 4 if dst < 2 else 0, src)

    for_halves(lambda *a: token_half(*a).start())
    for side in range(2):
        token_partner(side, own_at).start()

    for load in loads[1:]:
        load.start()

    def pair_copy(index, src, dst):
        return remote(src, dst, pair_s.at[index], pair_r.at[index], pair)

    my_half = pl.ds(pl.multiple_of(core * half_w, 128), half_w)
    other_half = pl.ds(pl.multiple_of((1 - core) * half_w, 128), half_w)

    send_cot = pair_copy(X_COT, cot_ref, cotp)
    send_cot.start()

    gain1 = line(g1_ref)
    shift1 = line(s1_ref)
    for i in range(chunks):
        b1s[i : i + 1, :] = b1_ref[i * width : (i + 1) * width].reshape(1, width)

    last = s * local_len + local_len - 1
    seg_last = seg_ref[:, local_len - 1 : local_len].astype(F32)
    inv_n = jnp.full((1, 1), 1.0 / IMAGE_TOKENS[-1], F32)
    is_long = jnp.ones((1, 1), F32)
    for size in IMAGE_TOKENS[:-1]:
        here = seg_last == (last // size).astype(F32)
        inv_n = jnp.where(here, 1.0 / size, inv_n)
        is_long = jnp.where(here, 0.0, is_long)
    k_pos = lax.broadcasted_iota(jnp.int32, (1, key_len), 1)
    k_open = jnp.where(k_pos < window, 0.0, jnp.where(k_pos < window + prompt_count, 1.0, 0.0))
    k_id = jnp.floor(((k_pos + start).astype(F32) + 0.5) * inv_n)
    k_id = jnp.where(k_pos < window, k_id, -1.0)

    def mask_of(q_pos):
        q_id = jnp.floor((q_pos.astype(F32) + 0.5) * inv_n)
        return jnp.where(q_id == k_id, 0.0, MASKED_SCORE * (1.0 - k_open))

    bias[...] = mask_of(lax.broadcasted_iota(jnp.int32, (local_len, 1), 0) + s * local_len)
    x_row = lax.broadcasted_iota(jnp.int32, (extra, 1), 0)
    bias_x[...] = mask_of(x_row + cut)
    shared = jnp.where(x_row + cut < IMAGE_TOKENS[-1], is_long, 0.0) > 0.5

    def project_q(normed, rows):
        q = dot_nn(normed, wqkv[:, :width]) + line(qb_ref)
        q_win[rows, :] = (q.astype(BF16).astype(F32) * SCALE).astype(BF16)

    def project(normed, rows):
        k_win[rows, :] = dot_nn(normed, wqkv[:, width : 2 * width]).astype(BF16)
        v_win[rows, :] = (dot_nn(normed, wqkv[:, 2 * width :]) + line(vb_ref)).astype(BF16)

    p_scaled, p_inverse = norm_stats(prompts_ref[...])
    p_block = local_len + PROMPT_PAD
    tok_block = p_block + extra
    nb[0, local_len:p_block, :] = jnp.zeros((PROMPT_PAD, width), BF16)
    nb[0, local_len : local_len + prompt_count, :] = (p_scaled * gain1 + shift1).astype(BF16)
    scaled1, _ = norm_stats(tokens_ref[...].astype(F32))
    nb[0, 0:local_len, :] = (scaled1 * gain1 + shift1).astype(BF16)
    send_norm = pair_copy(X_NORM, nb.at[0, pl.ds(0, p_block)], nb.at[1, pl.ds(0, p_block)])
    send_norm.start()

    tail = half_rows_needed(local_len, 2, 0)
    tail_rows = pl.ds(4 * half_len + tail, half_len - tail)

    @pl.when(s == 0)
    def _():
        tokw[tail_rows, :] = jnp.zeros((half_len - tail, width), BF16)
        ga_win[tail_rows, :] = jnp.zeros((half_len - tail, width), BF16)

    tail_one = half_rows_needed(local_len, 2, 1)
    tail_one_rows = pl.ds(4 * half_len + tail_one, half_len - tail_one)

    @pl.when(s == 1)
    def _():
        tokw[tail_one_rows, :] = jnp.zeros((half_len - tail_one, width), BF16)
        ga_win[tail_one_rows, :] = jnp.zeros((half_len - tail_one, width), BF16)

    loads[0].wait()
    project_q(nb[0, 0:local_len, :], own_rows)
    project(nb[0, 0:local_len, :], own_rows)
    p_low = nb[0, local_len:p_block, :]
    k_win[window:key_len, :] = dot_nn(p_low, wqkv[:, width : 2 * width]).astype(BF16)
    v_win[window:key_len, :] = (dot_nn(p_low, wqkv[:, 2 * width :]) + line(vb_ref)).astype(BF16)

    def normed_tokens(rows):
        scaled, _ = norm_stats(tokw[rows, :].astype(F32))
        return (scaled * gain1 + shift1).astype(BF16)

    loads[3].wait()

    held = chunks - 1

    def grad_act(i, carry):
        rows = pl.ds(pl.multiple_of(i * width, 128), width)
        dact[lax.rem(i, held)] = dot_nt(cot_ref[...], wfc2[rows, :])
        return carry

    lax.fori_loop(0, held, grad_act, 0)

    def partner_piece(side):
        token_partner(side, partner_at).wait_recv()
        rows = halves(partner_at + side, 1)
        normed = normed_tokens(rows)
        tokw[rows, :] = normed
        project(normed, rows)

    partner_piece(0)
    for_half_in(lambda *a: token_half(*a).wait_recv())

    @pl.when(s < groups - 1)
    def _():
        normed = normed_tokens(half_rows)
        project_q(normed, half_rows)
        project(normed, half_rows)

    partner_piece(1)

    @pl.when(s == groups - 1)
    def _():
        empty = jnp.zeros((half_len, width), BF16)
        q_win[0:half_len, :] = empty
        k_win[0:half_len, :] = empty
        v_win[0:half_len, :] = empty
        ga_win[0:half_len, :] = empty
        stat[0] = jnp.zeros((32, half_len), F32)

    @pl.when(s < 2)
    def _():
        scaled, _ = norm_stats(tokw[shared_rows, :].astype(F32))
        xh_x[...] = scaled
        nb[0, p_block:tok_block, :] = (scaled * gain1 + shift1).astype(BF16)

    @pl.when(s >= 2)
    def _():
        xh_x[...] = jnp.zeros((extra, width), F32)
        nb[0, p_block:tok_block, :] = jnp.zeros((extra, width), BF16)

    send_extra = pair_copy(
        X_EXTRA, nb.at[0, pl.ds(p_block, extra)], nb.at[1, pl.ds(p_block, extra)]
    )
    send_extra.start()

    pair_lane = lax.broadcasted_iota(jnp.int32, (1, 2 * HEAD_DIM), 1)
    first_head = jnp.where(pair_lane < HEAD_DIM, 1.0, 0.0)
    head_mask = (first_head.astype(BF16), (1.0 - first_head).astype(BF16))
    first_head_f32 = pair_lane < HEAD_DIM
    stat_lane = lax.broadcasted_iota(jnp.int32, (local_len, 128), 1)

    def lanes_of(hp):
        return pl.ds(pl.multiple_of(hp * 2 * HEAD_DIM, 128), 2 * HEAD_DIM)

    lse[...] = jnp.zeros((local_len, 128), F32)
    centre[...] = jnp.zeros((local_len, 128), F32)

    def softmax_heads(q, lanes, mask):
        k = k_win[:, lanes]
        v = v_win[:, lanes]
        outs, logs = [], []
        for h in range(2):
            scores = dot_nt(q * head_mask[h], k) + mask[...]
            highest = jnp.max(scores, axis=-1, keepdims=True)
            weights = jnp.exp(scores - highest)
            total = jnp.sum(weights, axis=-1, keepdims=True)
            outs.append(dot_nn(weights.astype(BF16), v) / total)
            logs.append(highest + jnp.log(total))
        return jnp.where(first_head_f32, outs[0], outs[1]), logs

    x_pairs = head_pairs // 2
    x_lane = lax.broadcasted_iota(jnp.int32, (extra, 128), 1)

    def x_lanes(j):
        return pl.ds(pl.multiple_of(j * half_w, 128), half_w)

    def att_back(j):
        return remote(
            att_x.at[:, x_lanes(j)], att_in.at[:, x_lanes(j)], ax_s.at[0], ax_r.at[0, j], (b, 2)
        )

    def lse_back(j):
        return remote(lse_x, lse_in.at[j], ax_s.at[1], ax_r.at[1, j], (b, 2))

    @pl.when(s < 2)
    def _():
        lse_x[...] = jnp.zeros((extra, 128), F32)

        def attend_shared(i, carry):
            hp = s * x_pairs + i
            lanes = lanes_of(hp)
            combined, logs = softmax_heads(q_win[shared_rows, lanes], lanes, bias_x)
            o32_x[:, lanes] = combined
            att_x[:, lanes] = combined.astype(BF16)
            for h in range(2):
                lse_x[...] = jnp.where(x_lane == 2 * hp + h, logs[h], lse_x[...])
            return carry

        lax.fori_loop(0, x_pairs, attend_shared, 0)
        att_back(s).start()
        lse_back(s).start()

    def attend(hp, carry):
        lanes = lanes_of(hp)
        combined, logs = softmax_heads(q_win[own_rows, lanes], lanes, bias)
        o32[:, lanes] = combined
        att[0:local_len, lanes] = combined.astype(BF16)
        for h in range(2):
            lse[...] = jnp.where(stat_lane == 2 * hp + h, logs[h], lse[...])
        return carry

    lax.fori_loop(0, head_pairs, attend, 0)

    @pl.when(s == 2)
    def _():
        for j in range(2):
            remote(
                att_x.at[:, x_lanes(j)], att_in.at[:, x_lanes(j)], ax_s.at[0], ax_r.at[0, j], (b, j)
            ).wait_recv()
            remote(lse_x, lse_in.at[j], ax_s.at[1], ax_r.at[1, j], (b, j)).wait_recv()
        merged = jnp.where(shared, att_in[...].astype(F32), o32[0:extra, :])
        o32[0:extra, :] = merged
        att[0:extra, :] = merged.astype(BF16)
        lse[0:extra, :] = jnp.where(shared, lse_in[0] + lse_in[1], lse[0:extra, :])

    own = pl.ds(0, local_len)
    theirs = pl.ds(local_len, local_len)
    send_att = pair_copy(X_ATT, att.at[own], att.at[theirs])
    send_att.start()

    loads[1].wait()
    mid[...] = (
        tokens_ref[...].astype(F32) + dot_nn(att[0:local_len, :], wout[...]) + line(ob_ref)
    )
    scaled2, _ = norm_stats(mid[...])
    n2[0:local_len, :] = (scaled2 * line(g2_ref) + line(s2_ref)).astype(BF16)
    send_n2 = pair_copy(X_N2, n2.at[own], n2.at[theirs])
    send_n2.start()
    acc_out[...] = jnp.zeros((local_len, width), F32)
    acc_dn[...] = jnp.zeros((local_len, width), F32)
    loads[2].wait()

    blk = zrows // 4

    def unit_of(p):
        return p // 2 + 4 * lax.rem(p, 2)

    def store_rows(u, grads):
        for z in range(groups):
            for a in range(2):
                for c in range(2):
                    r = z * zrows + (2 * a + c) * blk
                    units[u, a, c, z] = grads[r : r + blk, :].astype(BF16)

    def stage_one(u):
        return remote(units.at[u, 1 - h1], r1.at[u], one_s.at[u], one_r.at[u], nb1)

    def stage_two(u):
        return remote(units.at[u, h1, 1 - h2], r2u.at[u], two_s.at[u], two_r.at[u], nb2)

    def advance_one(u):
        stage_one(u).wait_recv()
        units[u, h1] = (units[u, h1].astype(F32) + r1[u].astype(F32)).astype(BF16)
        stage_two(u).start()

    def advance_two(u):
        stage_two(u).wait_recv()
        r2u[u] = (units[u, h1, h2].astype(F32) + r2u[u].astype(F32)).astype(BF16)

    def stage_three_fc2(u):
        return remote(
            r2u.at[u], r3.at[s, pl.ds(0, 4)], three_s.at[u, 0], three_r.at[0, s], (b, u)
        )

    def stage_three(u, d):
        t = along(d)
        return remote(r2u.at[u, t], r3.at[s, u], three_s.at[u, d - 1], three_r.at[u, s], (b, t))

    def start_three(u):
        if u < 4:

            @pl.when(s != u)
            def _():
                stage_three_fc2(u).start()

        else:
            for d in range(1, groups):
                stage_three(u, d).start()

    def drain_three(u):
        if u < 4:

            @pl.when(s != u)
            def _():
                stage_three_fc2(u).wait_send()

        else:
            for d in range(1, groups):
                stage_three(u, d).wait_send()

    def slots(g):
        return pl.ds(*SLOTS[g])

    def keep_final(g):
        return pltpu.make_async_copy(
            a3.at[slots(g)], final_ref.at[core, h1, h2, slots(g)], loc_sem.at[g]
        )

    def gather_one(g):
        return remote(
            a3.at[slots(g)],
            final_ref.at[core, h1, h2, slots(g)],
            ag1_s.at[g],
            ag1_r.at[g],
            nb2,
        )

    def gather_two(g):
        ref = final_ref.at[core, h1, :, slots(g)]
        return remote(ref, ref, ag2_s.at[g], ag2_r.at[g], nb1)

    def gather_pair(g):
        ref = final_ref.at[core, :, :, slots(g)]
        return pair_copy(X_FINAL + g, ref, ref)

    def finish_three(g):
        first, count = SLOTS[g]
        if g == 0:
            total = r2u[s].astype(F32)
            for d in range(1, groups):
                j = along(d)
                remote(
                    r2u.at[0], r3.at[j, pl.ds(0, 4)], three_s.at[0, 0], three_r.at[0, j], (b, j)
                ).wait_recv()
                total = total + r3[j, 0:4].astype(F32)
            a3[0:4] = total.astype(BF16)
        else:
            for u in range(first, first + count):
                total = r2u[u, s].astype(F32)
                for d in range(1, groups):
                    j = along(d)
                    remote(
                        r2u.at[u, 0], r3.at[j, u], three_s.at[u, 0], three_r.at[u, j], (b, j)
                    ).wait_recv()
                    total = total + r3[j, u].astype(F32)
                a3[u] = total.astype(BF16)
        keep_final(g).start()
        gather_one(g).start()

    def start_gather_two(g):
        keep_final(g).wait()
        gather_one(g).wait_recv()
        gather_two(g).start()

    def start_gather_pair(g):
        gather_two(g).wait_recv()
        gather_pair(g).start()

    def reduced(u):
        advance_two(u)
        start_three(u)

    sm[...] = jnp.zeros((SMALL_ROWS, width), F32)

    def send_act(j):
        return pair_copy(X_ACT + j, act.at[j, :, other_half], actp.at[j])

    def send_gp(j):
        return pair_copy(X_GP + j, gp.at[j, :, other_half], gpp.at[j])

    def hidden(i):
        cols = pl.ds(pl.multiple_of(i * width, 128), width)
        w1 = wfc1[:, cols]
        w2 = wfc2[cols, :]
        pre = dot_nn(n2[0:local_len, :], w1) + b1s[pl.ds(i, 1), :]
        phi = 0.5 * (1.0 + lax.erf(pre * ROOT_HALF))
        activated = (pre * phi).astype(BF16)
        act[i] = activated
        send_act(i).start()
        slope = phi + pre * jnp.exp(-0.5 * pre * pre) / ROOT_TWO_PI
        grad_pre = (dact[lax.rem(i, held)] * slope).astype(BF16)
        gp[i] = grad_pre
        send_gp(i).start()
        sm[pl.ds(prompt_count + 7 + i, 1), :] = column_sum(grad_pre.astype(F32))
        acc_out[...] += dot_nn(activated, w2)
        acc_dn[...] += dot_nt(grad_pre, w1)

    def grad_fc2(j):
        send_act(j).wait_recv()
        grads2 = dot_tn(act[j, :, my_half], cot_ref[...]) + dot_tn(actp[j], cotp[...])
        rows = half_w // 4
        for a in range(2):
            for c in range(2):
                for q in range(2):
                    for e in range(2):
                        r = (2 * a + c) * rows + e * blk
                        units[j, a, c, 2 * q + e] = grads2[
                            r : r + blk, q * half_w : (q + 1) * half_w
                        ].astype(BF16)
        stage_one(j).start()

    def grad_fc1(j):
        send_gp(j).wait_recv()
        store_rows(
            4 + j,
            dot_nn(n2t[:, 0:local_len], gp[j, :, my_half]) + dot_nn(n2t[:, local_len:], gpp[j]),
        )
        stage_one(4 + j).start()

    def mlp(i, carry):
        @pl.when(i == 1)
        def _():
            send_cot.wait_recv()
            grad_fc2(0)

        @pl.when(i < chunks)
        def _():
            hidden(i)

        @pl.when(i == 1)
        def _():
            grad_act(held, 0)
            n2t[:, 0:local_len] = n2[0:local_len, :].T
            send_n2.wait_recv()
            n2t[:, local_len:] = n2[local_len:, :].T

        @pl.when(i > 1)
        def _():
            grad_fc2(i - 1)

        @pl.when(i > 0)
        def _():
            grad_fc1(i - 1)

        return carry

    lax.fori_loop(0, chunks + 1, mlp, 0)

    grad_out = cot_ref[...].astype(F32)
    layer_out_ref[...] = (mid[...] + acc_out[...] + line(b2_ref)).astype(BF16)
    grad_n2 = acc_dn[...]
    scaled2, inverse2 = norm_stats(mid[...])
    sm[prompt_count + 11 : prompt_count + 12, :] = column_sum(grad_out)
    sm[prompt_count + 5 : prompt_count + 6, :] = column_sum(grad_n2 * scaled2)
    sm[prompt_count + 6 : prompt_count + 7, :] = column_sum(grad_n2)
    grad_mid = grad_out + norm_back(grad_n2, scaled2, inverse2, line(g2_ref))
    mid[...] = grad_mid
    branch = grad_mid.astype(BF16)
    gb[...] = branch
    send_gb = pair_copy(X_GB, gb.at[:, other_half], gbp)
    send_gb.start()
    sm[prompt_count + 4 : prompt_count + 5, :] = column_sum(branch.astype(F32))
    grad_att = dot_nt(branch, wout[...]).astype(BF16)
    ga_win[own_rows, :] = grad_att
    product = grad_att.astype(F32) * o32[...]
    for hp in range(head_pairs):
        block = product[:, hp * 128 : (hp + 1) * 128]
        for h in range(2):
            keep = first_head_f32 if h == 0 else jnp.logical_not(first_head_f32)
            total = jnp.sum(jnp.where(keep, block, 0.0), axis=-1, keepdims=True)
            centre[...] = jnp.where(stat_lane == 2 * hp + h, total, centre[...])
    for i in range(2):
        part = slice(i * half_len, (i + 1) * half_len)
        stat[own_at + i, 0:16, :] = lse[part, :].T[0:16, :]
        stat[own_at + i, 16:32, :] = centre[part, :].T[0:16, :]

    def ga_partner(at):
        part = ga_win.at[halves(at, 2)]
        return remote(part, part, ga_s.at[0], ga_r.at[0], (b, partner))

    def stat_partner(at):
        part = stat.at[pl.ds(at, 2)]
        return remote(part, part, st_s.at[0], st_r.at[0], (b, partner))

    def ga_half(i, side, at, to):
        count = half_rows_needed(local_len, HALVES[i][0], HALVES[i][1])
        rows = pl.ds(pl.multiple_of((own_at + side) * half_len, half_len), count)
        return remote(
            ga_win.at[rows],
            ga_win.at[pl.ds(at * half_len, count)],
            ga_s.at[1 + i],
            ga_r.at[1],
            (b, to),
        )

    def stat_half(i, side, at, to):
        return remote(stat.at[own_at + side], stat.at[at], st_s.at[1 + i], st_r.at[1], (b, to))

    def stat_line(row, at, count):
        return jnp.concatenate([stat[at + i, pl.ds(row, 1), :] for i in range(count)], axis=1)

    for_halves(lambda *a: stat_half(*a).start())
    for_halves(lambda *a: ga_half(*a).start())
    stat_partner(own_at).start()
    ga_partner(own_at).start()

    send_att.wait_recv()
    send_gb.wait_recv()
    store_rows(
        8, dot_tn(att[0:local_len, :], gb[:, my_half]) + dot_tn(att[local_len:, :], gbp[...])
    )
    stage_one(8).start()

    prompt_row = lax.broadcasted_iota(jnp.int32, (PROMPT_PAD, 1), 0)
    prompt_bias = jnp.where(prompt_row < prompt_count, 0.0, MASKED_SCORE)
    dqkv[local_len:tok_block, :] = jnp.zeros((PROMPT_PAD + extra, 3 * width), BF16)

    def own_queries(hp, carry):
        lanes = lanes_of(hp)
        q = q_win[own_rows, lanes]
        k = k_win[:, lanes]
        v = v_win[:, lanes]
        g = ga_win[own_rows, lanes]
        parts = []
        d_pk = jnp.zeros((PROMPT_PAD, 2 * HEAD_DIM), F32)
        d_pv = jnp.zeros((PROMPT_PAD, 2 * HEAD_DIM), F32)
        for h in range(2):
            head = 2 * hp + h
            qm = q * head_mask[h]
            gm = g * head_mask[h]
            here = stat_lane == head
            lse_col = jnp.sum(jnp.where(here, lse[...], 0.0), axis=-1, keepdims=True)
            centre_col = jnp.sum(jnp.where(here, centre[...], 0.0), axis=-1, keepdims=True)
            probs = jnp.exp(dot_nt(qm, k) + bias[...] - lse_col)
            grad_scores = (probs * (dot_nt(gm, v) - centre_col)).astype(BF16)
            parts.append(dot_nn(grad_scores, k))
            lse_line = stat_line(head, own_at, 2)
            centre_line = stat_line(16 + head, own_at, 2)
            kp = k_win[window:key_len, lanes]
            vp = v_win[window:key_len, lanes]
            probs_p = jnp.exp(dot_nt(kp, qm) + prompt_bias - lse_line)
            grads_p = (probs_p * (dot_nt(vp, gm) - centre_line)).astype(BF16)
            d_pk = d_pk + dot_nn(grads_p, qm)
            d_pv = d_pv + dot_nn(probs_p.astype(BF16), gm)
        grad_q = jnp.where(first_head_f32, parts[0], parts[1]) * SCALE
        dqkv[0:local_len, lanes] = grad_q.astype(BF16)
        k_lanes = pl.ds(pl.multiple_of(width + hp * 128, 128), 128)
        v_lanes = pl.ds(pl.multiple_of(2 * width + hp * 128, 128), 128)
        dqkv[local_len:p_block, k_lanes] = d_pk.astype(BF16)
        dqkv[local_len:p_block, v_lanes] = d_pv.astype(BF16)

        @pl.when(hp > 1)
        def _():
            advance_one(unit_of(hp - 2))

        return carry

    lax.fori_loop(0, head_pairs, own_queries, 0)
    project_q(tokw[partner_rows, :], partner_rows)
    nbt[0] = nb[0].T
    send_norm.wait_recv()
    send_extra.wait_recv()
    nbt[1] = nb[1].T

    dk, dv = acc_out, acc_dn
    dk[...] = jnp.zeros((local_len, width), F32)
    dv[...] = jnp.zeros((local_len, width), F32)

    def own_keys(at, count):
        cols = halves(at, count)
        mask = bias[:, cols]

        def body(hp, carry):
            lanes = lanes_of(hp)
            k = k_win[own_rows, lanes]
            v = v_win[own_rows, lanes]
            q = q_win[cols, lanes]
            g = ga_win[cols, lanes]
            d_k = dk[:, lanes]
            d_v = dv[:, lanes]
            for h in range(2):
                head = 2 * hp + h
                qm = q * head_mask[h]
                gm = g * head_mask[h]
                lse_line = stat_line(head, at, count)
                centre_line = stat_line(16 + head, at, count)
                probs = jnp.exp(dot_nt(k, qm) + mask - lse_line)
                grad_scores = (probs * (dot_nt(v, gm) - centre_line)).astype(BF16)
                d_k = d_k + dot_nn(grad_scores, qm)
                d_v = d_v + dot_nn(probs.astype(BF16), gm)
            dk[:, lanes] = d_k
            dv[:, lanes] = d_v
            return carry

        lax.fori_loop(0, head_pairs, body, 0)

    def shared_back(i, carry):
        hp = s * x_pairs + i
        lanes = lanes_of(hp)
        q_x = q_win[shared_rows, lanes]
        k_x = k_win[shared_rows, lanes]
        v_x = v_win[shared_rows, lanes]
        g_x = ga_win[shared_rows, lanes]
        k = k_win[:, lanes]
        v = v_win[:, lanes]
        q = q_win[:, lanes]
        g = ga_win[:, lanes]
        product = g_x.astype(F32) * o32_x[:, lanes]
        parts = []
        d_k = jnp.zeros((extra, 2 * HEAD_DIM), F32)
        d_v = jnp.zeros((extra, 2 * HEAD_DIM), F32)
        for h in range(2):
            head = 2 * hp + h
            keep = first_head_f32 if h == 0 else jnp.logical_not(first_head_f32)
            lse_col = jnp.sum(
                jnp.where(x_lane == head, lse_x[...], 0.0), axis=-1, keepdims=True
            )
            centre_col = jnp.sum(jnp.where(keep, product, 0.0), axis=-1, keepdims=True)
            probs = jnp.exp(dot_nt(q_x * head_mask[h], k) + bias_x[...] - lse_col)
            grad_scores = (probs * (dot_nt(g_x * head_mask[h], v) - centre_col)).astype(BF16)
            parts.append(dot_nn(grad_scores, k))
            qm = q * head_mask[h]
            gm = g * head_mask[h]
            lse_line = stat_line(head, 0, 5)
            centre_line = stat_line(16 + head, 0, 5)
            probs = jnp.exp(dot_nt(k_x, qm) + bias_x[:, 0:window] - lse_line)
            grad_scores = (probs * (dot_nt(v_x, gm) - centre_line)).astype(BF16)
            d_k = d_k + dot_nn(grad_scores, qm)
            d_v = d_v + dot_nn(probs.astype(BF16), gm)
        d_q = jnp.where(first_head_f32, parts[0], parts[1]) * SCALE
        for n, part in enumerate((d_q, d_k, d_v)):
            to = pl.ds(pl.multiple_of(n * width + hp * 128, 128), 128)
            dqkv[p_block:tok_block, to] = jnp.where(shared, part, 0.0).astype(BF16)
        return carry

    own_keys(own_at, 2)
    advance_one(2)
    advance_two(0)
    advance_two(4)
    stat_partner(partner_at).wait_recv()
    ga_partner(partner_at).wait_recv()

    for_half_in(lambda *a: stat_half(*a).wait_recv())
    for_half_in(lambda *a: ga_half(*a).wait_recv())

    @pl.when(s < 2)
    def _():
        lax.fori_loop(0, x_pairs, shared_back, 0)

    @pl.when(s == 2)
    def _():
        dqkv[0:extra, 0:width] = jnp.where(
            shared, 0.0, dqkv[0:extra, 0:width].astype(F32)
        ).astype(BF16)

    q_mine = pl.ds(pl.multiple_of(core * half_w, 128), half_w)
    q_other = pl.ds(pl.multiple_of((1 - core) * half_w, 128), half_w)
    send_q = pair_copy(X_Q, dqkv.at[:, q_other], dqp.at[0])
    send_q.start()
    start_three(0)
    start_three(4)
    own_keys(partner_at, 2)
    send_q.wait_recv()
    store_rows(9, dot_nn(nbt[0], dqkv[:, q_mine]) + dot_nn(nbt[1], dqp[0]))
    stage_one(9).start()
    advance_one(6)
    reduced(1)
    reduced(5)
    own_keys(half_at, 1)
    advance_one(3)
    reduced(2)
    advance_one(7)
    reduced(6)

    @pl.when(s == 2)
    def _():
        dk[0:extra, :] = jnp.where(shared, 0.0, dk[0:extra, :])
        dv[0:extra, :] = jnp.where(shared, 0.0, dv[0:extra, :])

    dqkv[0:local_len, width : 2 * width] = dk[...].astype(BF16)
    dqkv[0:local_len, 2 * width :] = dv[...].astype(BF16)
    send_kv = [
        pair_copy(
            X_KV + i,
            dqkv.at[:, pl.ds(pl.multiple_of((1 + i) * width + (1 - core) * half_w, 128), half_w)],
            dqp.at[1 + i],
        )
        for i in range(2)
    ]
    for copy in send_kv:
        copy.start()
    advance_one(8)

    def grad_kv(i):
        send_kv[i].wait_recv()
        lane = pl.ds(pl.multiple_of((1 + i) * width + core * half_w, 128), half_w)
        store_rows(
            10 + i,
            dot_nn(nbt[0], dqkv[:, lane]) + dot_nn(nbt[1], dqp[1 + i]),
        )
        stage_one(10 + i).start()

    grad_kv(0)
    grad_kv(1)
    reduced(3)
    reduced(7)
    grad_normed = dot_nt(dqkv[...], wqkv[...])
    grad_x = grad_normed[p_block:tok_block, :]
    e_x[...] = grad_x.astype(BF16)

    def e_back(j, to):
        return remote(e_x, e_in.at[j], ex_s.at[0], ex_r.at[j], (b, to))

    @pl.when(s < 2)
    def _():
        e_back(s, 2).start()

    advance_one(9)
    reduced(8)
    grad_tok = grad_normed[0:local_len, :]
    e_low[...] = grad_tok[0:extra, :]
    grad_pro = grad_normed[local_len : local_len + prompt_count, :]
    scaled1, inverse1 = norm_stats(tokens_ref[...].astype(F32))
    grad_input_ref[...] = (mid[...] + norm_back(grad_tok, scaled1, inverse1, gain1)).astype(BF16)
    p_scaled, p_inverse = norm_stats(prompts_ref[...])
    sm[0:prompt_count, :] = norm_back(grad_pro, p_scaled, p_inverse, gain1)
    sm[prompt_count : prompt_count + 1, :] = (
        column_sum(grad_tok * scaled1)
        + column_sum(grad_pro * p_scaled)
        + column_sum(grad_x * xh_x[...])
    )
    sm[prompt_count + 1 : prompt_count + 2, :] = (
        column_sum(grad_tok) + column_sum(grad_pro) + column_sum(grad_x)
    )
    sm[prompt_count + 2 : prompt_count + 3, :] = column_sum(dqkv[:, :width].astype(F32))
    sm[prompt_count + 3 : prompt_count + 4, :] = column_sum(dqkv[:, 2 * width :].astype(F32))
    send_sm = pair_copy(X_SMALL, sm.at[:, other_half], smp)
    send_sm.start()
    reduced(9)

    quarter = SMALL_ROWS // 4
    send_sm.wait_recv()
    small = sm[:, my_half] + smp[...]
    for a in range(2):
        for c in range(2):
            s0[a, c] = small[(2 * a + c) * quarter : (2 * a + c + 1) * quarter, :]

    small_one = remote(s0.at[1 - h1], rs1, one_s.at[12], one_r.at[12], nb1)
    small_one.start()
    advance_one(10)
    advance_one(11)
    small_one.wait_recv()
    s1b[...] = s0[h1] + rs1[...]
    small_two = remote(s1b.at[1 - h2], rs2, two_s.at[12], two_r.at[12], nb2)
    small_two.start()
    finish_three(0)
    reduced(10)
    reduced(11)
    small_two.wait_recv()
    rs3[s] = s1b[h2] + rs2[...]

    def small_three(d):
        return remote(
            rs3.at[s], rs3.at[s], three_s.at[12, d - 1], three_r.at[12, s], (b, along(d))
        )

    def small_three_recv(j):
        return remote(rs3.at[j], rs3.at[j], three_s.at[12, 0], three_r.at[12, j], (b, j))

    for d in range(1, groups):
        small_three(d).start()
    finish_three(1)
    start_gather_two(0)
    finish_three(2)
    start_gather_two(1)
    start_gather_pair(0)
    finish_three(3)
    start_gather_pair(1)
    for d in range(1, groups):
        small_three_recv(along(d)).wait_recv()
    total = rs3[0]
    for j in range(1, groups):
        total = total + rs3[j]
    s3[...] = total
    small_keep = pltpu.make_async_copy(s3, small_ref.at[core, h1, h2], loc_sem.at[SMALL])
    small_keep.start()
    small_gather = remote(
        s3, small_ref.at[core, h1, h2], ag1_s.at[SMALL], ag1_r.at[SMALL], nb2
    )
    small_gather.start()
    start_gather_two(2)

    @pl.when(s == 2)
    def _():
        for j in range(2):
            e_back(j, j).wait_recv()
        full = e_low[...] + e_in[0].astype(F32) + e_in[1].astype(F32)
        scaled, inverse = norm_stats(tokens_ref[0:extra, :].astype(F32))
        grad_input_ref[0:extra, :] = (
            mid[0:extra, :] + norm_back(full, scaled, inverse, gain1)
        ).astype(BF16)

    start_gather_two(3)
    small_keep.wait()
    small_gather.wait_recv()
    small_gather_two = remote(
        small_ref.at[core, h1], small_ref.at[core, h1], ag2_s.at[SMALL], ag2_r.at[SMALL], nb1
    )
    small_gather_two.start()
    start_gather_pair(2)
    start_gather_pair(3)
    small_gather_two.wait_recv()
    small_pair = pair_copy(X_FINAL + SMALL, small_ref.at[core], small_ref.at[core])
    small_pair.start()

    small_pair.wait()
    for g in range(len(SLOTS)):
        gather_pair(g).wait()
        gather_one(g).wait_send()
        gather_two(g).wait_send()
    for u in range(12):
        drain_three(u)
    small_one.wait_send()
    small_two.wait_send()
    small_gather.wait_send()
    small_gather_two.wait_send()
    for d in range(1, groups):
        small_three(d).wait_send()

    for side in range(2):
        token_partner(side, own_at).wait_send()
    stat_partner(own_at).wait_send()
    ga_partner(own_at).wait_send()
    for_halves(lambda *a: token_half(*a).wait_send())
    for_halves(lambda *a: stat_half(*a).wait_send())
    for_halves(lambda *a: ga_half(*a).wait_send())

    @pl.when(s < 2)
    def _():
        att_back(s).wait_send()
        lse_back(s).wait_send()
        e_back(s, 2).wait_send()

    def drain(u, carry):
        stage_one(u).wait_send()
        stage_two(u).wait_send()
        return carry

    lax.fori_loop(0, 12, drain, 0)

    def drain_mlp(j, carry):
        send_act(j).wait_send()
        send_gp(j).wait_send()
        return carry

    lax.fori_loop(0, chunks, drain_mlp, 0)
    for copy in (send_cot, send_norm, send_extra, send_att, send_n2, send_gb, send_q, *send_kv, send_sm):
        copy.wait_send()


def finish_kernel(
    width,
    prompt_count,
    ff,
    layer_in,
    grad_in,
    final_hbm,
    small_hbm,
    layer_out_ref,
    grad_input_ref,
    gp_ref,
    g1_ref,
    s1_ref,
    wqkv_ref,
    qb_ref,
    vb_ref,
    wout_ref,
    ob_ref,
    g2_ref,
    s2_ref,
    wfc1_ref,
    b1_ref,
    wfc2_ref,
    b2_ref,
    final,
    small_in,
    small,
    layer_buf,
    grad_buf,
    fc2_buf,
    fc1_buf,
    out_buf,
    qkv_buf,
    gp_buf,
    b1_buf,
    b2_buf,
    *rest,
):
    vec_bufs, (in_sem, out_sem) = rest[:7], rest[7:]
    half_w = width // 2
    blk = final_hbm.shape[4]
    small_loads = pltpu.make_async_copy(small_hbm, small_in, in_sem.at[3])
    small_loads.start()
    loads = [
        pltpu.make_async_copy(
            final_hbm.at[:, :, :, pl.ds(4 * g, 4)], final.at[g], in_sem.at[g]
        )
        for g in range(3)
    ]
    loads.append(pltpu.make_async_copy(layer_in, layer_buf, in_sem.at[4]))
    loads.append(pltpu.make_async_copy(grad_in, grad_buf, in_sem.at[5]))
    for load in loads:
        load.start()
    stores = []

    def store(src, dst):
        copy = pltpu.make_async_copy(src, dst, out_sem.at[len(stores)])
        copy.start()
        stores.append(copy)

    quads = [(c, a, e) for c in range(2) for a in range(2) for e in range(2)]
    small_loads.wait()
    quarter = small_in.shape[3]
    for c, a, e in quads:
        r = (2 * a + e) * quarter
        small[r : r + quarter, c * half_w : (c + 1) * half_w] = small_in[c, a, e]
    gp_buf[...] = small[0:prompt_count, :]
    store(gp_buf, gp_ref)
    vectors = (g1_ref, s1_ref, qb_ref, vb_ref, ob_ref, g2_ref, s2_ref)
    for k, (buf, ref) in enumerate(zip(vec_bufs, vectors)):
        buf[...] = small[prompt_count + k : prompt_count + k + 1, :].reshape(width)
        store(buf, ref)
    for k in range(ff // width):
        r = prompt_count + 7 + k
        b1_buf[k * width : (k + 1) * width] = small[r : r + 1, :].reshape(width)
    store(b1_buf, b1_ref)
    r = prompt_count + 7 + ff // width
    b2_buf[...] = small[r : r + 1, :].reshape(width)
    store(b2_buf, b2_ref)
    loads[0].wait()
    for c, a, e in quads:
        for i in range(4):
            q, r = i // 2, i % 2
            row = c * half_w + (2 * a + e) * (half_w // 4) + r * blk
            fc2_buf[row : row + blk, q * half_w : (q + 1) * half_w] = final[0, c, a, e, i].astype(
                F32
            )
    store(fc2_buf, wfc2_ref)
    loads[1].wait()
    for c, a, e in quads:
        rows = slice((2 * a + e) * blk, (2 * a + e + 1) * blk)
        for i in range(4):
            col = i * width + c * half_w
            fc1_buf[rows, col : col + half_w] = final[1, c, a, e, i].astype(F32)
    store(fc1_buf, wfc1_ref)
    loads[2].wait()
    for c, a, e in quads:
        rows = slice((2 * a + e) * blk, (2 * a + e + 1) * blk)
        cols = slice(c * half_w, (c + 1) * half_w)
        out_buf[rows, cols] = final[2, c, a, e, 0].astype(F32)
        for i in range(3):
            col = i * width + c * half_w
            qkv_buf[rows, col : col + half_w] = final[2, c, a, e, 1 + i].astype(F32)
    store(out_buf, wout_ref)
    store(qkv_buf, wqkv_ref)
    loads[3].wait()
    store(layer_buf, layer_out_ref)
    loads[4].wait()
    store(grad_buf, grad_input_ref)
    for copy in stores:
        copy.wait()


def local(
    tokens,
    segments,
    prompts,
    ln1_gain,
    ln1_shift,
    w_qkv,
    q_bias,
    v_bias,
    w_out,
    out_bias,
    ln2_gain,
    ln2_shift,
    w_fc1,
    fc1_bias,
    w_fc2,
    fc2_bias,
    cotangent,
):
    groups = lax.axis_size("seq")
    batch = lax.axis_size("batch")
    row_count, local_len, width = tokens.shape
    ff = w_fc1.shape[1]
    prompt_count = prompts.shape[0]
    assert row_count == 1 and groups == 4 and batch % GROUP == 0 and ff == 4 * width
    check_window(groups, local_len)
    dims = (groups, local_len, width, ff, prompt_count)
    window = 5 * (local_len // 2)
    extra = extra_rows(local_len)
    half_w = width // 2
    blk = width // groups // 4
    tok_block = local_len + PROMPT_PAD + extra
    quarter = SMALL_ROWS // 4

    vmem = pl.BlockSpec(memory_space=pltpu.VMEM)
    hbm = pl.BlockSpec(memory_space=pl.ANY)
    dma = pltpu.SemaphoreType.DMA
    V = pltpu.VMEM
    scratch = [
        V((width, 3 * width), BF16),
        V((width, width), BF16),
        V((width, ff), BF16),
        V((ff, width), BF16),
        V((window, width), BF16),
        V((2, tok_block, width), BF16),
        V((2, width, tok_block), BF16),
        V((window, width), BF16),
        V((window + PROMPT_PAD, width), BF16),
        V((window + PROMPT_PAD, width), BF16),
        V((local_len, window + PROMPT_PAD), F32),
        V((local_len, width), F32),
        V((2 * local_len, width), BF16),
        V((local_len, 128), F32),
        V((local_len, 128), F32),
        V((local_len, width), F32),
        V((2 * local_len, width), BF16),
        V((width, 2 * local_len), BF16),
        V((4, local_len, width), BF16),
        V((4, local_len, width), BF16),
        V((4, local_len, half_w), BF16),
        V((4, local_len, half_w), BF16),
        V((4, width), F32),
        V((local_len, width), F32),
        V((local_len, width), F32),
        V((local_len, width), BF16),
        V((local_len, width), BF16),
        V((local_len, half_w), BF16),
        V((window, width), BF16),
        V((5, 32, local_len // 2), F32),
        V((tok_block, 3 * width), BF16),
        V((3, tok_block, half_w), BF16),
        V((12, 2, 2, 4, blk, half_w), BF16),
        V((12, 2, 4, blk, half_w), BF16),
        V((12, 4, blk, half_w), BF16),
        V((groups, 12, blk, half_w), BF16),
        V((12, blk, half_w), BF16),
        V((SMALL_ROWS, width), F32),
        V((SMALL_ROWS, half_w), F32),
        V((2, 2, quarter, half_w), F32),
        V((2, quarter, half_w), F32),
        V((2, quarter, half_w), F32),
        V((quarter, half_w), F32),
        V((groups, quarter, half_w), F32),
        V((quarter, half_w), F32),
        V((extra, window + PROMPT_PAD), F32),
        V((extra, width), F32),
        V((extra, width), BF16),
        V((extra, 128), F32),
        V((extra, width), BF16),
        V((2, extra, 128), F32),
        V((extra, width), F32),
        V((extra, width), BF16),
        V((2, extra, width), BF16),
        V((extra, width), F32),
        V((3, local_len, width), F32),
        dma((4,)),
        dma((5,)),
        dma((3,)),
        dma((X_COUNT,)),
        dma((X_COUNT,)),
        dma((4,)),
        dma((2,)),
        dma((4,)),
        dma((2,)),
        dma((13,)),
        dma((13,)),
        dma((13,)),
        dma((13,)),
        dma((13, 3)),
        dma((13, groups)),
        dma((5,)),
        dma((5,)),
        dma((5,)),
        dma((5,)),
        dma((5,)),
        dma((2,)),
        dma((2, 2)),
        dma((1,)),
        dma((2,)),
    ]
    specs = [vmem] * 17
    for index in (5, 8, 12, 14):
        specs[index] = hbm
    layer_out, grad_input, final, small = pl.pallas_call(
        functools.partial(layer_kernel, dims),
        out_shape=(
            jax.ShapeDtypeStruct((local_len, width), BF16),
            jax.ShapeDtypeStruct((local_len, width), BF16),
            jax.ShapeDtypeStruct((2, 2, 2, 12, blk, half_w), BF16),
            jax.ShapeDtypeStruct((2, 2, 2, quarter, half_w), F32),
        ),
        in_specs=specs,
        out_specs=(vmem, vmem, hbm, hbm),
        scratch_shapes=scratch,
        compiler_params=pltpu.CompilerParams(
            collective_id=0, has_side_effects=True, vmem_limit_bytes=67043328
        ),
        name="layer",
    )(
        tokens.reshape(local_len, width),
        segments,
        prompts,
        ln1_gain,
        ln1_shift,
        w_qkv,
        q_bias,
        v_bias,
        w_out,
        out_bias,
        ln2_gain,
        ln2_shift,
        w_fc1,
        fc1_bias,
        w_fc2,
        fc2_bias,
        cotangent.reshape(local_len, width),
    )
    if batch > GROUP:
        rings = [list(range(k, batch, GROUP)) for k in range(GROUP)]
        final, small = lax.psum((final, small), "batch", axis_index_groups=rings)
    rows_z = width // groups

    def flat(n):
        return jax.ShapeDtypeStruct((n,), F32)

    outs = pl.pallas_call(
        functools.partial(finish_kernel, width, prompt_count, ff),
        out_shape=(
            jax.ShapeDtypeStruct((local_len, width), BF16),
            jax.ShapeDtypeStruct((local_len, width), BF16),
            jax.ShapeDtypeStruct((prompt_count, width), F32),
            flat(width),
            flat(width),
            jax.ShapeDtypeStruct((rows_z, 3 * width), F32),
            flat(width),
            flat(width),
            jax.ShapeDtypeStruct((rows_z, width), F32),
            flat(width),
            flat(width),
            flat(width),
            jax.ShapeDtypeStruct((rows_z, ff), F32),
            flat(ff),
            jax.ShapeDtypeStruct((ff // groups, width), F32),
            flat(width),
        ),
        in_specs=[pl.BlockSpec(memory_space=pltpu.HBM)] * 4,
        out_specs=(hbm,) * 16,
        scratch_shapes=[
            V((3, 2, 2, 2, 4, blk, half_w), BF16),
            V((2, 2, 2, quarter, half_w), F32),
            V((SMALL_ROWS, width), F32),
            V((local_len, width), BF16),
            V((local_len, width), BF16),
            V((ff // groups, width), F32),
            V((rows_z, ff), F32),
            V((rows_z, width), F32),
            V((rows_z, 3 * width), F32),
            V((prompt_count, width), F32),
            V((ff,), F32),
            V((width,), F32),
            *[V((width,), F32) for _ in range(7)],
            dma((6,)),
            dma((16,)),
        ],
        compiler_params=pltpu.CompilerParams(vmem_limit_bytes=67043328),
        name="finish",
    )(layer_out, grad_input, final, small)
    return tuple(o.reshape((1, local_len, width)) if i < 2 else o for i, o in enumerate(outs))


def solution(mesh):
    tok = P("batch", "seq", None)
    in_specs = (tok, P("batch", "seq")) + (P(),) * 14 + (tok,)
    out_specs = (
        tok,
        tok,
        P(),
        P(),
        P(),
        P("seq", None),
        P(),
        P(),
        P("seq", None),
        P(),
        P(),
        P(),
        P("seq", None),
        P(),
        P("seq", None),
        P(),
    )
    return jax.shard_map(local, mesh=mesh, in_specs=in_specs, out_specs=out_specs, check_vma=False)
```
